32 devices in a mesh: dp: 8 (over y, x, core), seq: 4 (over z).
Axes of the slice: x: 2, y: 2, z: 4, core: 2. Of those that a mesh axis runs over, the one named last changes fastest.
Arguments:
- hidden_in: bfloat16 [8, 2048, 1024], P('dp', 'seq'), may hold values from -6 to 6
- doc_lengths: int32 [8, 8], P('dp'), may hold values from 1 to 1024, 2048 in all within a row
- ln1_gain: float32 [1024], replicated, may hold values from 0.1 to 1.9
- ln1_bias: float32 [1024], replicated, may hold values from -1.75 to 1.75
- ln2_gain: float32 [1024], replicated, may hold values from 0.1 to 1.9
- ln2_bias: float32 [1024], replicated, may hold values from -1.75 to 1.75
- qkv_weight: bfloat16 [1024, 3072], replicated, may hold values from -0.1875 to 0.1875
- qkv_bias: float32 [3072], replicated, may hold values from -1.75 to 1.75
- dense_weight: bfloat16 [1024, 1024], replicated, may hold values from -0.75 to 0.75
- dense_bias: float32 [1024], replicated, may hold values from -1.75 to 1.75
- fc_in_weight: bfloat16 [1024, 4096], replicated, may hold values from -0.1875 to 0.1875
- fc_in_bias: float32 [4096], replicated, may hold values from -1.75 to 1.75
- fc_out_weight: bfloat16 [4096, 1024], replicated, may hold values from -0.09375 to 0.09375
- fc_out_bias: float32 [1024], replicated, may hold values from -1.75 to 1.75
- out_grad: bfloat16 [8, 2048, 1024], P('dp', 'seq'), may hold values from -8 to 8
Outputs:
- hidden_out: bfloat16 [8, 2048, 1024], P('dp', 'seq')
- grad_in: float32 [8, 2048, 1024], P('dp', 'seq')
- grad_ln1_gain: float32 [1024], P(('dp', 'seq'))
- grad_ln1_bias: float32 [1024], P(('dp', 'seq'))
- grad_ln2_gain: float32 [1024], P(('dp', 'seq'))
- grad_ln2_bias: float32 [1024], P(('dp', 'seq'))
- grad_qkv_weight: float32 [1024, 3072], P(('dp', 'seq'))
- grad_qkv_bias: float32 [3072], P(('dp', 'seq'))
- grad_dense_weight: float32 [1024, 1024], P(('dp', 'seq'))
- grad_dense_bias: float32 [1024], P(('dp', 'seq'))
- grad_fc_in_weight: float32 [1024, 4096], P(('dp', 'seq'))
- grad_fc_in_bias: float32 [4096], P(('dp', 'seq'))
- grad_fc_out_weight: float32 [4096, 1024], P(('dp', 'seq'))
- grad_fc_out_bias: float32 [1024], P(('dp', 'seq'))
The draws below stay inside these ranges and needn't reach their ends.
Inputs may be any that keep to these rules, and one draw needn't show every extreme that they name: `doc_lengths`: each row sums to 2048; its last entry is the padding document.
All inputs are finite; a program needn't handle non-finite values.
Results may differ from the reference program's by a relative error of at most 0.0097.
Values may be sent and summed in bfloat16 or wider, within the bound.
A program may use at most 256 MiB of HBM per device.

```python
import math
import jax
import jax.numpy as jnp
import numpy as np
from jax import lax

D = 1024
HEADS = 16
HEAD = 64
FF = 4096
ROT = 16
SEQ_LEN = 2048
DOCS = 8
SEQS = 8
DOC_MOST = 1024


def strengthened(result, key, source, target, blocks, factor):
    owner, partner = [(jnp.arange(result.shape[dim]) // (result.shape[dim] // blocks)).reshape([-1 if axis == dim else 1 for axis in range(result.ndim)]) for dim in (source, target)]
    chosen = jax.random.permutation(key, blocks)[partner]
    strong = (owner == chosen) | (owner == (partner + blocks // 2) % blocks)
    return jnp.where(strong, factor * result, result)


def shard_levels(own_key, shape, cuts, low, high):
    def one(position, shards_of):
        draws = jax.random.uniform(jax.random.fold_in(jax.random.fold_in(own_key, 6), position), (shards_of,), jnp.float32, low / len(cuts), high / len(cuts))
        return jnp.repeat(jnp.exp(draws), shape[position] // shards_of).reshape((-1,) + (1,) * (len(shape) - position - 1))

    level = one(*cuts[0])
    for cut in cuts[1:]:
        level = level * one(*cut)
    return level


def split_up(amount, total, most, lean):
    weights = [(1 << 20) // math.isqrt(grade ** lean) + 1 for grade in range(2, amount + 1)]
    rest, given = total - most - (amount - 1), [1] * (amount - 1)
    while rest > 0:
        free = [i for i in range(amount - 1) if given[i] < most]
        pool, left = sum([weights[i] for i in free]), rest
        for i in free:
            extra = min(most - given[i], max(1, left * weights[i] // pool), rest)
            given[i] = given[i] + extra
            rest = rest - extra
    return np.array([most] + given)


def uneven(own_key, number_of, total, reach, skew):
    if number_of == 2:
        one = jax.random.randint(own_key, (), max(1, total - reach), min(reach, total - 1) + 1)
        return jnp.stack([one, total - one])
    tallies = jnp.asarray(split_up(number_of, total, reach, skew), jnp.int32)
    couples = (number_of - 1) // 2
    source_of, taker = tallies[1:1 + 2 * couples:2], tallies[2:2 + 2 * couples:2]
    margin = jnp.minimum(source_of - 1, reach - taker)
    moved = jax.random.randint(jax.random.fold_in(own_key, 1), (couples,), 0, 1 << 20) % (margin + 1)
    tallies = tallies.at[1:1 + 2 * couples:2].set(source_of - moved).at[2:2 + 2 * couples:2].set(taker + moved)
    return tallies[jax.random.permutation(jax.random.fold_in(own_key, 2), number_of)]


def scatter_about(stream_key, extent, width, limit, cuts=(), kind=jnp.bfloat16):
    values = width * jax.random.normal(stream_key, extent, jnp.float32)
    if cuts:
        values = values * shard_levels(stream_key, extent, cuts, -0.22, 0.18)
    return jnp.clip(values, -limit, limit).astype(kind)


def gaussian_with(key, shape, scale, most, split, heavy, kind=jnp.bfloat16):
    entries = scale * jax.random.normal(key, shape, jnp.float32)
    if split:
        entries = entries * shard_levels(key, shape, split, -0.22, 0.18)
    return jnp.clip(strengthened(entries, jax.random.fold_in(key, 3), *heavy), -most, most).astype(kind)


def setup_inputs(seed: int = 0) -> dict:
    keys = jax.random.split(jax.random.key(seed), 16)
    hidden_in = scatter_about(keys[0], (SEQS, SEQ_LEN, D), 1.0, 6.0, ((0, 8), (1, 4)))
    doc_lengths = jax.vmap(lambda own: uneven(own, DOCS, SEQ_LEN, DOC_MOST, 2))(jax.random.split(keys[1], SEQS)).reshape((SEQS, DOCS)).astype(jnp.int32)
    ln1_gain = jnp.clip(1.0 + 0.18 * jax.random.normal(keys[2], (D,), jnp.float32), 0.1, 1.9)
    ln1_bias = scatter_about(keys[3], (D,), 0.3, 1.75, (), jnp.float32)
    ln2_gain = jnp.clip(1.0 + 0.18 * jax.random.normal(keys[4], (D,), jnp.float32), 0.1, 1.9)
    ln2_bias = scatter_about(keys[5], (D,), 0.3, 1.75, (), jnp.float32)
    qkv_weight = scatter_about(keys[6], (D, 3 * D), D ** -0.5, 0.1875)
    qkv_bias = scatter_about(keys[7], (3 * D,), 0.3, 1.75, (), jnp.float32)
    dense_weight = scatter_about(keys[8], (D, D), (D // 16) ** -0.5, 0.75)
    dense_bias = scatter_about(keys[9], (D,), 0.3, 1.75, (), jnp.float32)
    fc_in_weight = scatter_about(keys[10], (D, FF), D ** -0.5, 0.1875)
    fc_in_bias = scatter_about(keys[11], (FF,), 0.3, 1.75, (), jnp.float32)
    fc_out_weight = scatter_about(keys[12], (FF, D), FF ** -0.5, 0.09375)
    fc_out_bias = scatter_about(keys[13], (D,), 0.3, 1.75, (), jnp.float32)
    out_grad = gaussian_with(keys[14], (SEQS, SEQ_LEN, D), 1.0, 8.0, ((0, 8), (1, 4)), (0, 2, 8, 2.0))
    return dict(hidden_in=hidden_in, doc_lengths=doc_lengths, ln1_gain=ln1_gain, ln1_bias=ln1_bias, ln2_gain=ln2_gain, ln2_bias=ln2_bias, qkv_weight=qkv_weight, qkv_bias=qkv_bias, dense_weight=dense_weight, dense_bias=dense_bias, fc_in_weight=fc_in_weight, fc_in_bias=fc_in_bias, fc_out_weight=fc_out_weight, fc_out_bias=fc_out_bias, out_grad=out_grad)


epsilon = 1e-05
masked_score = -1e+30

@jax.custom_vjp
def low(v):
    return lax.optimization_barrier(v.astype(jnp.bfloat16)).astype(jnp.float32)

@jax.custom_vjp
def low_back(v):
    return v

def low_keep(v):
    return (low(v), None)

def low_pass(kept, grad):
    return (grad,)

def back_keep(v):
    return (v, None)

def back_low(kept, grad):
    return (low(grad),)
low.defvjp(low_keep, low_pass)
low_back.defvjp(back_keep, back_low)

def matmul(left, right):
    return jnp.dot(left, right, preferred_element_type=jnp.float32, precision=lax.Precision.HIGHEST)

def layout(lengths):
    positions = jnp.arange(SEQ_LEN, dtype=jnp.int32)
    doc_ends = jnp.cumsum(lengths).astype(jnp.int32)
    starts = doc_ends - lengths
    segment = lax.optimization_barrier(jnp.sum((positions[:, None] >= doc_ends[None, :]).astype(jnp.int32), axis=1))
    belongs = segment[:, None] == jnp.arange(DOCS, dtype=jnp.int32)[None, :]
    doc_start = lax.optimization_barrier(jnp.sum(jnp.where(belongs, starts[None, :], 0), axis=1)).astype(jnp.int32)
    return (segment, positions - doc_start)

def normalize(values, gain, bias):
    average = lax.optimization_barrier(jnp.mean(values, axis=-1, keepdims=True))
    centered = values - average
    variance = lax.optimization_barrier(jnp.mean(centered * centered, axis=-1, keepdims=True))
    return centered * lax.rsqrt(variance + epsilon) * gain + bias

def rotary_tables(positions):
    half_rot = ROT // 2
    inverse = 10000.0 ** (-(2.0 * jnp.arange(half_rot, dtype=jnp.float32)) / ROT)
    angle = positions.astype(jnp.float32)[:, None] * inverse[None, :]
    return (jnp.cos(angle)[:, None, None, :], jnp.sin(angle)[:, None, None, :])

def rotate(packed, cosine, sine_part):
    half_rot = cosine.shape[-1]
    first_half = packed[..., :half_rot]
    second_half = packed[..., half_rot:2 * half_rot]
    turned = jnp.concatenate([first_half * cosine - second_half * sine_part, second_half * cosine + first_half * sine_part, packed[..., 2 * half_rot:]], axis=-1)
    return jnp.concatenate([turned[..., :2, :], packed[..., 2:, :]], axis=-2)

def attention(queries, keys_all, values_all, segment):
    block_rows = min(512, SEQ_LEN)
    score_scale = HEAD ** (-0.5)
    key_index = jnp.arange(SEQ_LEN, dtype=jnp.int32)

    def one_block(block_index):
        first_row = (block_index * block_rows).astype(jnp.int32)
        query_block = lax.dynamic_slice_in_dim(queries, first_row, block_rows, 0)
        query_seg = lax.dynamic_slice_in_dim(segment, first_row, block_rows, 0)
        query_index = first_row + jnp.arange(block_rows, dtype=jnp.int32)
        scores = jnp.einsum('qhd,khd->hqk', query_block, keys_all, precision=lax.Precision.HIGHEST) * score_scale
        scores = low_back(scores)
        allowed = (query_seg[:, None] == segment[None, :]) & (query_index[:, None] >= key_index[None, :])
        scores = jnp.where(allowed[None], scores, masked_score)
        peak_score = lax.optimization_barrier(jnp.max(scores, axis=-1, keepdims=True))
        exponentials = jnp.exp(scores - peak_score)
        probability = exponentials / lax.optimization_barrier(jnp.sum(exponentials, axis=-1, keepdims=True))
        return jnp.einsum('hqk,khd->qhd', low(probability), values_all, precision=lax.Precision.HIGHEST)
    blocks = lax.map(jax.checkpoint(one_block), jnp.arange(SEQ_LEN // block_rows, dtype=jnp.int32))
    return blocks.reshape(SEQ_LEN, HEADS, HEAD)

def forward(input_f32, segment, positions, params):
    gain_one, bias_one, gain_two, bias_two, w_qkv, b_qkv, w_dense, b_dense, w_in, b_in, w_out, b_out = params
    normed_attn = low(normalize(input_f32, gain_one, bias_one))
    normed_mlp = low(normalize(input_f32, gain_two, bias_two))
    packed = low_back(matmul(normed_attn, w_qkv) + b_qkv).reshape(SEQ_LEN, HEADS, 3, HEAD)
    cosine, sine_part = rotary_tables(positions)
    packed = low_back(low(rotate(packed, cosine, sine_part)))
    context = attention(packed[:, :, 0], packed[:, :, 1], packed[:, :, 2], segment)
    context = low_back(low(context.reshape(SEQ_LEN, D)))
    attn_branch = matmul(context, w_dense) + b_dense
    pre_act = low_back(matmul(normed_mlp, w_in) + b_in)
    activated = low(jax.nn.gelu(pre_act, approximate=False))
    mlp_branch = matmul(activated, w_out) + b_out
    return input_f32 + attn_branch + mlp_branch

def reference(hidden_in, doc_lengths, ln1_gain, ln1_bias, ln2_gain, ln2_bias, qkv_weight, qkv_bias, dense_weight, dense_bias, fc_in_weight, fc_in_bias, fc_out_weight, fc_out_bias, out_grad):
    params = tuple((tensor.astype(jnp.float32) for tensor in (ln1_gain, ln1_bias, ln2_gain, ln2_bias, qkv_weight, qkv_bias, dense_weight, dense_bias, fc_in_weight, fc_in_bias, fc_out_weight, fc_out_bias)))

    def per_sequence(running, sequence):
        tokens, lengths, cotangent = sequence
        segment, positions = layout(lengths)
        live_rows = (segment < DOCS - 1).astype(jnp.float32)[:, None]

        def apply_layer(input_f32, *weights):
            return forward(input_f32, segment, positions, weights)
        output, pullback = jax.vjp(apply_layer, tokens.astype(jnp.float32), *params)
        grads = pullback(cotangent.astype(jnp.float32) * live_rows)
        running = tuple((summed + piece for summed, piece in zip(running, grads[1:])))
        return (running, (output.astype(jnp.bfloat16), grads[0]))
    initial = tuple((jnp.zeros(tensor.shape, jnp.float32) for tensor in params))
    sums, (hidden_out, grad_in) = lax.scan(per_sequence, initial, (hidden_in, doc_lengths, out_grad))
    return (hidden_out, grad_in, sums[0], sums[1], sums[2], sums[3], sums[4], sums[5], sums[6], sums[7], sums[8], sums[9], sums[10], sums[11])
```

```python
import functools
import math

import jax
import jax.numpy as jnp
from jax import lax
from jax.experimental import pallas as pl
from jax.experimental.pallas import tpu as pltpu
from jax.sharding import PartitionSpec as P

HEADS = 16
HEAD = 64
ROT = 16
DOC_MOST = 1024
EPS = 1e-05
NEG = -1e30
LANES = 128
PAIR = 3 * LANES
BLOCK = 256
F32 = jnp.float32
BF16 = jnp.bfloat16
MIB = 1 << 20


def params(mib=48):
    return pltpu.CompilerParams(vmem_limit_bytes=mib * MIB)


def cost(flops, nbytes, trans=0):
    return pl.CostEstimate(flops=int(flops), bytes_accessed=int(nbytes), transcendentals=int(trans))


def dot(a, b):
    return lax.dot_general(a, b, (((1,), (0,)), ((), ())), preferred_element_type=F32)


def dot_t(a, b):
    return lax.dot_general(a, b, (((1,), (1,)), ((), ())), preferred_element_type=F32)


def whole(shape):
    return pl.BlockSpec(shape, lambda *_: (0,) * len(shape))


def stage_bits(size):
    return [1 << b for b in range(size.bit_length() - 1)]


def stage_order(ndp, nseq, swap):
    dp_bits = stage_bits(ndp)
    if swap and len(dp_bits) > 1:
        dp_bits[-1], dp_bits[-2] = dp_bits[-2], dp_bits[-1]
    return [("dp", b) for b in dp_bits] + [("seq", b) for b in stage_bits(nseq)]


def relative(position, bits):
    out = jnp.zeros_like(position)
    for k, bit in enumerate(bits):
        out = out | jnp.where((position >> (len(bits) - 1 - k)) & 1 == 1, bit, 0)
    return out


def row_sources(rows, stages, ndp, nseq, me_dp, me_seq):
    block = rows // (ndp * nseq)
    i = jnp.arange(rows, dtype=jnp.int32)
    q = i // block
    dp_bits = [b for axis, b in stages if axis == "dp"]
    seq_bits = [b for axis, b in stages if axis == "seq"]
    dest_dp = me_dp ^ relative(q // nseq, dp_bits)
    dest_seq = me_seq ^ relative(q % nseq, seq_bits)
    return ((dest_dp * nseq + dest_seq) * block + i % block).reshape(rows, 1)


def halving(send, keep, stages, sizes):
    got = []
    rows = keep.shape[0]
    for k, (axis, bit) in enumerate(stages):
        if k:
            lo, hi = rows // 2, rows
            total = keep[lo:hi].astype(F32)
            for r in got:
                total = total + r[lo:hi].astype(F32)
            send = total.astype(BF16)
            rows = lo
        got.append(lax.ppermute(send, axis, [(i, i ^ bit) for i in range(sizes[axis])]))
    total = keep[:rows].astype(F32)
    for r in got:
        total = total + r[:rows].astype(F32)
    return total


def unit_of(x):
    mean = jnp.mean(x, axis=-1, keepdims=True)
    c = x - mean
    inv = lax.rsqrt(jnp.mean(c * c, axis=-1, keepdims=True) + EPS)
    return c * inv, inv


def norm_kernel(x_ref, dy_ref, live_ref, g1, b1, g2, b2, a_ref, m_ref, grad_ref, sum_ref):
    u, _ = unit_of(x_ref[...].astype(F32))
    a_ref[...] = (u * g1[...] + b1[...]).astype(BF16)
    m_ref[...] = (u * g2[...] + b2[...]).astype(BF16)
    grad = dy_ref[...].astype(F32) * live_ref[...]
    grad_ref[...] = grad.astype(BF16)

    @pl.when(pl.program_id(0) == 0)
    def _():
        sum_ref[...] = jnp.zeros_like(sum_ref)

    sum_ref[...] += jnp.sum(grad, axis=0, keepdims=True)


def norms(x, dy, live, g1, b1, g2, b2):
    rows, d = x.shape
    tr = 128
    row = pl.BlockSpec((tr, d), lambda i: (i, 0))
    return pl.pallas_call(
        norm_kernel,
        grid=(rows // tr,),
        in_specs=[row, row, pl.BlockSpec((tr, 1), lambda i: (i, 0))] + [whole((1, d))] * 4,
        out_specs=[row, row, row, whole((1, d))],
        out_shape=[jax.ShapeDtypeStruct((rows, d), BF16)] * 3 + [jax.ShapeDtypeStruct((1, d), F32)],
        compiler_params=params(),
        cost_estimate=cost(rows * d * 20, rows * d * 10),
        name="norms",
    )(x, dy, live, g1, b1, g2, b2)


def norm_back_kernel(x_ref, grad_ref, da_ref, db_ref, dm_ref, g1, g2, out_ref, s1g, s1b, s2g, s2b):
    u, inv = unit_of(x_ref[...].astype(F32))
    d1 = da_ref[...] + db_ref[...].astype(F32)
    d2 = dm_ref[...]
    e = d1 * g1[...] + d2 * g2[...]
    dx = inv * (e - jnp.mean(e, axis=-1, keepdims=True) - u * jnp.mean(e * u, axis=-1, keepdims=True))
    out_ref[...] = grad_ref[...].astype(F32) + dx

    @pl.when(pl.program_id(0) == 0)
    def _():
        for s in (s1g, s1b, s2g, s2b):
            s[...] = jnp.zeros_like(s)

    s1g[...] += jnp.sum(d1 * u, axis=0, keepdims=True)
    s1b[...] += jnp.sum(d1, axis=0, keepdims=True)
    s2g[...] += jnp.sum(d2 * u, axis=0, keepdims=True)
    s2b[...] += jnp.sum(d2, axis=0, keepdims=True)


def norm_back(x, grad, d_own, d_got, d_mlp, g1, g2):
    rows, d = x.shape
    tr = 128
    row = pl.BlockSpec((tr, d), lambda i: (i, 0))
    return pl.pallas_call(
        norm_back_kernel,
        grid=(rows // tr,),
        in_specs=[row] * 5 + [whole((1, d))] * 2,
        out_specs=[row] + [whole((1, d))] * 4,
        out_shape=[jax.ShapeDtypeStruct((rows, d), F32)] + [jax.ShapeDtypeStruct((1, d), F32)] * 4,
        compiler_params=params(),
        cost_estimate=cost(rows * d * 30, rows * d * 18),
        name="norm_back",
    )(x, grad, d_own, d_got, d_mlp, g1, g2)


def mlp_kernel(m_ref, grad_ref, win_ref, bin_ref, wout_ref, out_ref, act_ref, dpre_ref, dm_ref, bsum_ref):
    pre = dot(m_ref[...], win_ref[...]) + bin_ref[...]
    cdf = 0.5 * (1.0 + lax.erf(pre * math.sqrt(0.5)))
    act = (pre * cdf).astype(BF16)
    act_ref[...] = act
    d_act = dot_t(grad_ref[...], wout_ref[...])
    slope = cdf + pre * (jnp.exp(-0.5 * pre * pre) * (1.0 / math.sqrt(2.0 * math.pi)))
    d_pre = (d_act * slope).astype(BF16)
    dpre_ref[...] = d_pre
    bsum_ref[...] = jnp.sum(d_pre.astype(F32), axis=0, keepdims=True)

    @pl.when(pl.program_id(0) == 0)
    def _():
        out_ref[...] = jnp.zeros_like(out_ref)
        dm_ref[...] = jnp.zeros_like(dm_ref)

    out_ref[...] += dot(act, wout_ref[...])
    dm_ref[...] += dot_t(d_pre, win_ref[...])


def mlp(m, grad, win, b_in, wout):
    rows, d = m.shape
    ff = win.shape[1]
    tf = 512
    cols = pl.BlockSpec((rows, tf), lambda i: (0, i))
    line = pl.BlockSpec((1, tf), lambda i: (0, i))
    return pl.pallas_call(
        mlp_kernel,
        grid=(ff // tf,),
        in_specs=[
            whole((rows, d)),
            whole((rows, d)),
            pl.BlockSpec((d, tf), lambda i: (0, i)),
            line,
            pl.BlockSpec((tf, d), lambda i: (i, 0)),
        ],
        out_specs=[whole((rows, d)), cols, cols, whole((rows, d)), line],
        out_shape=[
            jax.ShapeDtypeStruct((rows, d), F32),
            jax.ShapeDtypeStruct((rows, ff), BF16),
            jax.ShapeDtypeStruct((rows, ff), BF16),
            jax.ShapeDtypeStruct((rows, d), F32),
            jax.ShapeDtypeStruct((1, ff), F32),
        ],
        compiler_params=params(),
        cost_estimate=cost(8 * rows * d * ff, 4 * d * ff + 4 * rows * ff + 12 * rows * d, rows * ff * 2),
        name="mlp",
    )(m, grad, win, b_in, wout)


def one_hot(src_ref, n):
    return (lax.broadcasted_iota(jnp.int32, (src_ref.shape[0], n), 1) == src_ref[...]).astype(BF16)


def wgrad_kernel(src_ref, left_ref, right_ref, send_ref, keep_ref, bsum_ref, lt_ref):
    @pl.when(pl.program_id(0) == 0)
    def _():
        lt_ref[...] = dot_t(one_hot(src_ref, left_ref.shape[1]), left_ref[...]).astype(BF16)

    half = keep_ref.shape[0]
    right = right_ref[...]
    keep_ref[...] = dot(lt_ref[:half, :], right).astype(BF16)
    send_ref[...] = dot(lt_ref[half:, :], right).astype(BF16)
    bsum_ref[...] = jnp.sum(right.astype(F32), axis=0, keepdims=True)


def wgrad(src, left, right, c0, cols, tn=512):
    toks, d = left.shape
    out = pl.BlockSpec((d // 2, tn), lambda i: (0, i))
    return pl.pallas_call(
        wgrad_kernel,
        grid=(cols // tn,),
        in_specs=[
            whole((d, 1)),
            whole((toks, d)),
            pl.BlockSpec((toks, tn), lambda i: (0, c0 // tn + i)),
        ],
        out_specs=[out, out, pl.BlockSpec((1, tn), lambda i: (0, i))],
        out_shape=[jax.ShapeDtypeStruct((d // 2, cols), BF16)] * 2 + [jax.ShapeDtypeStruct((1, cols), F32)],
        scratch_shapes=[pltpu.VMEM((d, toks), BF16)],
        compiler_params=params(),
        cost_estimate=cost(2 * toks * d * (cols + d), 2 * toks * (d + cols) + 2 * d * cols),
        name="wgrad",
    )(src, left, right)


def wgrad_rows_kernel(half, n, tiles_ref, src_ref, left_ref, right_ref, send_ref, keep_ref):
    i = pl.program_id(0)
    lt = dot_t(one_hot(src_ref, left_ref.shape[1]), left_ref[...]).astype(BF16)
    out = dot(lt, right_ref[...]).astype(BF16)

    @pl.when(i < half)
    def _():
        send_ref[...] = out

    @pl.when(i >= half)
    def _():
        keep_ref[...] = out


def wgrad_rows(tiles, src, left, right):
    toks, d = right.shape
    n = tiles.shape[0]
    tile = left.shape[1] // n
    half = n // 2
    return pl.pallas_call(
        functools.partial(wgrad_rows_kernel, half, n),
        grid_spec=pltpu.PrefetchScalarGridSpec(
            num_scalar_prefetch=1,
            grid=(n,),
            in_specs=[
                pl.BlockSpec((tile, 1), lambda i, t: (0, 0)),
                pl.BlockSpec((toks, tile), lambda i, t: (0, t[i])),
                pl.BlockSpec((toks, d), lambda i, t: (0, 0)),
            ],
            out_specs=[
                pl.BlockSpec((tile, d), lambda i, t: (jnp.minimum(i, half - 1), 0)),
                pl.BlockSpec((tile, d), lambda i, t: (jnp.maximum(i - half, 0), 0)),
            ],
        ),
        out_shape=[jax.ShapeDtypeStruct((half * tile, d), BF16)] * 2,
        compiler_params=params(),
        cost_estimate=cost(2 * toks * n * tile * (d + tile), 2 * (n * tile * (d + toks) + toks * d)),
        name="wgrad_rows",
    )(tiles, src, left, right)


def back_kernel(a_ref, w_ref, out_ref, acc_ref):
    i = pl.program_id(0)

    @pl.when(i == 0)
    def _():
        acc_ref[...] = jnp.zeros_like(acc_ref)

    acc_ref[...] += dot_t(a_ref[...], w_ref[...])

    @pl.when(i == pl.num_programs(0) - 1)
    def _():
        out_ref[...] = acc_ref[...].astype(out_ref.dtype)


def back_product(a, w, piece, rows, dtype, tk=512, name="back"):
    d, depth = w.shape
    return pl.pallas_call(
        back_kernel,
        grid=(depth // tk,),
        in_specs=[
            pl.BlockSpec((rows, tk), lambda i: (piece, i)),
            pl.BlockSpec((d, tk), lambda i: (0, i)),
        ],
        out_specs=whole((rows, d)),
        out_shape=jax.ShapeDtypeStruct((rows, d), dtype),
        scratch_shapes=[pltpu.VMEM((rows, d), F32)],
        compiler_params=params(),
        cost_estimate=cost(2 * rows * d * depth, 2 * depth * (rows + d) + 4 * rows * d),
        name=name,
    )(a, w)


def join_kernel(x_ref, mlp_ref, ctx_ref, w_ref, bias_ref, out_ref):
    total = x_ref[...].astype(F32) + mlp_ref[...] + dot(ctx_ref[...], w_ref[...]) + bias_ref[...]
    out_ref[...] = total.astype(BF16)


def join(x, mlp_out, ctx, w, bias, tn=256):
    rows, d = x.shape
    cols = pl.BlockSpec((rows, tn), lambda i: (0, i))
    return pl.pallas_call(
        join_kernel,
        grid=(d // tn,),
        in_specs=[cols, cols, whole((rows, d)), pl.BlockSpec((d, tn), lambda i: (0, i)), pl.BlockSpec((1, tn), lambda i: (0, i))],
        out_specs=cols,
        out_shape=jax.ShapeDtypeStruct((rows, d), BF16),
        compiler_params=params(),
        cost_estimate=cost(2 * rows * d * d, 10 * rows * d + 2 * d * d),
        name="join",
    )(x, mlp_out, ctx, w, bias)


def lane_ids(rows):
    return lax.broadcasted_iota(jnp.int32, (rows, LANES), 1)


def swapped(x):
    h = ROT // 2
    lane = lane_ids(x.shape[0]) % HEAD
    return jnp.where(lane < h, pltpu.roll(x, LANES - h, 1), pltpu.roll(x, h, 1))


def qkv_kernel(a_ref, w_ref, bias_ref, cos_ref, sin_ref, q_ref, k_ref, v_ref):
    packed = dot(a_ref[...], w_ref[...]) + bias_ref[...]
    rows = packed.shape[0]
    first = lane_ids(rows) < HEAD
    pa, pb, pc = packed[:, :LANES], packed[:, LANES : 2 * LANES], packed[:, 2 * LANES :]
    q = jnp.where(first, pa, pb)
    k = pltpu.roll(jnp.where(first, pc, pa), HEAD, 1)
    v = jnp.where(first, pb, pc)
    cos, sin = cos_ref[...], sin_ref[...]
    q_ref[...] = (q * cos + swapped(q) * sin).astype(BF16)
    k_ref[...] = (k * cos + swapped(k) * sin).astype(BF16)
    v_ref[...] = v.astype(BF16)


def qkv(a, w, bias, cos, sin):
    rows, d = a.shape
    out = pl.BlockSpec((rows, LANES), lambda i: (0, i))
    return pl.pallas_call(
        qkv_kernel,
        grid=(w.shape[1] // PAIR,),
        in_specs=[
            whole((rows, d)),
            pl.BlockSpec((d, PAIR), lambda i: (0, i)),
            pl.BlockSpec((1, PAIR), lambda i: (0, i)),
            whole((rows, LANES)),
            whole((rows, LANES)),
        ],
        out_specs=[out] * 3,
        out_shape=[jax.ShapeDtypeStruct((rows, w.shape[1] // 3), BF16)] * 3,
        compiler_params=params(),
        cost_estimate=cost(2 * rows * d * w.shape[1], 8 * rows * d + 2 * d * w.shape[1]),
        name="qkv",
    )(a, w, bias, cos, sin)


def attention_kernel(
    toks,
    win,
    low_ref,
    start_ref,
    q_ref,
    k_ref,
    v_ref,
    do_ref,
    cos_ref,
    sin_ref,
    ctx_ref,
    dp_ref,
    k2,
    v2,
    kt,
    vt,
    s_ref,
    e_ref,
    dq_acc,
    dk_acc,
    dv_acc,
):
    nk = win // BLOCK
    halo = win - toks
    first = lane_ids(BLOCK) < HEAD
    zero = jnp.zeros((BLOCK, LANES), BF16)
    top = lax.broadcasted_iota(jnp.int32, (LANES, BLOCK), 0) < HEAD
    for j in range(nk):
        rows = slice(j * BLOCK, (j + 1) * BLOCK)
        for src, two, tr in ((k_ref, k2, kt), (v_ref, v2, vt)):
            x = src[rows, :]
            a, b = jnp.where(first, x, zero), jnp.where(first, zero, x)
            two[j, :BLOCK, :] = a
            two[j, BLOCK:, :] = b
            tr[j, :, :BLOCK] = a.astype(F32).T.astype(BF16)
            tr[j, :, BLOCK:] = b.astype(F32).T.astype(BF16)
    dk_acc[...] = jnp.zeros_like(dk_acc)
    dv_acc[...] = jnp.zeros_like(dv_acc)
    scale = HEAD**-0.5
    for i in range(toks // BLOCK):
        rows = slice(i * BLOCK, (i + 1) * BLOCK)
        last = halo // BLOCK + i
        low = low_ref[i]
        q = (q_ref[rows, :].astype(F32) * scale).astype(BF16)
        q0, q1 = jnp.where(first, q, zero), jnp.where(first, zero, q)
        start = start_ref[:, rows]
        q_at = halo + i * BLOCK + lax.broadcasted_iota(jnp.int32, (1, BLOCK), 1)

        def scores(j, peak):
            s = dot_t(k2[j], q)
            at = j * BLOCK + lax.broadcasted_iota(jnp.int32, (BLOCK, BLOCK), 0)
            ok = (at >= start) & (at <= q_at)
            s0 = jnp.where(ok, s[:BLOCK], NEG)
            s1 = jnp.where(ok, s[BLOCK:], NEG)
            s_ref[j, :BLOCK, :] = s0
            s_ref[j, BLOCK:, :] = s1
            return (
                jnp.maximum(peak[0], jnp.max(s0, axis=0, keepdims=True)),
                jnp.maximum(peak[1], jnp.max(s1, axis=0, keepdims=True)),
            )

        floor = jnp.full((1, BLOCK), NEG, F32)
        m0, m1 = lax.fori_loop(low, last + 1, scores, (floor, floor))

        def weigh(j, carry):
            t0, t1, acc = carry
            e0 = jnp.exp(s_ref[j, :BLOCK, :] - m0)
            e1 = jnp.exp(s_ref[j, BLOCK:, :] - m1)
            e_ref[j, :BLOCK, :] = e0.astype(BF16)
            e_ref[j, BLOCK:, :] = e1.astype(BF16)
            acc = acc + dot(vt[j], e_ref[j])
            return (
                t0 + jnp.sum(e0, axis=0, keepdims=True),
                t1 + jnp.sum(e1, axis=0, keepdims=True),
                acc,
            )

        none = jnp.zeros((1, BLOCK), F32)
        t0, t1, acc = lax.fori_loop(low, last + 1, weigh, (none, none, jnp.zeros((LANES, BLOCK), F32)))
        r0, r1 = 1.0 / t0, 1.0 / t1
        share = jnp.where(top, r0, r1)
        ctx_t = acc * share
        ctx_ref[rows, :] = ctx_t.T.astype(BF16)
        do_t = do_ref[rows, :].astype(F32).T * share
        both = do_t * ctx_t
        d0 = jnp.sum(jnp.where(top, both, 0.0), axis=0, keepdims=True)
        d1 = jnp.sum(jnp.where(top, 0.0, both), axis=0, keepdims=True)
        do = do_t.T.astype(BF16)
        do0, do1 = jnp.where(first, do, zero), jnp.where(first, zero, do)

        def back(j, dq):
            dp = dot_t(v2[j], do)
            e = e_ref[j]
            e0, e1 = e[:BLOCK], e[BLOCK:]
            ds0 = (e0.astype(F32) * (dp[:BLOCK] - d0)).astype(BF16)
            ds1 = (e1.astype(F32) * (dp[BLOCK:] - d1)).astype(BF16)
            at = pl.ds(pl.multiple_of(j * BLOCK, BLOCK), BLOCK)
            dk_acc[at, :] += dot(ds0, q0) + dot(ds1, q1)
            dv_acc[at, :] += dot(e0, do0) + dot(e1, do1)
            return dq + dot(kt[j, :, :BLOCK], ds0) + dot(kt[j, :, BLOCK:], ds1)

        dq_t = lax.fori_loop(low, last + 1, back, jnp.zeros((LANES, BLOCK), F32))
        dq_acc[rows, :] = dq_t.T * scale
    for j in range(nk):
        rows = slice(j * BLOCK, (j + 1) * BLOCK)
        cos, sin = cos_ref[rows, :], sin_ref[rows, :]
        dk = dk_acc[rows, :]
        dk = pltpu.roll(dk * cos - swapped(dk) * sin, HEAD, 1)
        dv = dv_acc[rows, :]
        if j * BLOCK >= halo:
            own = slice(j * BLOCK - halo, (j + 1) * BLOCK - halo)
            dq = dq_acc[own, :]
            dq = dq * cos - swapped(dq) * sin
        else:
            dq = jnp.zeros_like(dk)
        dp_ref[rows, :LANES] = jnp.where(first, dq, dk).astype(BF16)
        dp_ref[rows, LANES : 2 * LANES] = jnp.where(first, dv, dq).astype(BF16)
        dp_ref[rows, 2 * LANES :] = jnp.where(first, dk, dv).astype(BF16)


def attention(low, start, q, k, v, d_ctx, cos, sin):
    win, d = k.shape
    toks = d_ctx.shape[0]
    nk = win // BLOCK
    own = pl.BlockSpec((toks, LANES), lambda i, t: (0, i))
    own_q = pl.BlockSpec((toks, LANES), lambda i, t: (win // toks - 1, i))
    every = pl.BlockSpec((win, LANES), lambda i, t: (0, i))
    fixed = lambda shape: pl.BlockSpec(shape, lambda i, t: (0, 0))
    pairs = d // LANES
    return pl.pallas_call(
        functools.partial(attention_kernel, toks, win),
        grid_spec=pltpu.PrefetchScalarGridSpec(
            num_scalar_prefetch=1,
            grid=(pairs,),
            in_specs=[fixed((1, toks)), own_q, every, every, own, fixed((win, LANES)), fixed((win, LANES))],
            out_specs=[own, pl.BlockSpec((win, PAIR), lambda i, t: (0, i))],
            scratch_shapes=[
                pltpu.VMEM((nk, 2 * BLOCK, LANES), BF16),
                pltpu.VMEM((nk, 2 * BLOCK, LANES), BF16),
                pltpu.VMEM((nk, LANES, 2 * BLOCK), BF16),
                pltpu.VMEM((nk, LANES, 2 * BLOCK), BF16),
                pltpu.VMEM((nk, 2 * BLOCK, BLOCK), F32),
                pltpu.VMEM((nk, 2 * BLOCK, BLOCK), BF16),
                pltpu.VMEM((toks, LANES), F32),
                pltpu.VMEM((win, LANES), F32),
                pltpu.VMEM((win, LANES), F32),
            ],
        ),
        out_shape=[
            jax.ShapeDtypeStruct((toks, d), BF16),
            jax.ShapeDtypeStruct((win, 3 * d), BF16),
        ],
        compiler_params=params(),
        cost_estimate=cost(pairs * toks * DOC_MOST * 4 * 6 * LANES, 14 * win * d, pairs * 2 * toks * DOC_MOST),
        name="attention",
    )(low, start, q, k, v, d_ctx, cos, sin)


def shards(
    hidden_in,
    doc_lengths,
    ln1_gain,
    ln1_bias,
    ln2_gain,
    ln2_bias,
    qkv_weight,
    qkv_bias,
    dense_weight,
    dense_bias,
    fc_in_weight,
    fc_in_bias,
    fc_out_weight,
    fc_out_bias,
    out_grad,
):
    _, toks, d = hidden_in.shape
    ff = fc_in_weight.shape[1]
    ndp, nseq = lax.axis_size("dp"), lax.axis_size("seq")
    ndev = ndp * nseq
    sizes = {"dp": ndp, "seq": nseq}
    me_dp, me_seq = lax.axis_index("dp"), lax.axis_index("seq")
    row = lambda v: v.reshape(1, -1)

    halos = min(-(-(DOC_MOST - 1) // toks), nseq - 1)
    halos = max(halos, 1)
    win = (halos + 1) * toks
    base = (me_seq - halos) * toks
    lengths = doc_lengths.reshape(-1)
    docs = lengths.shape[0]
    order = jnp.arange(docs, dtype=jnp.int32)
    ends = jnp.sum(jnp.where(order[None, :] <= order[:, None], lengths[None, :], 0), axis=1)
    at = base + jnp.arange(win, dtype=jnp.int32)
    begin = jnp.max(jnp.where(at[:, None] >= ends[None, :], ends[None, :], 0), axis=1)
    doc_pos = at - begin
    live = (at[halos * toks :] < ends[docs - 2]).astype(F32).reshape(toks, 1)
    start = (begin - base)[halos * toks :]
    low = start[::BLOCK] // BLOCK
    lane = jnp.arange(LANES, dtype=jnp.int32) % HEAD
    half = ROT // 2
    freq = 10000.0 ** (-(2.0 * (lane % half).astype(F32)) / ROT)
    angle = doc_pos.astype(F32)[:, None] * freq[None, :]
    cos = jnp.where(lane < ROT, jnp.cos(angle), 1.0)
    sin = jnp.where(lane < half, -1.0, jnp.where(lane < ROT, 1.0, 0.0)) * jnp.sin(angle)

    x = hidden_in.reshape(toks, d)
    a_own, m_own, grad, grad_sum = norms(
        x, out_grad.reshape(toks, d), live, row(ln1_gain), row(ln1_bias), row(ln2_gain), row(ln2_bias)
    )

    ahead = [(i, i + 1) for i in range(nseq - 1)]
    behind = [(i + 1, i) for i in range(nseq - 1)]
    pieces = [a_own]
    for _ in range(halos):
        pieces.append(lax.ppermute(pieces[-1], "seq", ahead))
    mlp_out, act, d_pre, d_mlp, b_in_sum = mlp(m_own, grad, fc_in_weight, row(fc_in_bias), fc_out_weight)

    order_a, order_b = stage_order(ndp, nseq, False), stage_order(ndp, nseq, True)
    src_a = row_sources(d, order_a, ndp, nseq, me_dp, me_seq)
    src_b = row_sources(d, order_b, ndp, nseq, me_dp, me_seq)
    in_send, in_keep, _ = wgrad(src_a, m_own, d_pre, 0, ff)
    g_in = halving(in_send, in_keep, order_a, sizes)

    dp_bits = [b for axis, b in order_b if axis == "dp"]
    spots = jnp.arange(ndp, dtype=jnp.int32)
    tiles = me_dp ^ relative(jnp.where(spots < ndp // 2, spots + ndp // 2, spots - ndp // 2), dp_bits)
    src_t = row_sources(ff // ndp, [s for s in order_b if s[0] == "seq"], 1, nseq, 0, me_seq)
    out_send, out_keep = wgrad_rows(tiles, src_t, act, grad)
    g_out = halving(out_send, out_keep, order_b, sizes)

    d_ctx = back_product(grad, dense_weight, 0, toks, BF16, name="d_ctx")
    a_all = jnp.concatenate(pieces[::-1], axis=0)
    q, k, v = qkv(a_all, qkv_weight, row(qkv_bias), cos, sin)
    ctx, d_packed = attention(low, row(start), q, k, v, d_ctx, cos, sin)

    got = None
    for piece in range(halos):
        part = back_product(d_packed, qkv_weight, piece, toks, F32 if got is not None else BF16, name="d_attn")
        if got is not None:
            part = (part + got.astype(F32)).astype(BF16)
        got = lax.ppermute(part, "seq", behind)
    d_own = back_product(d_packed, qkv_weight, halos, toks, F32, name="d_attn")

    cut = 3 * d // 2
    qa_send, qa_keep, b_qkv_a = wgrad(src_a, a_all, d_packed, 0, cut)
    g_qkv_a = halving(qa_send, qa_keep, order_a, sizes)
    qb_send, qb_keep, b_qkv_b = wgrad(src_b, a_all, d_packed, cut, cut)
    g_qkv_b = halving(qb_send, qb_keep, order_b, sizes)
    de_send, de_keep, _ = wgrad(src_a, ctx, grad, 0, d)
    g_dense = halving(de_send, de_keep, order_a, sizes)

    hidden_out = join(x, mlp_out, ctx, dense_weight, row(dense_bias + fc_out_bias))
    grad_in, s1g, s1b, s2g, s2b = norm_back(x, grad, d_own, got, d_mlp, row(ln1_gain), row(ln2_gain))

    small = jnp.concatenate(
        [v.reshape(ndev, -1) for v in (s1g, s1b, s2g, s2b, grad_sum, b_qkv_a, b_qkv_b, b_in_sum)], axis=1
    )
    per = d // ndev
    b_qkv = jnp.concatenate([b_qkv_a, b_qkv_b], axis=1)
    small = jnp.concatenate(
        [v.reshape(ndev, -1) for v in (s1g, s1b, s2g, s2b, grad_sum, b_qkv, b_in_sum)], axis=1
    )
    small = lax.psum_scatter(small, ("dp", "seq"), scatter_dimension=0, tiled=True).reshape(-1)
    cuts = [per, 2 * per, 3 * per, 4 * per, 5 * per, 8 * per]
    o1g, o1b, o2g, o2b, o_db, o_qb, o_ib = jnp.split(small, cuts)
    g_qkv = jnp.concatenate([g_qkv_a, g_qkv_b], axis=1)
    return (
        hidden_out.reshape(hidden_in.shape),
        grad_in.reshape(hidden_in.shape),
        o1g,
        o1b,
        o2g,
        o2b,
        g_qkv,
        o_qb,
        g_dense,
        o_db,
        g_in,
        o_ib,
        g_out,
        o_db,
    )


def solution(mesh):
    both = P(("dp", "seq"))
    rows = P(("dp", "seq"), None)
    toks = P("dp", "seq", None)
    return jax.shard_map(
        shards,
        mesh=mesh,
        in_specs=(toks, P("dp", None)) + (P(),) * 12 + (toks,),
        out_specs=(toks, toks, both, both, both, both, rows, both, rows, both, rows, both, rows, both),
        check_vma=False,
    )
```

```python
import functools
import math

import jax
import jax.numpy as jnp
from jax import lax
from jax.experimental import pallas as pl
from jax.experimental.pallas import tpu as pltpu
from jax.sharding import PartitionSpec as P

HEADS = 16
HEAD = 64
ROT = 16
DOC_MOST = 1024
EPS = 1e-05
NEG = -1e30
LANES = 128
PAIR = 3 * LANES
BLOCK = 256
F32 = jnp.float32
BF16 = jnp.bfloat16
MIB = 1 << 20
VMEM_MIB = 56


def dot(a, b):
    return lax.dot_general(a, b, (((1,), (0,)), ((), ())), preferred_element_type=F32)


def dot_t(a, b):
    return lax.dot_general(a, b, (((1,), (1,)), ((), ())), preferred_element_type=F32)


def whole(shape):
    return pl.BlockSpec(shape, lambda *_: (0,) * len(shape))


def call(kernel, *args, grid, in_specs, out_specs, out_shape, name, flops, nbytes, trans=0, scalars=0, scratch=(), after=(), mib=VMEM_MIB):
    n = scalars + len(in_specs)

    def body(*refs):
        kernel(*refs[:n], *refs[n + len(after) :])

    return pl.pallas_call(
        body,
        grid_spec=pltpu.PrefetchScalarGridSpec(
            num_scalar_prefetch=scalars,
            grid=grid,
            in_specs=[*in_specs, *[pl.BlockSpec(memory_space=pl.ANY)] * len(after)],
            out_specs=out_specs,
            scratch_shapes=list(scratch),
        ),
        out_shape=out_shape,
        compiler_params=pltpu.CompilerParams(vmem_limit_bytes=mib * MIB),
        cost_estimate=pl.CostEstimate(flops=int(flops), bytes_accessed=int(nbytes), transcendentals=int(trans)),
        name=name,
    )(*args, *after)


def stage_bits(size):
    return [1 << b for b in range(size.bit_length() - 1)]


def stage_order(ndp, nseq, swap):
    dp_bits = stage_bits(ndp)
    if swap and len(dp_bits) > 1:
        dp_bits[-1], dp_bits[-2] = dp_bits[-2], dp_bits[-1]
    return [("dp", [b]) for b in dp_bits] + [("seq", [b]) for b in stage_bits(nseq)]


def short_order(ndp, nseq):
    dp_bits = stage_bits(ndp)
    return [("dp", dp_bits[:1]), ("dp", dp_bits[1:]), ("seq", stage_bits(nseq))]


def relative(position, bits):
    out = jnp.zeros_like(position)
    for k, bit in enumerate(bits):
        out = out | jnp.where((position >> (len(bits) - 1 - k)) & 1 == 1, bit, 0)
    return out


def block_sources(stages, ndp, nseq, me_dp, me_seq):
    q = jnp.arange(ndp * nseq, dtype=jnp.int32)
    flat = [(axis, b) for axis, bits in stages for b in bits]
    dest_dp = me_dp ^ relative(q // nseq, [b for axis, b in flat if axis == "dp"])
    dest_seq = me_seq ^ relative(q % nseq, [b for axis, b in flat if axis == "seq"])
    return dest_dp * nseq + dest_seq


def fan(bits):
    return [sum(b for k, b in enumerate(bits) if (part >> (len(bits) - 1 - k)) & 1) for part in range(1 << len(bits))]


def combine_kernel(counts, *refs):
    outs = refs[len(refs) - len(counts) :]
    at = 0
    for n, out in zip(counts, outs):
        total = refs[at][...].astype(F32)
        for r in refs[at + 1 : at + n]:
            total += r[...].astype(F32)
        out[...] = total.astype(out.dtype)
        at += n


def combine(items, after=()):
    steps = 4 if all(rows % 64 == 0 for _, _, rows, _ in items) else 1
    ins, specs, out_specs, out_shape, nbytes = [], [], [], [], 0
    for arrays, lo, rows, dtype in items:
        block, cols = rows // steps, arrays[0].shape[1]
        for a in arrays:
            ins.append(a)
            specs.append(pl.BlockSpec((block, cols), lambda i, at=lo // block: (at + i, 0)))
        out_specs.append(pl.BlockSpec((block, cols), lambda i: (i, 0)))
        out_shape.append(jax.ShapeDtypeStruct((rows, cols), dtype))
        nbytes += rows * cols * 2 * (len(arrays) + 2)
    return call(
        functools.partial(combine_kernel, [len(arrays) for arrays, _, _, _ in items]),
        *ins,
        grid=(steps,),
        in_specs=specs,
        out_specs=out_specs,
        out_shape=out_shape,
        name="combine",
        flops=nbytes,
        nbytes=nbytes,
        after=after,
    )


class Halving:
    def __init__(self, send, keep, stages, sizes):
        self.keep, self.stages, self.sizes = keep, list(stages), sizes
        self.rows, self.got, self.result = keep.shape[0], [], None
        self.send([send])

    def send(self, parts):
        axis, bits = self.stages.pop(0)
        for part, offset in zip(parts, fan(bits)[1:]):
            self.got.append(lax.ppermute(part, axis, [(i, i ^ offset) for i in range(self.sizes[axis])]))

    def items(self):
        arrays = [self.keep, *self.got]
        if not self.stages:
            return [(arrays, 0, self.rows, F32)]
        parts = 1 << len(self.stages[0][1])
        self.rows //= parts
        return [(arrays, k * self.rows, self.rows, BF16) for k in range(1, parts)]

    def take(self, outs):
        if self.stages:
            self.send(outs)
        else:
            (self.result,) = outs

    def rest(self):
        return [self.keep, *self.got], 0, self.rows, BF16


def advance(sums, after, extra=()):
    groups = [r.items() for r in sums]
    outs = combine([item for group in groups for item in group] + list(extra), after)
    at = 0
    for r, group in zip(sums, groups):
        r.take(outs[at : at + len(group)])
        at += len(group)
    return [outs[0]], outs[at:]


def finish_kernel(plans, ndp, nseq, *refs):
    n_in = 1 + sum(2 if len(p) > 1 else 1 for p in plans)
    n_out = 1 + sum(len(fan(p[-1][1])) - (len(p) == 1) for p in plans)
    ins, outs, scratch = refs[:n_in], refs[n_in : n_in + n_out], refs[n_in + n_out :]
    send_sem, recv_sem, buffers = scratch[0], scratch[1], list(scratch[2:])
    me = {"dp": lax.axis_index("dp"), "seq": lax.axis_index("seq")}

    def other(axis, offset):
        at = {"dp": me["dp"], "seq": me["seq"]}
        at[axis] = at[axis] ^ offset
        return (at["dp"], at["seq"])

    partners = sorted({(axis, o) for p in plans for axis, bits in p for o in fan(bits)[1:]})
    behind = (me["dp"], lax.rem(me["seq"] + nseq - 1, nseq))
    ahead = (me["dp"], lax.rem(me["seq"] + 1, nseq))
    greet = [other(axis, o) for axis, o in partners] + [behind, ahead]
    barrier = pltpu.get_barrier_semaphore()
    for device in greet:
        pl.semaphore_signal(barrier, inc=1, device_id=device, device_id_type=pl.DeviceIdType.MESH)
    pl.semaphore_wait(barrier, len(greet))
    count = [0]

    def start(src, dst, device):
        k = count[0]
        count[0] += 1
        copy = pltpu.make_async_remote_copy(
            src_ref=src,
            dst_ref=dst,
            send_sem=send_sem.at[k],
            recv_sem=recv_sem.at[k],
            device_id=device,
            device_id_type=pl.DeviceIdType.MESH,
        )
        copy.start()
        return copy

    pending = [start(ins[0], outs[0], behind)]
    states, i_in, i_out = [], 1, 1
    for p in plans:
        final = len(fan(p[-1][1]))
        own, got = outs[i_out], outs[i_out + (len(p) > 1) :][: final - 1]
        i_out += final - (len(p) == 1)
        if len(p) > 1:
            send, keep = ins[i_in : i_in + 2]
            i_in += 2
            first_got = buffers.pop(0)
            axis, bits = p[0]
            copy = start(send, first_got, other(axis, bits[0]))
            states.append([p, keep, first_got, copy, own, got])
        else:
            rows_left = ins[i_in]
            i_in += 1
            axis, bits = p[0]
            for k, offset in enumerate(fan(bits)[1:]):
                pending.append(start(rows_left.at[k + 1], got[k], other(axis, offset)))
    waves = []
    for p, keep, first_got, copy, own, got in states:
        out_buf, in_buf = buffers.pop(0), buffers.pop(0)
        copy.wait()
        axis, bits = p[1]
        rows = out_buf.shape[1]
        copies = []
        for k, offset in enumerate(fan(bits)[1:]):
            at = slice((k + 1) * rows, (k + 2) * rows)
            out_buf[k] = (keep[at, :].astype(F32) + first_got[at, :].astype(F32)).astype(BF16)
            copies.append(start(out_buf.at[k], in_buf.at[k], other(axis, offset)))
        waves.append((p, keep, first_got, copies, in_buf, own, got))
    for p, keep, first_got, copies, in_buf, own, got in waves:
        out_buf = buffers.pop(0)
        for copy in copies:
            copy.wait()
        axis, bits = p[2]
        rows = own.shape[0]
        for k, offset in reversed(list(enumerate(fan(bits)))):
            at = slice(k * rows, (k + 1) * rows)
            total = keep[at, :].astype(F32) + first_got[at, :].astype(F32)
            for b in range(len(copies)):
                total += in_buf[b, at, :].astype(F32)
            if k:
                out_buf[k - 1] = total.astype(out_buf.dtype)
                pending.append(start(out_buf.at[k - 1], got[k - 1], other(axis, offset)))
            else:
                own[...] = total
    for copy in pending:
        copy.wait()


def finish(part, sums, ndp, nseq, after=()):
    ins, in_specs = [part], [pl.BlockSpec(memory_space=pl.ANY)]
    outs, out_specs = [jax.ShapeDtypeStruct(part.shape, part.dtype)], [pl.BlockSpec(memory_space=pl.ANY)]
    firsts, seconds, thirds, copies = [], [], [], 1
    vmem = pl.BlockSpec(memory_space=pltpu.VMEM)
    hbm = pl.BlockSpec(memory_space=pl.ANY)
    for stages, arrays in sums:
        last = len(fan(stages[-1][1]))
        if len(stages) > 1:
            rows, cols = arrays[1].shape
            ins += arrays
            in_specs += [vmem, vmem]
            mid = len(fan(stages[1][1]))
            firsts.append(pltpu.VMEM((rows, cols), BF16))
            seconds += [pltpu.VMEM((mid - 1, rows // mid, cols), BF16)] * 2
            left = rows // mid // last
            kind = BF16 if left % 16 == 0 else F32
            thirds.append(pltpu.VMEM((last - 1, left, cols), kind))
            copies += 1 + mid - 1 + last - 1
            outs.append(jax.ShapeDtypeStruct((left, cols), F32))
            out_specs.append(vmem)
        else:
            rows, cols = arrays[0].shape
            left, kind = rows // last, arrays[0].dtype
            ins.append(arrays[0].reshape(last, left, cols))
            in_specs.append(hbm)
            copies += last - 1
        outs += [jax.ShapeDtypeStruct((left, cols), kind)] * (last - 1)
        out_specs += [hbm] * (last - 1)
    n = len(ins)

    def body(*refs):
        finish_kernel([stages for stages, _ in sums], ndp, nseq, *refs[:n], *refs[n + len(after) :])

    nbytes = sum(a.size * 2 for a in ins)
    got = pl.pallas_call(
        body,
        in_specs=in_specs + [hbm] * len(after),
        out_specs=out_specs,
        out_shape=outs,
        scratch_shapes=[pltpu.SemaphoreType.DMA((copies,)), pltpu.SemaphoreType.DMA((copies,))] + firsts + seconds + thirds,
        compiler_params=pltpu.CompilerParams(vmem_limit_bytes=VMEM_MIB * MIB, collective_id=1, has_side_effects=True),
        cost_estimate=pl.CostEstimate(flops=nbytes, bytes_accessed=nbytes, transcendentals=0),
        name="finish",
    )(*ins, *after)
    terms, at = [], 1
    for stages, arrays in sums:
        last = len(fan(stages[-1][1]))
        if len(stages) > 1:
            terms.append((list(got[at : at + last]), 0, got[at].shape[0], F32))
        else:
            terms.append(([arrays[0], *got[at : at + last - 1]], 0, got[at].shape[0], F32))
            at -= 1
        at += last
    return got[0], terms


def unit_of(x):
    mean = jnp.mean(x, axis=-1, keepdims=True)
    c = x - mean
    inv = lax.rsqrt(jnp.mean(c * c, axis=-1, keepdims=True) + EPS)
    return c * inv, inv


def norm_kernel(x_ref, dy_ref, live_ref, g1, b1, g2, b2, a_ref, m_ref, grad_ref, sum_ref):
    u, _ = unit_of(x_ref[...].astype(F32))
    a_ref[...] = (u * g1[...] + b1[...]).astype(BF16)
    m_ref[...] = (u * g2[...] + b2[...]).astype(BF16)
    grad = dy_ref[...].astype(F32) * live_ref[...]
    grad_ref[...] = grad.astype(BF16)

    @pl.when(pl.program_id(0) == 0)
    def _():
        sum_ref[...] = jnp.zeros_like(sum_ref)

    sum_ref[...] += jnp.sum(grad, axis=0, keepdims=True)


def norms(x, dy, live, g1, b1, g2, b2, after=()):
    rows, d = x.shape
    tr = 128
    row = pl.BlockSpec((tr, d), lambda i: (i, 0))
    return call(
        norm_kernel,
        x, dy, live, g1, b1, g2, b2,
        grid=(rows // tr,),
        in_specs=[row, row, pl.BlockSpec((tr, 1), lambda i: (i, 0))] + [whole((1, d))] * 4,
        out_specs=[row, row, row, whole((1, d))],
        out_shape=[jax.ShapeDtypeStruct((rows, d), BF16)] * 3 + [jax.ShapeDtypeStruct((1, d), F32)],
        flops=rows * d * 20, nbytes=rows * d * 10,
        name="norms",
        after=after,
    )


def norm_back_kernel(x_ref, grad_ref, da_ref, db_ref, dm_ref, g1, g2, out_ref, s1g, s1b, s2g, s2b):
    u, inv = unit_of(x_ref[...].astype(F32))
    d1 = da_ref[...] + db_ref[...].astype(F32)
    d2 = dm_ref[...]
    e = d1 * g1[...] + d2 * g2[...]
    dx = inv * (e - jnp.mean(e, axis=-1, keepdims=True) - u * jnp.mean(e * u, axis=-1, keepdims=True))
    out_ref[...] = grad_ref[...].astype(F32) + dx

    @pl.when(pl.program_id(0) == 0)
    def _():
        for s in (s1g, s1b, s2g, s2b):
            s[...] = jnp.zeros_like(s)

    s1g[...] += jnp.sum(d1 * u, axis=0, keepdims=True)
    s1b[...] += jnp.sum(d1, axis=0, keepdims=True)
    s2g[...] += jnp.sum(d2 * u, axis=0, keepdims=True)
    s2b[...] += jnp.sum(d2, axis=0, keepdims=True)


def norm_back(x, grad, d_own, d_got, d_mlp, g1, g2, after=()):
    rows, d = x.shape
    tr = 128
    row = pl.BlockSpec((tr, d), lambda i: (i, 0))
    return call(
        norm_back_kernel,
        x, grad, d_own, d_got, d_mlp, g1, g2,
        grid=(rows // tr,),
        in_specs=[row] * 5 + [whole((1, d))] * 2,
        out_specs=[row] + [whole((1, d))] * 4,
        out_shape=[jax.ShapeDtypeStruct((rows, d), F32)] + [jax.ShapeDtypeStruct((1, d), F32)] * 4,
        flops=rows * d * 30, nbytes=rows * d * 18,
        name="norm_back",
        after=after,
    )


def mlp_kernel(m_ref, grad_ref, win_ref, bin_ref, wout_ref, out_ref, act_ref, dpre_ref, dm_ref, bsum_ref):
    pre = dot(m_ref[...], win_ref[...]) + bin_ref[...]
    cdf = 0.5 * (1.0 + lax.erf(pre * math.sqrt(0.5)))
    act = (pre * cdf).astype(BF16)
    act_ref[...] = act
    d_act = dot_t(grad_ref[...], wout_ref[...])
    slope = cdf + pre * (jnp.exp(-0.5 * pre * pre) * (1.0 / math.sqrt(2.0 * math.pi)))
    d_pre = (d_act * slope).astype(BF16)
    dpre_ref[...] = d_pre
    bsum_ref[...] = jnp.sum(d_pre.astype(F32), axis=0, keepdims=True)

    @pl.when(pl.program_id(0) == 0)
    def _():
        out_ref[...] = jnp.zeros_like(out_ref)
        dm_ref[...] = jnp.zeros_like(dm_ref)

    out_ref[...] += dot(act, wout_ref[...])
    dm_ref[...] += dot_t(d_pre, win_ref[...])


def mlp(m, grad, win, b_in, wout, after=()):
    rows, d = m.shape
    ff = win.shape[1]
    tf = 512
    cols = pl.BlockSpec((rows, tf), lambda i: (0, i))
    line = pl.BlockSpec((1, tf), lambda i: (0, i))
    return call(
        mlp_kernel,
        m, grad, win, b_in, wout,
        grid=(ff // tf,),
        in_specs=[
            whole((rows, d)),
            whole((rows, d)),
            pl.BlockSpec((d, tf), lambda i: (0, i)),
            line,
            pl.BlockSpec((tf, d), lambda i: (i, 0)),
        ],
        out_specs=[whole((rows, d)), cols, cols, whole((rows, d)), line],
        out_shape=[
            jax.ShapeDtypeStruct((rows, d), F32),
            jax.ShapeDtypeStruct((rows, ff), BF16),
            jax.ShapeDtypeStruct((rows, ff), BF16),
            jax.ShapeDtypeStruct((rows, d), F32),
            jax.ShapeDtypeStruct((1, ff), F32),
        ],
        flops=8 * rows * d * ff, nbytes=4 * d * ff + 4 * rows * ff + 12 * rows * d, trans=rows * ff * 2,
        name="mlp",
        after=after,
    )


def turned(left, nat_ref, at):
    n = min(BLOCK, left.shape[1])
    eye = lax.broadcasted_iota(jnp.int32, (n, n), 0) == lax.broadcasted_iota(jnp.int32, (n, n), 1)
    eye = jnp.where(eye, 1.0, 0.0).astype(BF16)
    for c in range(0, left.shape[1], n):
        nat_ref[at + c : at + c + n, :] = dot_t(eye, left[:, c : c + n])


def placed(blocks_ref, nat_ref, lt_ref, blocks):
    size = nat_ref.shape[0] // blocks
    for b in range(blocks):
        rows = pl.ds(pl.multiple_of(blocks_ref[b] * size, size), size)
        lt_ref[b * size : (b + 1) * size, :] = nat_ref[rows, :].astype(BF16)


def wgrad_kernel(blocks_ref, *refs):
    *lefts, right_ref, send_ref, keep_ref, bsum_ref, nat_ref, lt_ref = refs

    @pl.when(pl.program_id(0) == 0)
    def _():
        for k, left in enumerate(lefts):
            turned(left[...], nat_ref, k * left.shape[1])
        placed(blocks_ref, nat_ref, lt_ref, blocks_ref.shape[0])

    half = keep_ref.shape[0]
    right = right_ref[...]
    keep_ref[...] = dot(lt_ref[:half, :], right).astype(BF16)
    send_ref[...] = dot(lt_ref[half:, :], right).astype(BF16)
    bsum_ref[...] = jnp.sum(right.astype(F32), axis=0, keepdims=True)


def wgrad(blocks, lefts, right, tn=512, after=()):
    toks, cols = right.shape
    d = sum(left.shape[1] for left in lefts)
    out = pl.BlockSpec((d // 2, tn), lambda i, t: (0, i))
    return call(
        wgrad_kernel,
        blocks, *lefts, right,

            scalars=1,
            grid=(cols // tn,),
            in_specs=[
                *[whole(left.shape) for left in lefts],
                pl.BlockSpec((toks, tn), lambda i, t: (0, i)),
            ],
            out_specs=[out, out, pl.BlockSpec((1, tn), lambda i, t: (0, i))],
            scratch=[pltpu.VMEM((d, toks), F32), pltpu.VMEM((d, toks), BF16)],

        out_shape=[jax.ShapeDtypeStruct((d // 2, cols), BF16)] * 2 + [jax.ShapeDtypeStruct((1, cols), F32)],
        flops=2 * toks * d * cols, nbytes=2 * toks * (d + cols) + 2 * d * cols,
        name="wgrad",
        after=after,
    )


def wgrad_rows_kernel(half, tiles_ref, blocks_ref, left_ref, right_ref, send_ref, keep_ref, nat_ref, lt_ref):
    i = pl.program_id(0)
    turned(left_ref[...], nat_ref, 0)
    placed(blocks_ref, nat_ref, lt_ref, blocks_ref.shape[0])
    out = dot(lt_ref[...], right_ref[...]).astype(BF16)

    @pl.when(i < half)
    def _():
        send_ref[...] = out

    @pl.when(i >= half)
    def _():
        keep_ref[...] = out


def wgrad_rows(tiles, blocks, left, right, after=()):
    toks, d = right.shape
    n = tiles.shape[0]
    tile = left.shape[1] // n
    half = n // 2
    return call(
        functools.partial(wgrad_rows_kernel, half),
        tiles, blocks, left, right,

            scalars=2,
            grid=(n,),
            in_specs=[
                pl.BlockSpec((toks, tile), lambda i, t, u: (0, t[i])),
                pl.BlockSpec((toks, d), lambda i, t, u: (0, 0)),
            ],
            out_specs=[
                pl.BlockSpec((tile, d), lambda i, t, u: (jnp.minimum(i, half - 1), 0)),
                pl.BlockSpec((tile, d), lambda i, t, u: (jnp.maximum(i - half, 0), 0)),
            ],
            scratch=[pltpu.VMEM((tile, toks), F32), pltpu.VMEM((tile, toks), BF16)],

        out_shape=[jax.ShapeDtypeStruct((half * tile, d), BF16)] * 2,
        flops=2 * toks * n * tile * d, nbytes=2 * (n * tile * (d + toks) + toks * d),
        name="wgrad_rows",
        after=after,
    )


def d_ctx_kernel(a_ref, w_ref, out_ref):
    out_ref[...] = dot_t(a_ref[...], w_ref[...]).astype(BF16)


def d_context(grad, w, tn=256, after=()):
    rows, d = grad.shape
    return call(
        d_ctx_kernel,
        grad, w,
        grid=(d // tn,),
        in_specs=[whole((rows, d)), pl.BlockSpec((tn, d), lambda i: (i, 0))],
        out_specs=pl.BlockSpec((rows, tn), lambda i: (0, i)),
        out_shape=jax.ShapeDtypeStruct((rows, d), BF16),
        flops=2 * rows * d * d, nbytes=2 * d * (2 * rows + d),
        name="d_ctx",
        after=after,
    )


def d_attn_kernel(pieces, *refs):
    a_refs, w_ref, outs = refs[: len(refs) - pieces - 1], refs[len(refs) - pieces - 1], refs[len(refs) - pieces :]
    n = a_refs[0].shape[1]
    total = dot_t(a_refs[0][...], w_ref[:, :n])
    for k in range(1, len(a_refs)):
        total += dot_t(a_refs[k][...], w_ref[:, k * n : (k + 1) * n])
    for k, out in enumerate(outs):

        @pl.when(pl.program_id(0) == k)
        def _():
            out[...] = total.astype(out.dtype)


def d_attn_in(parts, w, toks, first, pieces, dtype, after=()):
    d, depth = w.shape
    return call(
        functools.partial(d_attn_kernel, pieces),
        *parts,
        w,
        grid=(pieces,),
        in_specs=[pl.BlockSpec((toks, a.shape[1]), lambda i: (first + i, 0)) for a in parts] + [whole((d, depth))],
        out_specs=[whole((toks, d))] * pieces,
        out_shape=[jax.ShapeDtypeStruct((toks, d), dtype)] * pieces,
        flops=2 * pieces * toks * d * depth,
        nbytes=2 * depth * (pieces * toks + d) + 4 * pieces * toks * d,
        name="d_attn",
        after=after,
    )


def join_kernel(x_ref, mlp_ref, bias_ref, *refs):
    *ctxs, w_ref, out_ref = refs
    total = x_ref[...].astype(F32) + mlp_ref[...] + bias_ref[...]
    n = ctxs[0].shape[1]
    for k, ctx in enumerate(ctxs):
        total += dot(ctx[...], w_ref[k * n : (k + 1) * n, :])
    out_ref[...] = total.astype(BF16)


def join(x, mlp_out, ctxs, w, bias, tn=256, after=()):
    rows, d = x.shape
    cols = pl.BlockSpec((rows, tn), lambda i: (0, i))
    return call(
        join_kernel,
        x, mlp_out, bias, *ctxs, w,
        grid=(d // tn,),
        in_specs=[cols, cols, pl.BlockSpec((1, tn), lambda i: (0, i))]
        + [whole(c.shape) for c in ctxs]
        + [pl.BlockSpec((d, tn), lambda i: (0, i))],
        out_specs=cols,
        out_shape=jax.ShapeDtypeStruct((rows, d), BF16),
        flops=2 * rows * d * d, nbytes=10 * rows * d + 2 * d * d,
        name="join",
        after=after,
    )


def lane_ids(rows):
    return lax.broadcasted_iota(jnp.int32, (rows, LANES), 1)


def turns():
    frm = lax.broadcasted_iota(jnp.int32, (LANES, LANES), 0)
    to = lax.broadcasted_iota(jnp.int32, (LANES, LANES), 1)
    half = ROT // 2
    within = frm % HEAD
    partner = jnp.where(within < half, frm + half, frm - half)
    rotated = within < ROT
    turned = (frm + HEAD) % LANES
    one = lambda hit: jnp.where(hit, 1.0, 0.0).astype(BF16)
    return one(turned == to), one(rotated & (partner == to)), one(rotated & ((partner + HEAD) % LANES == to))


def split(x):
    high = x.astype(BF16)
    return jnp.concatenate([high, (x - high.astype(F32)).astype(BF16)], axis=1)


def qkv_kernel(halo, a_ref, w_ref, bias_ref, cos_ref, sin_ref, q_ref, k_ref, v_ref):
    turn, swap, swap_turn = turns()
    k_moves = jnp.concatenate([turn, swap_turn], axis=1)
    k_moves = jnp.concatenate([k_moves, k_moves], axis=0)
    q_moves = jnp.concatenate([swap, swap], axis=0)
    win = a_ref.shape[0]
    step = min(2 * BLOCK, win - halo)
    first = lane_ids(step) < HEAD
    for r in range(0, win, step):
        rows = slice(r, r + step)
        packed = dot(a_ref[rows, :], w_ref[...]) + bias_ref[...]
        cos, sin = cos_ref[rows, :], sin_ref[rows, :]
        for g in range(w_ref.shape[1] // PAIR):
            c = g * PAIR
            lanes = slice(g * LANES, (g + 1) * LANES)
            pa, pb, pc = packed[:, c : c + LANES], packed[:, c + LANES : c + 2 * LANES], packed[:, c + 2 * LANES : c + PAIR]
            both = dot(split(jnp.where(first, pc, pa)), k_moves)
            k_ref[rows, lanes] = (both[:, :LANES] * cos + both[:, LANES:] * sin).astype(BF16)
            v_ref[rows, lanes] = jnp.where(first, pb, pc).astype(BF16)
            if r >= halo:
                q = jnp.where(first, pa, pb)
                q_ref[r - halo : r - halo + step, lanes] = (q * cos + dot(split(q), q_moves) * sin).astype(BF16)


def qkv(a, w, bias, cos, sin, toks, group=2, after=()):
    win, d = a.shape
    cols = w.shape[1]
    out = pl.BlockSpec((win, group * LANES), lambda i: (0, i))
    return call(
        functools.partial(qkv_kernel, win - toks),
        a, w, bias, cos, sin,
        grid=(cols // PAIR // group,),
        in_specs=[
            whole((win, d)),
            pl.BlockSpec((d, group * PAIR), lambda i: (0, i)),
            pl.BlockSpec((1, group * PAIR), lambda i: (0, i)),
            whole((win, LANES)),
            whole((win, LANES)),
        ],
        out_specs=[pl.BlockSpec((toks, group * LANES), lambda i: (0, i)), out, out],
        out_shape=[jax.ShapeDtypeStruct((toks, cols // 3), BF16)] + [jax.ShapeDtypeStruct((win, cols // 3), BF16)] * 2,
        flops=2 * win * d * cols, nbytes=8 * win * d + 2 * d * cols,
        name="qkv",
        after=after,
    )


GROUP = 4
QB = 256


def attention_kernel(
    toks, win, low_ref, start_ref, q_ref, k_ref, v_ref, do_ref, cos_ref, sin_ref, ctx_ref, dp_ref,
    k2, v2, kt, vt, s_ref, e_ref, dq_acc, dk_acc, dv_acc,
):
    nk = win // BLOCK
    halo = win - toks
    first = lane_ids(BLOCK) < HEAD
    first_q = lane_ids(QB) < HEAD
    zero = jnp.zeros((BLOCK, LANES), BF16)
    zero_q = jnp.zeros((QB, LANES), BF16)
    top = lax.broadcasted_iota(jnp.int32, (LANES, QB), 0) < HEAD
    groups = range(GROUP)
    lanes = [slice(g * LANES, (g + 1) * LANES) for g in groups]
    eye = lax.broadcasted_iota(jnp.int32, (LANES, LANES), 0) == lax.broadcasted_iota(jnp.int32, (LANES, LANES), 1)
    upper = lax.broadcasted_iota(jnp.int32, (LANES, LANES), 0) < HEAD
    eye0 = jnp.where(eye & upper, 1.0, 0.0).astype(BF16)
    eye1 = jnp.where(eye & ~upper, 1.0, 0.0).astype(BF16)
    low_all = low_ref[0]

    def prepare(j, _):
        rows = pl.ds(pl.multiple_of(j * BLOCK, BLOCK), BLOCK)
        for g in groups:
            for src, two, tr in ((k_ref, k2, kt), (v_ref, v2, vt)):
                x = src[rows, lanes[g]]
                two[g, j, :BLOCK, :] = jnp.where(first, x, zero)
                two[g, j, BLOCK:, :] = jnp.where(first, zero, x)
                tr[g, j, :, :BLOCK] = dot_t(eye0, x).astype(BF16)
                tr[g, j, :, BLOCK:] = dot_t(eye1, x).astype(BF16)
        return 0

    lax.fori_loop(low_all, nk, prepare, 0)
    dk_acc[...] = jnp.zeros_like(dk_acc)
    dv_acc[...] = jnp.zeros_like(dv_acc)
    scale = HEAD**-0.5
    for i in range(toks // QB):
        rows = slice(i * QB, (i + 1) * QB)
        last = (halo + (i + 1) * QB) // BLOCK
        low = low_ref[i * (QB // BLOCK)]
        qs = [q_ref[rows, lanes[g]].astype(F32) * scale for g in groups]
        qts = [q.T.astype(BF16) for q in qs]
        qs = [q.astype(BF16) for q in qs]
        q2 = [jnp.concatenate([jnp.where(first_q, q, zero_q), jnp.where(first_q, zero_q, q)], axis=0) for q in qs]
        start = start_ref[:, rows]
        q_at = halo + i * QB + lax.broadcasted_iota(jnp.int32, (1, QB), 1)

        def scores(j, peaks):
            at = j * BLOCK + lax.broadcasted_iota(jnp.int32, (BLOCK, QB), 0)
            ok = (at >= start) & (at <= q_at)
            out = []
            for g in groups:
                s = dot(k2[g, j], qts[g])
                s0 = jnp.where(ok, s[:BLOCK], NEG)
                s1 = jnp.where(ok, s[BLOCK:], NEG)
                s_ref[g, j, :BLOCK, :] = s0
                s_ref[g, j, BLOCK:, :] = s1
                out.append(jnp.maximum(peaks[2 * g], jnp.max(s0, axis=0, keepdims=True)))
                out.append(jnp.maximum(peaks[2 * g + 1], jnp.max(s1, axis=0, keepdims=True)))
            return tuple(out)

        floor = jnp.full((1, QB), NEG, F32)
        peaks = lax.fori_loop(low, last, scores, (floor,) * (2 * GROUP))

        def weigh(j, carry):
            out = []
            for g in groups:
                t0, t1, acc = carry[3 * g : 3 * g + 3]
                e0 = jnp.exp(s_ref[g, j, :BLOCK, :] - peaks[2 * g])
                e1 = jnp.exp(s_ref[g, j, BLOCK:, :] - peaks[2 * g + 1])
                b0, b1 = e0.astype(BF16), e1.astype(BF16)
                e_ref[g, j, :BLOCK, :] = b0
                e_ref[g, j, BLOCK:, :] = b1
                acc = acc + dot(vt[g, j], jnp.concatenate([b0, b1], axis=0))
                out += [t0 + jnp.sum(e0, axis=0, keepdims=True), t1 + jnp.sum(e1, axis=0, keepdims=True), acc]
            return tuple(out)

        none = jnp.zeros((1, QB), F32)
        sums = lax.fori_loop(low, last, weigh, (none, none, jnp.zeros((LANES, QB), F32)) * GROUP)
        do_l, do2, d0, d1 = [], [], [], []
        for g in groups:
            t0, t1, acc = sums[3 * g : 3 * g + 3]
            share = jnp.where(top, 1.0 / t0, 1.0 / t1)
            ctx_t = acc * share
            ctx_ref[rows, lanes[g]] = ctx_t.T.astype(BF16)
            do_t = do_ref[rows, lanes[g]].astype(F32).T * share
            both = do_t * ctx_t
            d0.append(jnp.sum(both[:HEAD], axis=0, keepdims=True))
            d1.append(jnp.sum(both[HEAD:], axis=0, keepdims=True))
            do = do_t.T.astype(BF16)
            do_l.append(do_t.astype(BF16))
            do2.append(jnp.concatenate([jnp.where(first_q, do, zero_q), jnp.where(first_q, zero_q, do)], axis=0))

        def back(j, dqs):
            at = pl.ds(pl.multiple_of(j * BLOCK, BLOCK), BLOCK)
            out = []
            for g in groups:
                dp = dot(v2[g, j], do_l[g])
                e0, e1 = e_ref[g, j, :BLOCK, :], e_ref[g, j, BLOCK:, :]
                ds0 = (e0.astype(F32) * (dp[:BLOCK] - d0[g])).astype(BF16)
                ds1 = (e1.astype(F32) * (dp[BLOCK:] - d1[g])).astype(BF16)
                dv_acc[at, lanes[g]] += dot(jnp.concatenate([e0, e1], axis=1), do2[g])
                dk_acc[at, lanes[g]] += dot(jnp.concatenate([ds0, ds1], axis=1), q2[g])
                out.append(dqs[g] + dot(kt[g, j], jnp.concatenate([ds0, ds1], axis=0)))
            return tuple(out)

        dqs = lax.fori_loop(low, last, back, (jnp.zeros((LANES, QB), F32),) * GROUP)
        for g in groups:
            dq_acc[rows, lanes[g]] = dqs[g].T * scale

    turn, swap, swap_turn = turns()
    for j in range(nk):
        rows = slice(j * BLOCK, (j + 1) * BLOCK)

        def finish():
            cos, sin = cos_ref[rows, :], sin_ref[rows, :]
            for g in groups:
                dk = dk_acc[rows, lanes[g]].astype(BF16)
                dk = dot(dk, turn) * cos - dot(dk, swap_turn) * sin
                dv = dv_acc[rows, lanes[g]]
                if j * BLOCK >= halo:
                    own = slice(j * BLOCK - halo, (j + 1) * BLOCK - halo)
                    dq = dq_acc[own, lanes[g]]
                    dq = dq * cos - dot(dq.astype(BF16), swap) * sin
                else:
                    dq = jnp.zeros_like(dk)
                c = g * PAIR
                dp_ref[rows, c : c + LANES] = jnp.where(first, dq, dk).astype(BF16)
                dp_ref[rows, c + LANES : c + 2 * LANES] = jnp.where(first, dv, dq).astype(BF16)
                dp_ref[rows, c + 2 * LANES : c + PAIR] = jnp.where(first, dk, dv).astype(BF16)

        if j * BLOCK >= halo:
            finish()
        else:
            pl.when(j >= low_all)(finish)

            @pl.when(j < low_all)
            def _():
                dp_ref[rows, :] = jnp.zeros((BLOCK, GROUP * PAIR), BF16)


def attention(low, start, q, k, v, d_ctx, cos, sin, part, parts, after=()):
    win, d = k.shape
    toks = d_ctx.shape[0]
    nk = win // BLOCK
    width = GROUP * LANES
    own = pl.BlockSpec((toks, width), lambda i, t: (0, at + i))
    every = pl.BlockSpec((win, width), lambda i, t: (0, at + i))
    fixed = lambda shape: pl.BlockSpec(shape, lambda i, t: (0, 0))
    pairs = d // LANES // parts
    at = part * pairs // GROUP
    return call(
        functools.partial(attention_kernel, toks, win),
        low, start, q, k, v, d_ctx, cos, sin,

            scalars=1,
            grid=(pairs // GROUP,),
            in_specs=[fixed((1, toks)), own, every, every, own, fixed((win, LANES)), fixed((win, LANES))],
            out_specs=[pl.BlockSpec((toks, width), lambda i, t: (0, i)), pl.BlockSpec((win, GROUP * PAIR), lambda i, t: (0, i))],
            scratch=[
                pltpu.VMEM((GROUP, nk, 2 * BLOCK, LANES), BF16),
                pltpu.VMEM((GROUP, nk, 2 * BLOCK, LANES), BF16),
                pltpu.VMEM((GROUP, nk, LANES, 2 * BLOCK), BF16),
                pltpu.VMEM((GROUP, nk, LANES, 2 * BLOCK), BF16),
                pltpu.VMEM((GROUP, nk, 2 * BLOCK, QB), F32),
                pltpu.VMEM((GROUP, nk, 2 * BLOCK, QB), BF16),
                pltpu.VMEM((toks, width), F32),
                pltpu.VMEM((win, width), F32),
                pltpu.VMEM((win, width), F32),
            ],

        out_shape=[
            jax.ShapeDtypeStruct((toks, d // parts), BF16),
            jax.ShapeDtypeStruct((win, 3 * d // parts), BF16),
        ],
        flops=pairs * toks * DOC_MOST * 4 * 6 * LANES, nbytes=14 * win * d // parts, trans=pairs * 2 * toks * DOC_MOST,
        name="attention",
        after=after,
    )


def shards(
    hidden_in,
    doc_lengths,
    ln1_gain,
    ln1_bias,
    ln2_gain,
    ln2_bias,
    qkv_weight,
    qkv_bias,
    dense_weight,
    dense_bias,
    fc_in_weight,
    fc_in_bias,
    fc_out_weight,
    fc_out_bias,
    out_grad,
):
    _, toks, d = hidden_in.shape
    ff = fc_in_weight.shape[1]
    ndp, nseq = lax.axis_size("dp"), lax.axis_size("seq")
    ndev = ndp * nseq
    sizes = {"dp": ndp, "seq": nseq}
    me_dp, me_seq = lax.axis_index("dp"), lax.axis_index("seq")
    row = lambda v: v.reshape(1, -1)

    halos = min(-(-(DOC_MOST - 1) // toks), nseq - 1)
    halos = max(halos, 1)
    win = (halos + 1) * toks
    base = (me_seq - halos) * toks
    lengths = doc_lengths.reshape(-1)
    docs = lengths.shape[0]
    doc = jnp.arange(docs, dtype=jnp.int32)
    ends = jnp.sum(jnp.where(doc[None, :] <= doc[:, None], lengths[None, :], 0), axis=1)
    at = base + jnp.arange(win, dtype=jnp.int32)
    begin = jnp.max(jnp.where(at[:, None] >= ends[None, :], ends[None, :], 0), axis=1)
    doc_pos = at - begin
    live = (at[halos * toks :] < ends[docs - 2]).astype(F32).reshape(toks, 1)
    start = (begin - base)[halos * toks :]
    low = start[::BLOCK] // BLOCK
    lane = jnp.arange(LANES, dtype=jnp.int32) % HEAD
    half = ROT // 2
    freq = 10000.0 ** (-(2.0 * (lane % half).astype(F32)) / ROT)
    angle = doc_pos.astype(F32)[:, None] * freq[None, :]
    cos = jnp.where(lane < ROT, jnp.cos(angle), 1.0)
    sin = jnp.where(lane < half, -1.0, jnp.where(lane < ROT, 1.0, 0.0)) * jnp.sin(angle)

    x = hidden_in.reshape(toks, d)
    a_own, m_own, grad, grad_sum = norms(
        x, out_grad.reshape(toks, d), live, row(ln1_gain), row(ln1_bias), row(ln2_gain), row(ln2_bias)
    )

    ahead = [(i, i + 1) for i in range(nseq - 1)]
    behind = [(i + 1, i) for i in range(nseq - 1)]
    pieces = [a_own]
    for _ in range(halos):
        pieces.append(lax.ppermute(pieces[-1], "seq", ahead))
    mlp_out, act, d_pre, d_mlp, b_in_sum = mlp(m_own, grad, fc_in_weight, row(fc_in_bias), fc_out_weight)

    order_a, order_b = stage_order(ndp, nseq, False), stage_order(ndp, nseq, True)
    src_a = block_sources(order_a, ndp, nseq, me_dp, me_seq)
    src_b = block_sources(order_b, ndp, nseq, me_dp, me_seq)
    in_send, in_keep, line = wgrad(src_a, [m_own], d_pre, tn=1024, after=[pieces[1]])
    r_in = Halving(in_send, in_keep, order_a, sizes)

    dp_bits = [b for axis, bits in order_b for b in bits if axis == "dp"]
    spots = jnp.arange(ndp, dtype=jnp.int32)
    tiles = me_dp ^ relative(jnp.where(spots < ndp // 2, spots + ndp // 2, spots - ndp // 2), dp_bits)
    src_t = block_sources([s for s in order_b if s[0] == "seq"], 1, nseq, 0, me_seq)
    out_send, out_keep = wgrad_rows(tiles, src_t, act, grad, after=[line])
    r_out = Halving(out_send, out_keep, order_b, sizes)

    last, _ = advance([r_in], [out_keep])
    d_ctx = d_context(grad, dense_weight, after=last)
    last, _ = advance([r_out], [d_ctx])
    a_all = jnp.concatenate(pieces[::-1], axis=0)
    q, k, v = qkv(a_all, qkv_weight, row(qkv_bias), cos, sin, toks, after=last)

    order_c = short_order(ndp, nseq)
    src_c = block_sources(order_c, ndp, nseq, me_dp, me_seq)
    ctx_a, dp_a = attention(low, row(start), q, k, v, d_ctx, cos, sin, 0, 2)
    last, _ = advance([r_in, r_out], [ctx_a])
    qa_send, qa_keep, b_qkv_a = wgrad(src_c, [a_all], dp_a, after=last)
    r_qa = Halving(qa_send, qa_keep, order_c, sizes)
    ctx_b, dp_b = attention(low, row(start), q, k, v, d_ctx, cos, sin, 1, 2, after=[b_qkv_a])

    far = d_attn_in([dp_a, dp_b], qkv_weight, toks, 0, halos, BF16)
    got = lax.ppermute(far[0], "seq", behind)
    last, _ = advance([r_in, r_out, r_qa], [far[0]])
    while len(r_in.stages) > 1:
        last, _ = advance([r_in, r_out], last)
    qb_send, qb_keep, b_qkv_b = wgrad(src_c, [a_all], dp_b, after=last)
    de_send, de_keep, line = wgrad(src_c, [ctx_a, ctx_b], grad, after=[b_qkv_b])
    (d_own,) = d_attn_in([dp_a, dp_b], qkv_weight, toks, halos, 1, F32, after=[line])
    hidden_out = join(x, mlp_out, [ctx_a, ctx_b], dense_weight, row(dense_bias + fc_out_bias), after=[d_own])
    last = [hidden_out]
    for piece in range(1, halos - 1):
        last, (part,) = advance([], last, [([far[piece], got], 0, toks, BF16)])
        got = lax.ppermute(part, "seq", behind)
    part = [far[halos - 1], got] if halos > 1 else [far[0]]
    _, (part, in_left, out_left, qa_left) = advance(
        [], last, [(part, 0, toks, BF16), r_in.rest(), r_out.rest(), r_qa.rest()]
    )
    got, terms = finish(
        part,
        [
            (r_in.stages[:1], [in_left]),
            (r_out.stages[:1], [out_left]),
            (order_c[2:], [qa_left]),
            (order_c, [qb_send, qb_keep]),
            (order_c, [de_send, de_keep]),
        ],
        ndp,
        nseq,
    )
    grad_in, s1g, s1b, s2g, s2b = norm_back(x, grad, d_own, got, d_mlp, row(ln1_gain), row(ln2_gain))
    per = d // ndev
    b_qkv = jnp.concatenate([b_qkv_a, b_qkv_b], axis=1)
    small = jnp.concatenate(
        [v.reshape(ndev, -1) for v in (s1g, s1b, s2g, s2b, grad_sum, b_qkv, b_in_sum)], axis=1
    )
    small = jnp.sum(lax.all_to_all(small, ("dp", "seq"), 0, 0, tiled=True), axis=0)
    cuts = [per, 2 * per, 3 * per, 4 * per, 5 * per, 8 * per]
    o1g, o1b, o2g, o2b, o_db, o_qb, o_ib = jnp.split(small, cuts)
    g_in, g_out, g_qkv_a, g_qkv_b, g_dense = combine(terms, [s1g])
    g_qkv = jnp.concatenate([g_qkv_a, g_qkv_b], axis=1)
    return (
        hidden_out.reshape(hidden_in.shape),
        grad_in.reshape(hidden_in.shape),
        o1g,
        o1b,
        o2g,
        o2b,
        g_qkv,
        o_qb,
        g_dense,
        o_db,
        g_in,
        o_ib,
        g_out,
        o_db,
    )


def solution(mesh):
    both = P(("dp", "seq"))
    rows = P(("dp", "seq"), None)
    toks = P("dp", "seq", None)
    return jax.shard_map(
        shards,
        mesh=mesh,
        in_specs=(toks, P("dp", None)) + (P(),) * 12 + (toks,),
        out_specs=(toks, toks, both, both, both, both, rows, both, rows, both, rows, both, rows, both),
        check_vma=False,
    )
```

```python
import functools
import math

import jax
import jax.numpy as jnp
from jax import lax
from jax.experimental import pallas as pl
from jax.experimental.pallas import tpu as pltpu
from jax.sharding import PartitionSpec as P

HEADS = 16
HEAD = 64
ROT = 16
DOC_MOST = 1024
EPS = 1e-05
NEG = -1e30
LANES = 128
PAIR = 3 * LANES
BLOCK = 256
F32 = jnp.float32
BF16 = jnp.bfloat16
MIB = 1 << 20
VMEM_MIB = 56


def dot(a, b):
    return lax.dot_general(a, b, (((1,), (0,)), ((), ())), preferred_element_type=F32)


def dot_t(a, b):
    return lax.dot_general(a, b, (((1,), (1,)), ((), ())), preferred_element_type=F32)


def whole(shape):
    return pl.BlockSpec(shape, lambda *_: (0,) * len(shape))


def place(to):
    at = {"dp": lax.axis_index("dp"), "seq": lax.axis_index("seq")}
    if to[0] == "ring":
        at["seq"] = lax.rem(at["seq"] + to[1] + to[2], to[2])
    else:
        at[to[0]] = at[to[0]] ^ to[1]
    return (at["dp"], at["seq"])


def both_ways(targets):
    back = [("ring", -to[1], to[2]) for to in targets if to[0] == "ring"]
    return [place(to) for to in sorted({*targets, *back})]


def greet(devices):
    barrier = pltpu.get_barrier_semaphore()
    for device in devices:
        pl.semaphore_signal(barrier, inc=1, device_id=device, device_id_type=pl.DeviceIdType.MESH)
    pl.semaphore_wait(barrier, len(devices))


def call(kernel, *args, grid, in_specs, out_specs, out_shape, name, flops, nbytes, trans=0, scalars=0, scratch=(), after=(), sends=(), cid=None):
    n, n_out, m = scalars + len(in_specs), len(out_specs), len(sends)

    def body(*refs):
        refs = list(refs)
        ins, _, srcs = refs[:n], refs[n : n + len(after)], refs[n + len(after) :][:m]
        rest = refs[n + len(after) + m :]
        outs, gots, own = rest[:n_out], rest[n_out : n_out + m], rest[n_out + m :]
        if not m:
            kernel(*ins, *outs, *own)
            return
        *own, send_sem, recv_sem = own

        def copy(k):
            _, lo, rows, to = sends[k]
            return pltpu.make_async_remote_copy(
                src_ref=srcs[k].at[pl.ds(lo, rows)],
                dst_ref=gots[k],
                send_sem=send_sem.at[k],
                recv_sem=recv_sem.at[k],
                device_id=place(to),
                device_id_type=pl.DeviceIdType.MESH,
            )

        @pl.when(pl.program_id(0) == 0)
        def _():
            greet(both_ways([to for *_, to in sends]))
            for k in range(m):
                copy(k).start()

        kernel(*ins, *outs, *own)

        @pl.when(pl.program_id(0) == grid[0] - 1)
        def _():
            for k in range(m):
                copy(k).wait()

    hbm = pl.BlockSpec(memory_space=pl.ANY)
    more = dict(collective_id=cid, has_side_effects=True) if m else {}
    sems = [pltpu.SemaphoreType.DMA((m,))] * 2 if m else []
    return pl.pallas_call(
        body,
        grid_spec=pltpu.PrefetchScalarGridSpec(
            num_scalar_prefetch=scalars,
            grid=grid,
            in_specs=[*in_specs, *[hbm] * (len(after) + m)],
            out_specs=[*out_specs, *[hbm] * m],
            scratch_shapes=[*scratch, *sems],
        ),
        out_shape=[*out_shape, *[jax.ShapeDtypeStruct((rows, a.shape[1]), a.dtype) for a, _, rows, _ in sends]],
        compiler_params=pltpu.CompilerParams(vmem_limit_bytes=VMEM_MIB * MIB, **more),
        cost_estimate=pl.CostEstimate(flops=int(flops), bytes_accessed=int(nbytes), transcendentals=int(trans)),
        name=name,
    )(*args, *after, *[a for a, *_ in sends])


def stage_bits(size):
    return [1 << b for b in range(size.bit_length() - 1)]


def stage_order(ndp, nseq, kind):
    dp_bits = [("dp", [b]) for b in stage_bits(ndp)]
    seq_bits = [("seq", [b]) for b in stage_bits(nseq)]
    cycle = [*dp_bits[1:], *seq_bits[:1]]
    kind = min(kind, len(cycle) - 1)
    at = (0, len(cycle) - 1, 1)[kind] if kind else 0
    return dp_bits[:1] + cycle[at:] + cycle[:at] + seq_bits[1:]


def short_order(ndp, nseq):
    dp_bits = stage_bits(ndp)
    return [("dp", dp_bits[:1]), ("dp", dp_bits[1:]), ("seq", stage_bits(nseq))]


def flat_bits(stages):
    return [(axis, bit) for axis, bits in stages for bit in bits]


def source(spot, stages, nseq):
    at = {"dp": lax.axis_index("dp"), "seq": lax.axis_index("seq")}
    bits = flat_bits(stages)
    for k, (axis, bit) in enumerate(bits):
        flag = spot // (1 << (len(bits) - 1 - k)) % 2
        if not (isinstance(flag, int) and flag == 0):
            at[axis] = at[axis] + flag * bit * (1 - 2 * (at[axis] // bit % 2))
    return at["dp"] * nseq + at["seq"]


def fan(bits):
    return [sum(b for k, b in enumerate(bits) if (part >> (len(bits) - 1 - k)) & 1) for part in range(1 << len(bits))]


def combine_kernel(counts, slots, *refs):
    outs = refs[sum(counts) :]
    at = 0
    for n, (k, col) in zip(counts, slots):
        total = refs[at][...].astype(F32)
        for r in refs[at + 1 : at + n]:
            total += r[...].astype(F32)
        outs[k][:, col : col + total.shape[1]] = total.astype(outs[k].dtype)
        at += n


def combine(items, after=(), joined=()):
    steps = 4 if all(rows % 64 == 0 for _, _, rows, _ in items) else 1
    ins, specs, counts, slots, shapes, nbytes = [], [], [], [], [], 0
    for k, (arrays, lo, rows, dtype) in enumerate(items):
        block, cols = rows // steps, arrays[0][0].shape[1]
        arrays = [(a, off) for a, off in arrays if off <= lo < off + a.shape[0]]
        for a, off in arrays:
            ins.append(a)
            specs.append(pl.BlockSpec((block, cols), lambda i, at=(lo - off) // block: (at + i, 0)))
        counts.append(len(arrays))
        if k in joined:
            slots.append((len(shapes) - 1, shapes[-1][1]))
            shapes[-1] = (rows, shapes[-1][1] + cols, dtype)
        else:
            slots.append((len(shapes), 0))
            shapes.append((rows, cols, dtype))
        nbytes += rows * cols * 2 * (len(arrays) + 2)
    return call(
        functools.partial(combine_kernel, counts, slots),
        *ins,
        grid=(steps,),
        in_specs=specs,
        out_specs=[pl.BlockSpec((rows // steps, cols), lambda i: (i, 0)) for rows, cols, _ in shapes],
        out_shape=[jax.ShapeDtypeStruct((rows, cols), dtype) for rows, cols, dtype in shapes],
        name="combine",
        flops=nbytes,
        nbytes=nbytes,
        after=after,
    )


class Halving:
    def __init__(self, send, keep, stages, sizes):
        self.keep, self.stages, self.sizes = keep, list(stages), sizes
        self.rows, self.got, self.ready = keep.shape[0], [], [send]

    def targets(self):
        axis, bits = self.stages[0]
        return [(axis, offset) for offset in fan(bits)[1:]]

    def permute(self):
        for part, (axis, offset) in zip(self.ready, self.targets()):
            self.got.append((lax.ppermute(part, axis, [(i, i ^ offset) for i in range(self.sizes[axis])]), 0))
        self.stages.pop(0)

    def sends(self, lo=0, hi=1, parts=1):
        size = self.ready[0].shape[0] // parts
        return [(a, lo * size, (hi - lo) * size, to) for a, to in zip(self.ready, self.targets())]

    def receive(self, arrays, lo=0, hi=1, parts=1, last=True):
        size = self.ready[0].shape[0] // parts
        self.got += [(a, lo * size) for a in arrays]
        if last:
            self.stages.pop(0)

    def items(self):
        arrays = [(self.keep, 0), *self.got]
        parts = 1 << len(self.stages[0][1])
        self.rows //= parts
        return [(arrays, k * self.rows, self.rows, BF16) for k in range(1, parts)]

    def rest(self):
        arrays = [(self.keep, 0), *self.got]
        return arrays, 0, self.rows, BF16


def advance(sums, after):
    groups = [r.items() for r in sums]
    outs = combine([item for group in groups for item in group], after)
    at = 0
    for r, group in zip(sums, groups):
        r.ready = outs[at : at + len(group)]
        at += len(group)
    return [outs[0]]


def unit_of(x):
    mean = jnp.mean(x, axis=-1, keepdims=True)
    c = x - mean
    inv = lax.rsqrt(jnp.mean(c * c, axis=-1, keepdims=True) + EPS)
    return c * inv, inv


def norm_kernel(x_ref, dy_ref, live_ref, g1, b1, g2, b2, a_ref, m_ref, grad_ref, sum_ref):
    u, _ = unit_of(x_ref[...].astype(F32))
    a_ref[...] = (u * g1[...] + b1[...]).astype(BF16)
    m_ref[...] = (u * g2[...] + b2[...]).astype(BF16)
    grad = dy_ref[...].astype(F32) * live_ref[...]
    grad_ref[...] = grad.astype(BF16)

    @pl.when(pl.program_id(0) == 0)
    def _():
        sum_ref[...] = jnp.zeros_like(sum_ref)

    sum_ref[...] += jnp.sum(grad, axis=0, keepdims=True)


def norms(x, dy, live, g1, b1, g2, b2, after=()):
    rows, d = x.shape
    tr = 128
    row = pl.BlockSpec((tr, d), lambda i: (i, 0))
    return call(
        norm_kernel,
        x, dy, live, g1, b1, g2, b2,
        grid=(rows // tr,),
        in_specs=[row, row, pl.BlockSpec((tr, 1), lambda i: (i, 0))] + [whole((1, d))] * 4,
        out_specs=[row, row, row, whole((1, d))],
        out_shape=[jax.ShapeDtypeStruct((rows, d), BF16)] * 3 + [jax.ShapeDtypeStruct((1, d), F32)],
        flops=rows * d * 20, nbytes=rows * d * 10,
        name="norms",
        after=after,
    )


def mlp_kernel(m_ref, grad_ref, win_ref, bin_ref, wout_ref, out_ref, act_ref, dpre_ref, dm_ref, bsum_ref):
    pre = dot(m_ref[...], win_ref[...]) + bin_ref[...]
    cdf = 0.5 * (1.0 + lax.erf(pre * math.sqrt(0.5)))
    act = (pre * cdf).astype(BF16)
    act_ref[...] = act
    d_act = dot_t(grad_ref[...], wout_ref[...])
    slope = cdf + pre * (jnp.exp(-0.5 * pre * pre) * (1.0 / math.sqrt(2.0 * math.pi)))
    d_pre = (d_act * slope).astype(BF16)
    dpre_ref[...] = d_pre
    bsum_ref[...] = jnp.sum(d_pre.astype(F32), axis=0, keepdims=True)

    @pl.when(pl.program_id(0) == 0)
    def _():
        out_ref[...] = jnp.zeros_like(out_ref)
        dm_ref[...] = jnp.zeros_like(dm_ref)

    out_ref[...] += dot(act, wout_ref[...])
    dm_ref[...] += dot_t(d_pre, win_ref[...])


def mlp(m, grad, win, b_in, wout, after=(), sends=(), cid=None):
    rows, d = m.shape
    ff = win.shape[1]
    tf = 512
    cols = pl.BlockSpec((rows, tf), lambda i: (0, i))
    line = pl.BlockSpec((1, tf), lambda i: (0, i))
    return call(
        mlp_kernel,
        m, grad, win, b_in, wout,
        grid=(ff // tf,),
        in_specs=[
            whole((rows, d)),
            whole((rows, d)),
            pl.BlockSpec((d, tf), lambda i: (0, i)),
            line,
            pl.BlockSpec((tf, d), lambda i: (i, 0)),
        ],
        out_specs=[whole((rows, d)), cols, cols, whole((rows, d)), line],
        out_shape=[
            jax.ShapeDtypeStruct((rows, d), F32),
            jax.ShapeDtypeStruct((rows, ff), BF16),
            jax.ShapeDtypeStruct((rows, ff), BF16),
            jax.ShapeDtypeStruct((rows, d), F32),
            jax.ShapeDtypeStruct((1, ff), F32),
        ],
        flops=8 * rows * d * ff, nbytes=4 * d * ff + 4 * rows * ff + 12 * rows * d, trans=rows * ff * 2,
        name="mlp",
        after=after,
        sends=sends,
        cid=cid,
    )


def turned(left, nat_ref, at):
    n = min(BLOCK, left.shape[1])
    eye = lax.broadcasted_iota(jnp.int32, (n, n), 0) == lax.broadcasted_iota(jnp.int32, (n, n), 1)
    eye = jnp.where(eye, 1.0, 0.0).astype(BF16)
    for c in range(0, left.shape[1], n):
        nat_ref[at + c : at + c + n, :] = dot_t(eye, left[:, c : c + n])


def placed(order, nat_ref, lt_ref):
    blocks = 1 << len(flat_bits(order[0]))
    size = nat_ref.shape[0] // blocks
    for b in range(blocks):
        rows = pl.ds(pl.multiple_of(source(b, *order) * size, size), size)
        lt_ref[b * size : (b + 1) * size, :] = nat_ref[rows, :].astype(BF16)


def wgrad_kernel(stacked, orders, steps, starts, per, *refs):
    n = len(starts)
    n_right = -(-sum(steps) // per)
    n_left = len(refs) - n_right - 3 * n - 2
    lefts, rights, refs = refs[:n_left], refs[n_left : n_left + n_right], refs[n_left + n_right :]
    outs, (nat_ref, lt_ref) = refs[:-2], refs[-2:]
    i = pl.program_id(0)

    @pl.when(i == 0)
    def _():
        row = col = 0
        for left in lefts:
            toks, width = left.shape
            turned(left[...], nat_ref.at[:, col : col + toks], row)
            if stacked:
                col += toks
            else:
                row += width

    for g in range(n):
        send_ref, keep_ref, bsum_ref = outs[3 * g : 3 * g + 3]

        @pl.when(i == starts[g])
        def _():
            placed(orders[g], nat_ref, lt_ref)

        for k, right_ref in enumerate(rights):
            first, end = max(starts[g], k * per), min(starts[g] + steps[g], (k + 1) * per)

            @pl.when((i >= first) & (i < end))
            def _():
                half = keep_ref.shape[0]
                right = right_ref[...]
                send_ref[...] = dot(lt_ref[half:, :], right).astype(BF16)
                keep_ref[...] = dot(lt_ref[:half, :], right).astype(BF16)
                bsum_ref[...] = jnp.sum(right.astype(F32), axis=0, keepdims=True)


def wgrad(groups, lefts, right, tn=512, after=(), sends=(), cid=None):
    rights = right if isinstance(right, list) else [right]
    toks, width = rights[0].shape
    stacked = lefts[0].shape[0] < toks
    per = width // tn
    d = lefts[0].shape[1] if stacked else sum(left.shape[1] for left in lefts)
    steps = [cols // tn for _, cols in groups]
    starts = [sum(steps[:g]) for g in range(len(groups))]
    out_specs, out_shape = [], []
    for (_, cols), first, n in zip(groups, starts, steps):
        at = lambda i, *_, first=first, n=n: (0, jnp.clip(i - first, 0, n - 1))
        out_specs += [pl.BlockSpec((d // 2, tn), at)] * 2 + [pl.BlockSpec((1, tn), at)]
        out_shape += [jax.ShapeDtypeStruct((d // 2, cols), BF16)] * 2 + [jax.ShapeDtypeStruct((1, cols), F32)]
    cols = sum(r.shape[1] for r in rights)
    return call(
        functools.partial(wgrad_kernel, stacked, [o for o, _ in groups], steps, starts, per if len(rights) > 1 else sum(steps)),
        *lefts,
        *rights,
        grid=(sum(steps),),
        in_specs=[
            *[whole(left.shape) for left in lefts],
            *[pl.BlockSpec((toks, tn), lambda i, *_, k=k: (0, jnp.clip(i - k * per, 0, per - 1))) for k in range(len(rights))],
        ],
        out_specs=out_specs,
        scratch=[pltpu.VMEM((d, toks), F32), pltpu.VMEM((d, toks), BF16)],
        out_shape=out_shape,
        flops=2 * toks * d * cols,
        nbytes=2 * toks * (d + cols) + 2 * d * cols,
        name="wgrad",
        after=after,
        sends=sends,
        cid=cid,
    )


def wgrad_rows_kernel(turns_n, orders, groups, *refs):
    n = len(groups)
    (left_ref, right_ref), refs = refs[:2], refs[2:]
    outs, (nat_ref, lt_ref) = refs[: 2 * n], refs[2 * n :]
    i = pl.program_id(0)
    tile = left_ref.shape[1]

    @pl.when(i < turns_n)
    def _():
        turned(left_ref[...], nat_ref, 0)
        lt_ref[pl.ds(pl.multiple_of(i * tile, tile), tile), :] = nat_ref[...].astype(lt_ref.dtype)

    for g, (first, steps, lo, cols) in enumerate(groups):
        send_ref, keep_ref = outs[2 * g : 2 * g + 2]
        rows = send_ref.shape[0]

        @pl.when((i >= first) & (i < first + steps))
        def _():
            total = 1 << len(flat_bits(orders[g][0]))
            blocks = total // steps
            size = rows // blocks
            for b in range(blocks):
                spot = ((i - first) * blocks + b + total // 2) % total
                at = pl.ds(pl.multiple_of(source(spot, *orders[g]) * size, size), size)
                nat_ref[b * size : (b + 1) * size, :] = lt_ref[at, :].astype(F32)
            out = dot(nat_ref[:rows, :].astype(BF16), right_ref[:, lo : lo + cols]).astype(BF16)

            @pl.when(i < first + steps // 2)
            def _():
                send_ref[...] = out

            @pl.when(i >= first + steps // 2)
            def _():
                keep_ref[...] = out


def wgrad_rows(groups, left, right, tile=1024, after=(), sends=(), cid=None):
    toks, d = right.shape
    rows = left.shape[1]
    n = rows // tile
    half = n // 2
    orders = [o for o, _ in groups]
    kind = BF16 if (rows >> len(flat_bits(orders[0][0]))) % 16 == 0 else F32
    cuts, out_specs, out_shape, lo = [], [], [], 0
    for g, (_, cols) in enumerate(groups):
        first = n * (g + 1)
        cuts.append((first, n, lo, cols))
        lo += cols
        out_specs.append(pl.BlockSpec((tile, cols), lambda i, *_, first=first: (jnp.clip(i - first, 0, half - 1), 0)))
        out_specs.append(pl.BlockSpec((tile, cols), lambda i, *_, first=first: (jnp.clip(i - first - half, 0, half - 1), 0)))
        out_shape += [jax.ShapeDtypeStruct((rows // 2, cols), BF16)] * 2
    return call(
        functools.partial(wgrad_rows_kernel, n, orders, cuts),
        left,
        right,
        grid=(n * (1 + len(groups)),),
        in_specs=[
            pl.BlockSpec((toks, tile), lambda i, *_: (0, jnp.minimum(i, n - 1))),
            pl.BlockSpec((toks, d), lambda i, *_: (0, 0)),
        ],
        out_specs=out_specs,
        scratch=[pltpu.VMEM((tile, toks), F32), pltpu.VMEM((rows, toks), kind)],
        out_shape=out_shape,
        flops=2 * toks * rows * d,
        nbytes=2 * (rows * (d + toks) + toks * d),
        name="wgrad_rows",
        after=after,
        sends=sends,
        cid=cid,
    )


def d_ctx_kernel(a_ref, w_ref, out_ref):
    out_ref[...] = dot_t(a_ref[...], w_ref[...]).astype(BF16)


def d_context(grad, w, tn=256, after=(), sends=(), cid=None):
    rows, d = grad.shape
    return call(
        d_ctx_kernel,
        grad, w,
        grid=(d // tn,),
        in_specs=[whole((rows, d)), pl.BlockSpec((tn, d), lambda i: (i, 0))],
        out_specs=[pl.BlockSpec((rows, tn), lambda i: (0, i))],
        out_shape=[jax.ShapeDtypeStruct((rows, d), BF16)],
        flops=2 * rows * d * d, nbytes=2 * d * (2 * rows + d),
        name="d_ctx",
        after=after,
        sends=sends,
        cid=cid,
    )


def lane_ids(rows):
    return lax.broadcasted_iota(jnp.int32, (rows, LANES), 1)


def turns():
    frm = lax.broadcasted_iota(jnp.int32, (LANES, LANES), 0)
    to = lax.broadcasted_iota(jnp.int32, (LANES, LANES), 1)
    half = ROT // 2
    within = frm % HEAD
    partner = jnp.where(within < half, frm + half, frm - half)
    rotated = within < ROT
    turned = (frm + HEAD) % LANES
    one = lambda hit: jnp.where(hit, 1.0, 0.0).astype(BF16)
    return one(turned == to), one(rotated & (partner == to)), one(rotated & ((partner + HEAD) % LANES == to))


def split(x):
    high = x.astype(BF16)
    return jnp.concatenate([high, (x - high.astype(F32)).astype(BF16)], axis=1)


def qkv_kernel(n, *refs):
    a_refs, (w_ref, bias_ref, cos_ref, sin_ref, q_ref, k_ref, v_ref) = refs[:n], refs[n:]
    turn, swap, swap_turn = turns()
    k_moves = jnp.concatenate([turn, swap_turn], axis=1)
    k_moves = jnp.concatenate([k_moves, k_moves], axis=0)
    q_moves = jnp.concatenate([swap, swap], axis=0)
    r = 0
    for a_ref in a_refs:
        rows = slice(r, r + a_ref.shape[0])
        r += a_ref.shape[0]
        first = lane_ids(a_ref.shape[0]) < HEAD
        packed = dot(a_ref[...], w_ref[...]) + bias_ref[...]
        cos, sin = cos_ref[rows, :], sin_ref[rows, :]
        for g in range(w_ref.shape[1] // PAIR):
            c = g * PAIR
            lanes = slice(g * LANES, (g + 1) * LANES)
            pa, pb, pc = packed[:, c : c + LANES], packed[:, c + LANES : c + 2 * LANES], packed[:, c + 2 * LANES : c + PAIR]
            both = dot(split(jnp.where(first, pc, pa)), k_moves)
            k_ref[rows, lanes] = (both[:, :LANES] * cos + both[:, LANES:] * sin).astype(BF16)
            v_ref[rows, lanes] = jnp.where(first, pb, pc).astype(BF16)
            if a_ref is a_refs[-1]:
                q = jnp.where(first, pa, pb)
                q_ref[:, lanes] = (q * cos + dot(split(q), q_moves) * sin).astype(BF16)


def qkv(pieces, w, bias, cos, sin, group=4, after=()):
    toks, d = pieces[-1].shape
    win = sum(p.shape[0] for p in pieces)
    cols = w.shape[1]
    out = pl.BlockSpec((win, group * LANES), lambda i: (0, i))
    return call(
        functools.partial(qkv_kernel, len(pieces)),
        *pieces, w, bias, cos, sin,
        grid=(cols // PAIR // group,),
        in_specs=[
            *[whole(p.shape) for p in pieces],
            pl.BlockSpec((d, group * PAIR), lambda i: (0, i)),
            pl.BlockSpec((1, group * PAIR), lambda i: (0, i)),
            whole((win, LANES)),
            whole((win, LANES)),
        ],
        out_specs=[pl.BlockSpec((toks, group * LANES), lambda i: (0, i)), out, out],
        out_shape=[jax.ShapeDtypeStruct((toks, cols // 3), BF16)] + [jax.ShapeDtypeStruct((win, cols // 3), BF16)] * 2,
        flops=2 * win * d * cols, nbytes=8 * win * d + 2 * d * cols,
        name="qkv",
        after=after,
    )


GROUP = 2
QB = 256


def attention_kernel(
    toks, win, start_ref, q_ref, k_ref, v_ref, do_ref, cos_ref, sin_ref, ctx_ref, dp_ref,
    k2, v2, kt, vt, s_ref, e_ref, dq_acc, dk_acc, dv_acc,
):
    nk = win // BLOCK
    halo = win - toks
    first = lane_ids(BLOCK) < HEAD
    first_q = lane_ids(QB) < HEAD
    zero = jnp.zeros((BLOCK, LANES), BF16)
    zero_q = jnp.zeros((QB, LANES), BF16)
    top = lax.broadcasted_iota(jnp.int32, (LANES, QB), 0) < HEAD
    groups = range(GROUP)
    lanes = [slice(g * LANES, (g + 1) * LANES) for g in groups]
    eye = lax.broadcasted_iota(jnp.int32, (LANES, LANES), 0) == lax.broadcasted_iota(jnp.int32, (LANES, LANES), 1)
    upper = lax.broadcasted_iota(jnp.int32, (LANES, LANES), 0) < HEAD
    eye0 = jnp.where(eye & upper, 1.0, 0.0).astype(BF16)
    eye1 = jnp.where(eye & ~upper, 1.0, 0.0).astype(BF16)

    def prepare(j, _):
        rows = pl.ds(pl.multiple_of(j * BLOCK, BLOCK), BLOCK)
        for g in groups:
            for src, two, tr in ((k_ref, k2, kt), (v_ref, v2, vt)):
                x = src[rows, lanes[g]]
                two[g, j, :BLOCK, :] = jnp.where(first, x, zero)
                two[g, j, BLOCK:, :] = jnp.where(first, zero, x)
                tr[g, j, :, :BLOCK] = dot_t(eye0, x).astype(BF16)
                tr[g, j, :, BLOCK:] = dot_t(eye1, x).astype(BF16)
        return 0

    lax.fori_loop(0, nk, prepare, 0)
    dk_acc[...] = jnp.zeros_like(dk_acc)
    dv_acc[...] = jnp.zeros_like(dv_acc)
    scale = HEAD**-0.5
    for i in range(toks // QB):
        rows = slice(i * QB, (i + 1) * QB)
        last = (halo + (i + 1) * QB) // BLOCK
        low = max(halo + i * QB - DOC_MOST + 1, 0) // BLOCK
        qs = [q_ref[rows, lanes[g]].astype(F32) * scale for g in groups]
        qts = [q.T.astype(BF16) for q in qs]
        qs = [q.astype(BF16) for q in qs]
        q2 = [jnp.concatenate([jnp.where(first_q, q, zero_q), jnp.where(first_q, zero_q, q)], axis=0) for q in qs]
        start = start_ref[:, rows]
        q_at = halo + i * QB + lax.broadcasted_iota(jnp.int32, (1, QB), 1)

        def scores(j, peaks):
            at = j * BLOCK + lax.broadcasted_iota(jnp.int32, (BLOCK, QB), 0)
            ok = (at >= start) & (at <= q_at)
            out = []
            for g in groups:
                s = dot(k2[g, j], qts[g])
                s0 = jnp.where(ok, s[:BLOCK], NEG)
                s1 = jnp.where(ok, s[BLOCK:], NEG)
                s_ref[g, j, :BLOCK, :] = s0
                s_ref[g, j, BLOCK:, :] = s1
                out.append(jnp.maximum(peaks[2 * g], jnp.max(s0, axis=0, keepdims=True)))
                out.append(jnp.maximum(peaks[2 * g + 1], jnp.max(s1, axis=0, keepdims=True)))
            return tuple(out)

        floor = jnp.full((1, QB), NEG, F32)
        peaks = lax.fori_loop(low, last, scores, (floor,) * (2 * GROUP), unroll=True)

        def weigh(j, carry):
            out = []
            for g in groups:
                t0, t1, acc = carry[3 * g : 3 * g + 3]
                e0 = jnp.exp(s_ref[g, j, :BLOCK, :] - peaks[2 * g])
                e1 = jnp.exp(s_ref[g, j, BLOCK:, :] - peaks[2 * g + 1])
                b0, b1 = e0.astype(BF16), e1.astype(BF16)
                e_ref[g, j, :BLOCK, :] = b0
                e_ref[g, j, BLOCK:, :] = b1
                acc = acc + dot(vt[g, j], jnp.concatenate([b0, b1], axis=0))
                out += [t0 + jnp.sum(e0, axis=0, keepdims=True), t1 + jnp.sum(e1, axis=0, keepdims=True), acc]
            return tuple(out)

        none = jnp.zeros((1, QB), F32)
        sums = lax.fori_loop(low, last, weigh, (none, none, jnp.zeros((LANES, QB), F32)) * GROUP, unroll=True)
        do_l, do2, d0, d1 = [], [], [], []
        for g in groups:
            t0, t1, acc = sums[3 * g : 3 * g + 3]
            share = jnp.where(top, 1.0 / t0, 1.0 / t1)
            ctx_t = acc * share
            ctx_ref[rows, lanes[g]] = ctx_t.T.astype(BF16)
            do_t = do_ref[rows, lanes[g]].astype(F32).T * share
            both = do_t * ctx_t
            d0.append(jnp.sum(both[:HEAD], axis=0, keepdims=True))
            d1.append(jnp.sum(both[HEAD:], axis=0, keepdims=True))
            do = do_t.T.astype(BF16)
            do_l.append(do_t.astype(BF16))
            do2.append(jnp.concatenate([jnp.where(first_q, do, zero_q), jnp.where(first_q, zero_q, do)], axis=0))

        def back(j, dqs):
            at = pl.ds(pl.multiple_of(j * BLOCK, BLOCK), BLOCK)
            out = []
            for g in groups:
                dp = dot(v2[g, j], do_l[g])
                e0, e1 = e_ref[g, j, :BLOCK, :], e_ref[g, j, BLOCK:, :]
                ds0 = (e0.astype(F32) * (dp[:BLOCK] - d0[g])).astype(BF16)
                ds1 = (e1.astype(F32) * (dp[BLOCK:] - d1[g])).astype(BF16)
                dv_acc[at, lanes[g]] += dot(jnp.concatenate([e0, e1], axis=1), do2[g])
                dk_acc[at, lanes[g]] += dot(jnp.concatenate([ds0, ds1], axis=1), q2[g])
                out.append(dqs[g] + dot(kt[g, j], jnp.concatenate([ds0, ds1], axis=0)))
            return tuple(out)

        dqs = lax.fori_loop(low, last, back, (jnp.zeros((LANES, QB), F32),) * GROUP, unroll=True)
        for g in groups:
            dq_acc[rows, lanes[g]] = dqs[g].T * scale

    turn, swap, swap_turn = turns()
    for j in range(nk):
        rows = slice(j * BLOCK, (j + 1) * BLOCK)
        cos, sin = cos_ref[rows, :], sin_ref[rows, :]
        for g in groups:
            dk = dk_acc[rows, lanes[g]].astype(BF16)
            dk = dot(dk, turn) * cos - dot(dk, swap_turn) * sin
            dv = dv_acc[rows, lanes[g]]
            if j * BLOCK >= halo:
                own = slice(j * BLOCK - halo, (j + 1) * BLOCK - halo)
                dq = dq_acc[own, lanes[g]]
                dq = dq * cos - dot(dq.astype(BF16), swap) * sin
            else:
                dq = jnp.zeros_like(dk)
            c = g * PAIR
            dp_ref[rows, c : c + LANES] = jnp.where(first, dq, dk).astype(BF16)
            dp_ref[rows, c + LANES : c + 2 * LANES] = jnp.where(first, dv, dq).astype(BF16)
            dp_ref[rows, c + 2 * LANES : c + PAIR] = jnp.where(first, dk, dv).astype(BF16)


def attention(start, q, k, v, d_ctx, cos, sin, pair, pairs, after=(), sends=(), cid=None):
    win, d = k.shape
    toks = d_ctx.shape[0]
    nk = win // BLOCK
    width = GROUP * LANES
    at = pair // GROUP
    own = pl.BlockSpec((toks, width), lambda i: (0, at + i))
    every = pl.BlockSpec((win, width), lambda i: (0, at + i))
    out = pairs * LANES
    return call(
        functools.partial(attention_kernel, toks, win),
        start,
        q,
        k,
        v,
        d_ctx,
        cos,
        sin,
        grid=(pairs // GROUP,),
        in_specs=[whole((1, toks)), own, every, every, own, whole((win, LANES)), whole((win, LANES))],
        out_specs=[pl.BlockSpec((toks, width), lambda i: (0, i)), pl.BlockSpec((win, GROUP * PAIR), lambda i: (0, i))],
        out_shape=[jax.ShapeDtypeStruct((toks, out), BF16), jax.ShapeDtypeStruct((win, 3 * out), BF16)],
        scratch=[
            pltpu.VMEM((GROUP, nk, 2 * BLOCK, LANES), BF16),
            pltpu.VMEM((GROUP, nk, 2 * BLOCK, LANES), BF16),
            pltpu.VMEM((GROUP, nk, LANES, 2 * BLOCK), BF16),
            pltpu.VMEM((GROUP, nk, LANES, 2 * BLOCK), BF16),
            pltpu.VMEM((GROUP, nk, 2 * BLOCK, QB), F32),
            pltpu.VMEM((GROUP, nk, 2 * BLOCK, QB), BF16),
            pltpu.VMEM((toks, width), F32),
            pltpu.VMEM((win, width), F32),
            pltpu.VMEM((win, width), F32),
        ],
        flops=pairs * toks * DOC_MOST * 4 * 6 * LANES,
        nbytes=14 * win * out,
        trans=pairs * 2 * toks * DOC_MOST,
        name="attention",
        after=after,
        sends=sends,
        cid=cid,
    )


def tail_kernel(cfg, *refs):
    ndp, nseq, halos, n_pieces, n_dp, n_ctx, joins, last_c = cfg
    refs = list(refs)
    take = lambda n: [refs.pop(0) for _ in range(n)]
    dp_rows, (w_ref,), dp_cols, pieces, ctxs = take(n_dp), take(1), take(n_dp - 2), take(n_pieces), take(n_ctx)
    grad_ref, x_ref, mlp_ref, d_mlp_ref, wd_ref, bias_ref, g1, g2 = take(8)
    gsum_ref, qsum_ref, isum_ref = take(3)
    left_q, own_q = take(2)
    hidden_ref, grad_in_ref, small = take(3)
    owns = take(3)
    last_gots = [take(len(fan(last_c)) - 1) for _ in owns]
    nat, lt, own_acc, far, far_got = take(5)
    group_bufs = [take(6), take(6), [None, own_q.at[0], None, left_q, *take(2)]]
    bsum_ref, small_got = take(2)
    send_sem, recv_sem = refs
    toks, d = x_ref.shape
    me_dp, me_seq = lax.axis_index("dp"), lax.axis_index("seq")
    dp_bits = stage_bits(ndp)
    core, cross = fan(dp_bits[:1]), fan(dp_bits[1:])
    across = fan(last_c)

    def device(axis, offset):
        return (me_dp ^ offset, me_seq) if axis == "dp" else (me_dp, me_seq ^ offset)

    behind = (me_dp, lax.rem(me_seq + nseq - 1, nseq))
    ahead = (me_dp, lax.rem(me_seq + 1, nseq))
    names = {}

    def copy(name, src, dst, to):
        k = names.setdefault(name, len(names))
        return pltpu.make_async_remote_copy(
            src_ref=src,
            dst_ref=dst,
            send_sem=send_sem.at[k],
            recv_sem=recv_sem.at[k],
            device_id=to,
            device_id_type=pl.DeviceIdType.MESH,
        )

    far_copy = lambda k: copy(("far", k), far.at[k], far_got.at[k], behind)

    def first(n):
        send, _, got, *_ = group_bufs[n]
        return copy(("core", n), send, got, device("dp", core[1]))

    def second(n):
        _, _, _, out, into, _ = group_bufs[n]
        start = 1 if n < 2 else 0
        return [copy(("cross", n, k), out.at[k - start], into.at[k - 1], device("dp", cross[k])) for k in range(1, len(cross))]

    def third(n):
        out, got = group_bufs[n][5], last_gots[(n + 1) % 3]
        return [copy(("across", n, k), out.at[k - 1], got[k - 1], device("seq", across[k])) for k in range(1, len(across))]

    def to_second(n):
        _, keep, got, out, _, _ = group_bufs[n]
        first(n).wait()
        rows = out.shape[1]
        for k, c in enumerate(second(n), 1):
            at = slice(k * rows, (k + 1) * rows)
            out[k - 1] = (keep[at, :].astype(F32) + got[at, :].astype(F32)).astype(BF16)
            c.start()

    def to_third(n):
        _, keep, got, _, into, out = group_bufs[n]
        for c in second(n):
            c.wait()
        own = owns[(n + 1) % 3]
        rows = own.shape[0]
        copies = third(n)
        for k in reversed(range(len(across))):
            at = slice(k * rows, (k + 1) * rows)
            total = keep[at, :].astype(F32)
            if got is not None:
                total += got[at, :].astype(F32)
            for b in range(len(cross) - 1):
                total += into[b, at, :].astype(F32)
            if k:
                out[k - 1] = total.astype(out.dtype)
                copies[k - 1].start()
            else:
                own[...] = total

    def pass_on(k):
        far_copy(k - 1).wait()
        far[k] = (far[k].astype(F32) + far_got[k - 1].astype(F32)).astype(BF16)
        far_copy(k).start()

    def back(cols=None):
        total, at = None, 0
        for a_ref in dp_rows:
            n = a_ref.shape[1]
            term = dot_t(a_ref[...], w_ref[:, at : at + n])
            total, at = term if total is None else total + term, at + n
        return total

    step = [0]
    pid = pl.program_id(0)

    def phase(fn):
        pl.when(pid == step[0])(fn)
        step[0] += 1

    for k in range(halos):

        def do_far(k=k):
            if k == 0:
                offsets = [("dp", o) for o in (*core[1:], *cross[1:])] + [("seq", o) for o in across[1:]]
                greet([device(*o) for o in offsets] + [behind, ahead])
                for c in second(2):
                    c.start()
            far[k] = back().astype(BF16)
            if k == 0:
                far_copy(0).start()

        phase(do_far)

    def do_columns():
        col = 0
        for left in pieces:
            n = left.shape[0]
            turned(left[...], nat.at[:, :n], 0)
            placed((short_order(ndp, nseq), nseq), nat.at[:, :n], lt.at[:, col : col + n])
            col += n
        send, keep = group_bufs[0][:2]
        half, at = keep.shape[0], 0
        for right_ref in dp_cols:
            right = right_ref[...]
            n = right.shape[1]
            send[:, at : at + n] = dot(lt[half:, :], right).astype(BF16)
            keep[:, at : at + n] = dot(lt[:half, :], right).astype(BF16)
            bsum_ref[:, at : at + n] = jnp.sum(right.astype(F32), axis=0, keepdims=True)
            at += n
        first(0).start()

    phase(do_columns)

    def do_dense():
        at = 0
        for ctx in ctxs:
            turned(ctx[...], nat, at)
            at += ctx.shape[1]
        placed((short_order(ndp, nseq), nseq), nat, lt.at[:, :toks])
        send, keep = group_bufs[1][:2]
        half = keep.shape[0]
        send[...] = dot(lt[half:, :toks], grad_ref[...]).astype(BF16)
        first(1).start()
        keep[...] = dot(lt[:half, :toks], grad_ref[...]).astype(BF16)
        to_second(0)
        to_third(2)

    phase(do_dense)

    def do_own():
        own_acc[...] = back()
        to_second(1)

    phase(do_own)
    for t in range(joins):

        def do_join(t=t):
            cols = hidden_ref.shape[1]
            at = slice(t * cols, (t + 1) * cols)
            total, row = x_ref[:, at].astype(F32) + mlp_ref[...] + bias_ref[:, at], 0
            for ctx in ctxs:
                n = ctx.shape[1]
                total += dot(ctx[...], wd_ref[row : row + n, :])
                row += n
            hidden_ref[...] = total.astype(BF16)
            if t == 0 and halos > 1:
                pass_on(1)

        phase(do_join)

    def do_rest():
        for k in range(2, halos):
            pass_on(k)
        to_third(0)
        to_third(1)
        far_copy(halos - 1).wait()
        small[...] = jnp.zeros_like(small)
        rows = min(128, toks)
        for r in range(0, toks, rows):
            at = slice(r, r + rows)
            u, inv = unit_of(x_ref[at, :].astype(F32))
            d1 = own_acc[at, :] + far_got[halos - 1, at, :].astype(F32)
            d2 = d_mlp_ref[at, :]
            e = d1 * g1[...] + d2 * g2[...]
            dx = inv * (e - jnp.mean(e, axis=-1, keepdims=True) - u * jnp.mean(e * u, axis=-1, keepdims=True))
            grad_in_ref[at, :] = grad_ref[at, :].astype(F32) + dx
            for k, v in enumerate((d1 * u, d1, d2 * u, d2)):
                small[k : k + 1, :] += jnp.sum(v, axis=0, keepdims=True)
        small[4:5, :] = gsum_ref[...]
        row = 5
        for parts in ((qsum_ref, bsum_ref), (isum_ref,)):
            flat = jnp.concatenate([p[...] for p in parts], axis=1)
            for c in range(0, flat.shape[1], d):
                small[row : row + 1, :] = flat[:, c : c + d]
                row += 1
        used = 0
        for axis, offsets in (("dp", core), ("dp", cross), ("seq", across)):
            copies = []
            for o in offsets[1:]:
                copies.append(copy(("small", used), small, small_got.at[used], device(axis, o)))
                copies[-1].start()
                used += 1
            for c in copies:
                c.wait()
            total = small[...]
            for k in range(used - len(copies), used):
                total += small_got[k]
            small[...] = total
        for c in third(0) + third(1) + third(2):
            c.wait()

    phase(do_rest)


def tail(dps, w, pieces, ctxs, grad, x, mlp_out, d_mlp, w_d, bias, g1, g2, sums, left_q, ndp, nseq, halos, after=()):
    toks, d = x.shape
    depth = w.shape[1]
    joins = 4
    own_at = halos + 2
    dp_bits, seq_bits = stage_bits(ndp), stage_bits(nseq)
    cross, across = 1 << len(dp_bits[1:]), 1 << len(seq_bits)
    tile = d // joins
    once = lambda shape: pl.BlockSpec(shape, lambda i: (0,) * len(shape), pipeline_mode=pl.Buffered(1))
    piece_at = lambda i: (jnp.where(i < halos, i, jnp.where(i < own_at, halos - 1, halos)), 0)
    join_at = lambda i: (0, jnp.clip(i - own_at - 1, 0, joins - 1))
    hbm = pl.BlockSpec(memory_space=pl.ANY)
    cut_up = lambda a, n: a.reshape(n, a.shape[0] // n, a.shape[1])
    left_q = cut_up(left_q, cross)
    ins = [*dps, w, *dps[2:], *pieces, *ctxs, grad, x, mlp_out, d_mlp, w_d, bias, g1, g2, *sums, left_q, left_q]
    in_specs = (
        [pl.BlockSpec((toks, a.shape[1]), piece_at) for a in dps]
        + [once(w.shape)]
        + [once(a.shape) for a in dps[2:]]
        + [once(p.shape) for p in pieces]
        + [once(c.shape) for c in ctxs]
        + [once((toks, d))] * 2
        + [pl.BlockSpec((toks, tile), join_at), once((toks, d)), pl.BlockSpec((d, tile), join_at)]
        + [once((1, d))] * 3
        + [once(v.shape) for v in sums]
        + [hbm, once((1, *left_q.shape[1:]))]
    )
    rest = sum(a.shape[1] for a in dps[2:])
    lines = 4 + sum(v.shape[1] for v in sums) // d + 1
    lines += -lines % 8
    widths = [left_q.shape[2], rest, d]
    left = d // 2 // cross // across
    kind = BF16 if left % 16 == 0 else F32
    out_shape = [
        jax.ShapeDtypeStruct((toks, d), BF16),
        jax.ShapeDtypeStruct((toks, d), F32),
        jax.ShapeDtypeStruct((lines, d), F32),
        *[jax.ShapeDtypeStruct((left, n), F32) for n in widths],
        *[jax.ShapeDtypeStruct((left, n), kind) for n in widths for _ in range(across - 1)],
    ]
    fixed = lambda shape: pl.BlockSpec(shape, lambda i: (0,) * len(shape))
    out_specs = (
        [pl.BlockSpec((toks, tile), join_at), fixed((toks, d))]
        + [fixed((lines, d))]
        + [fixed((left, n)) for n in widths]
        + [hbm] * (len(widths) * (across - 1))
    )
    scratch = [
        pltpu.VMEM((d, toks), F32),
        pltpu.VMEM((d, toks * (halos + 1)), BF16),
        pltpu.VMEM((toks, d), F32),
        pltpu.VMEM((halos, toks, d), BF16),
        pltpu.VMEM((halos, toks, d), BF16),
    ]
    for n in widths[1:]:
        scratch += [pltpu.VMEM((d // 2, n), BF16)] * 3
        scratch += [pltpu.VMEM((cross - 1, d // 2 // cross, n), BF16)] * 2
        scratch += [pltpu.VMEM((across - 1, left, n), kind)]
    scratch += [pltpu.VMEM((cross - 1, *left_q.shape[1:]), BF16), pltpu.VMEM((across - 1, left, widths[0]), kind)]
    scratch += [pltpu.VMEM((1, rest), F32), pltpu.VMEM((1 + cross - 1 + across - 1, lines, d), F32)]
    copies = halos + 4 * (1 + cross - 1 + across - 1)
    scratch += [pltpu.SemaphoreType.DMA((copies,))] * 2
    cfg = (ndp, nseq, halos, len(pieces), len(dps), len(ctxs), joins, seq_bits)
    n = len(ins)

    def body(*refs):
        tail_kernel(cfg, *refs[:n], *refs[n + len(after) :])

    outs = pl.pallas_call(
        body,
        grid_spec=pltpu.PrefetchScalarGridSpec(
            num_scalar_prefetch=0,
            grid=(own_at + 1 + joins + 1,),
            in_specs=in_specs + [hbm] * len(after),
            out_specs=out_specs,
            scratch_shapes=scratch,
        ),
        out_shape=out_shape,
        compiler_params=pltpu.CompilerParams(vmem_limit_bytes=63 * MIB, collective_id=1, has_side_effects=True),
        cost_estimate=pl.CostEstimate(flops=20 * toks * d * depth, bytes_accessed=40 * toks * d, transcendentals=0),
        name="tail",
    )(*ins, *after)
    outs = list(outs)
    main, own, outs = outs[:3], outs[3:6], outs[6:]
    terms = []
    for a in own:
        terms.append(([(v, 0) for v in (a, *outs[: across - 1])], 0, left, F32))
        outs = outs[across - 1 :]
    return main, terms


def shards(
    hidden_in,
    doc_lengths,
    ln1_gain,
    ln1_bias,
    ln2_gain,
    ln2_bias,
    qkv_weight,
    qkv_bias,
    dense_weight,
    dense_bias,
    fc_in_weight,
    fc_in_bias,
    fc_out_weight,
    fc_out_bias,
    out_grad,
):
    _, toks, d = hidden_in.shape
    ff = fc_in_weight.shape[1]
    ndp, nseq = lax.axis_size("dp"), lax.axis_size("seq")
    ndev = ndp * nseq
    sizes = {"dp": ndp, "seq": nseq}
    me_dp, me_seq = lax.axis_index("dp"), lax.axis_index("seq")
    row = lambda v: v.reshape(1, -1)

    halos = min(-(-(DOC_MOST - 1) // toks), nseq - 1)
    halos = max(halos, 1)
    win = (halos + 1) * toks
    base = (me_seq - halos) * toks
    lengths = doc_lengths.reshape(-1)
    docs = lengths.shape[0]
    doc = jnp.arange(docs, dtype=jnp.int32)
    ends = jnp.sum(jnp.where(doc[None, :] <= doc[:, None], lengths[None, :], 0), axis=1)
    at = base + jnp.arange(win, dtype=jnp.int32)
    begin = jnp.max(jnp.where(at[:, None] >= ends[None, :], ends[None, :], 0), axis=1)
    doc_pos = at - begin
    live = (at[halos * toks :] < ends[docs - 2]).astype(F32).reshape(toks, 1)
    start = (begin - base)[halos * toks :]
    lane = jnp.arange(LANES, dtype=jnp.int32) % HEAD
    half = ROT // 2
    freq = 10000.0 ** (-(2.0 * (lane % half).astype(F32)) / ROT)
    angle = doc_pos.astype(F32)[:, None] * freq[None, :]
    cos = jnp.where(lane < ROT, jnp.cos(angle), 1.0)
    sin = jnp.where(lane < half, -1.0, jnp.where(lane < ROT, 1.0, 0.0)) * jnp.sin(angle)

    x = hidden_in.reshape(toks, d)
    a_own, m_own, grad, grad_sum = norms(
        x, out_grad.reshape(toks, d), live, row(ln1_gain), row(ln1_bias), row(ln2_gain), row(ln2_bias)
    )

    ahead = [(i, (i + 1) % nseq) for i in range(nseq)]
    on = ("ring", 1, nseq)
    mlp_out, act, d_pre, d_mlp, b_in_sum, near = mlp(
        m_own, grad, fc_in_weight, row(fc_in_bias), fc_out_weight, sends=[(a_own, 0, toks, on)], cid=2
    )
    pieces = [a_own, near]

    orders = [stage_order(ndp, nseq, kind) for kind in range(3)]
    srcs = [(o, nseq) for o in orders]
    in_cut, out_cut = ff * 5 // 8, d // 4
    hop = [[(near, k * toks // 2, toks // 2, on)] if halos > 1 else [] for k in range(2)]
    s0, k0, _, s1, k1, _, *far_low = wgrad(
        [(srcs[0], in_cut), (srcs[2], ff - in_cut)], [m_own], d_pre, sends=hop[0], cid=3 if hop[0] else None
    )
    early = [Halving(s0, k0, orders[0], sizes), Halving(s1, k1, orders[2], sizes)]
    s2, k2, s3, k3, *got = wgrad_rows(
        [(srcs[2], out_cut), (srcs[1], d - out_cut)],
        act,
        grad,
        after=far_low,
        sends=[send for r in early for send in r.sends()] + hop[1],
        cid=4,
    )
    for r in early:
        r.receive([got.pop(0)])
    if halos > 1:
        pieces += [got[0], far_low[0]]
    for k in range(2, halos):
        after_two = jnp.concatenate([pieces[3], pieces[2]], axis=0) if k == 2 else pieces[-1]
        pieces.append(lax.ppermute(after_two, "seq", ahead))
    late = [Halving(s2, k2, orders[2], sizes), Halving(s3, k3, orders[1], sizes)]
    fc = early + late
    d_ctx, *got = d_context(grad, dense_weight, sends=[send for r in late for send in r.sends()], cid=5)
    for r in late:
        r.receive([got.pop(0)])
    last = advance(fc, [d_ctx])
    for r in fc:
        r.permute()
    pieces = pieces[::-1]
    q, k, v = qkv(pieces, qkv_weight, row(qkv_bias), cos, sin, after=last)

    order_c = short_order(ndp, nseq)
    src_c = (order_c, nseq)
    pairs = d // LANES
    quarter = pairs // 4

    def part(at, n, sums=(), **more):
        sends = [send for r in sums for send in r.sends()]
        ctx, dp, *got = attention(
            row(start), q, k, v, d_ctx, cos, sin, at * quarter, n * quarter, sends=sends, cid=6 + at if sends else None, **more
        )
        for r in sums:
            r.receive([got.pop(0) for _ in r.targets()])
        return ctx, dp

    ctx_a, dp_a = part(0, 1)
    advance(fc, [ctx_a])
    ctx_b, dp_b = part(1, 1, fc)
    advance(fc, [ctx_b])
    qa_send, qa_keep, b_qkv_a, *got = wgrad(
        [(src_c, dp_a.shape[1] * 2)], pieces, [dp_a, dp_b], tn=dp_a.shape[1], sends=[send for r in fc for send in r.sends()], cid=10
    )
    for r in fc:
        r.receive([got.pop(0) for _ in r.targets()])
    r_qa = Halving(qa_send, qa_keep, order_c, sizes)
    last = advance(fc, [b_qkv_a])
    while len(fc[0].stages) > 1:
        for r in fc:
            r.permute()
        last = advance(fc, last)
    ctx_c, dp_c = part(2, 2, [*fc, r_qa])
    left_q, g_in, g_out = combine([r_qa.rest(), *[(*r.rest()[:3], F32) for r in fc]], [ctx_c], joined=(2, 4))
    main, terms = tail(
        [dp_a, dp_b, dp_c],
        qkv_weight,
        pieces,
        [ctx_a, ctx_b, ctx_c],
        grad,
        x,
        mlp_out,
        d_mlp,
        dense_weight,
        row(dense_bias + fc_out_bias),
        row(ln1_gain),
        row(ln2_gain),
        [grad_sum, b_qkv_a, b_in_sum],
        left_q,
        ndp,
        nseq,
        halos,
    )
    hidden_out, grad_in, small = main
    g_qkv, g_dense = combine(terms, joined=(1,))
    mine = lambda lo, rows: lax.dynamic_slice_in_dim(
        small[lo : lo + rows].reshape(-1), (me_dp * nseq + me_seq) * (rows * d // ndev), rows * d // ndev
    )
    o1g, o1b, o2g, o2b, o_db = (mine(k, 1) for k in range(5))
    o_qb, o_ib = mine(5, 3), mine(8, ff // d)
    return (
        hidden_out.reshape(hidden_in.shape),
        grad_in.reshape(hidden_in.shape),
        o1g,
        o1b,
        o2g,
        o2b,
        g_qkv,
        o_qb,
        g_dense,
        o_db,
        g_in,
        o_ib,
        g_out,
        o_db,
    )


def solution(mesh):
    both = P(("dp", "seq"))
    rows = P(("dp", "seq"), None)
    toks = P("dp", "seq", None)
    return jax.shard_map(
        shards,
        mesh=mesh,
        in_specs=(toks, P("dp", None)) + (P(),) * 12 + (toks,),
        out_specs=(toks, toks, both, both, both, both, rows, both, rows, both, rows, both, rows, both),
        check_vma=False,
    )
```

```python
import functools
import math

import jax
import jax.numpy as jnp
from jax import lax
from jax.experimental import pallas as pl
from jax.experimental.pallas import tpu as pltpu
from jax.sharding import PartitionSpec as P

HEADS = 16
HEAD = 64
ROT = 16
DOC_MOST = 1024
EPS = 1e-05
NEG = -1e30
LANES = 128
PAIR = 3 * LANES
BLOCK = 256
F32 = jnp.float32
BF16 = jnp.bfloat16
MIB = 1 << 20
VMEM_MIB = 56


def dot(a, b):
    return lax.dot_general(a, b, (((1,), (0,)), ((), ())), preferred_element_type=F32)


def dot_t(a, b):
    return lax.dot_general(a, b, (((1,), (1,)), ((), ())), preferred_element_type=F32)


def whole(shape):
    return pl.BlockSpec(shape, lambda *_: (0,) * len(shape))


def place(to):
    at = {"dp": lax.axis_index("dp"), "seq": lax.axis_index("seq")}
    if to[0] == "ring":
        at["seq"] = lax.rem(at["seq"] + to[1] + to[2], to[2])
    else:
        at[to[0]] = at[to[0]] ^ to[1]
    return (at["dp"], at["seq"])


def both_ways(targets):
    back = [("ring", -to[1], to[2]) for to in targets if to[0] == "ring"]
    return [place(to) for to in sorted({*targets, *back})]


def greet(devices):
    barrier = pltpu.get_barrier_semaphore()
    for device in devices:
        pl.semaphore_signal(barrier, inc=1, device_id=device, device_id_type=pl.DeviceIdType.MESH)
    pl.semaphore_wait(barrier, len(devices))


def call(kernel, *args, grid, in_specs, out_specs, out_shape, name, flops, nbytes, trans=0, scalars=0, scratch=(), after=(), sends=(), cid=None):
    n, n_out, m = scalars + len(in_specs), len(out_specs), len(sends)

    def body(*refs):
        refs = list(refs)
        ins, _, srcs = refs[:n], refs[n : n + len(after)], refs[n + len(after) :][:m]
        rest = refs[n + len(after) + m :]
        outs, gots, own = rest[:n_out], rest[n_out : n_out + m], rest[n_out + m :]
        if not m:
            kernel(*ins, *outs, *own)
            return
        *own, send_sem, recv_sem = own

        def copy(k):
            _, lo, rows, to = sends[k]
            return pltpu.make_async_remote_copy(
                src_ref=srcs[k].at[pl.ds(lo, rows)],
                dst_ref=gots[k],
                send_sem=send_sem.at[k],
                recv_sem=recv_sem.at[k],
                device_id=place(to),
                device_id_type=pl.DeviceIdType.MESH,
            )

        @pl.when(pl.program_id(0) == 0)
        def _():
            greet(both_ways([to for *_, to in sends]))
            for k in range(m):
                copy(k).start()

        kernel(*ins, *outs, *own)

        @pl.when(pl.program_id(0) == grid[0] - 1)
        def _():
            for k in range(m):
                copy(k).wait()

    hbm = pl.BlockSpec(memory_space=pl.ANY)
    more = dict(collective_id=cid, has_side_effects=True) if m else {}
    sems = [pltpu.SemaphoreType.DMA((m,))] * 2 if m else []
    return pl.pallas_call(
        body,
        grid_spec=pltpu.PrefetchScalarGridSpec(
            num_scalar_prefetch=scalars,
            grid=grid,
            in_specs=[*in_specs, *[hbm] * (len(after) + m)],
            out_specs=[*out_specs, *[hbm] * m],
            scratch_shapes=[*scratch, *sems],
        ),
        out_shape=[*out_shape, *[jax.ShapeDtypeStruct((rows, a.shape[1]), a.dtype) for a, _, rows, _ in sends]],
        compiler_params=pltpu.CompilerParams(vmem_limit_bytes=VMEM_MIB * MIB, **more),
        cost_estimate=pl.CostEstimate(flops=int(flops), bytes_accessed=int(nbytes), transcendentals=int(trans)),
        name=name,
    )(*args, *after, *[a for a, *_ in sends])


def stage_bits(size):
    return [1 << b for b in range(size.bit_length() - 1)]


def stage_order(ndp, nseq, kind):
    dp_bits = [("dp", [b]) for b in stage_bits(ndp)]
    seq_bits = [("seq", [b]) for b in stage_bits(nseq)]
    cycle = [*dp_bits[1:], *seq_bits[:1]]
    kind = min(kind, len(cycle) - 1)
    at = (0, len(cycle) - 1, 1)[kind] if kind else 0
    return dp_bits[:1] + cycle[at:] + cycle[:at] + seq_bits[1:]


def short_order(ndp, nseq):
    dp_bits = stage_bits(ndp)
    return [("dp", dp_bits[:1]), ("dp", dp_bits[1:]), ("seq", stage_bits(nseq))]


def flat_bits(stages):
    return [(axis, bit) for axis, bits in stages for bit in bits]


def source(spot, stages, nseq):
    at = {"dp": lax.axis_index("dp"), "seq": lax.axis_index("seq")}
    bits = flat_bits(stages)
    for k, (axis, bit) in enumerate(bits):
        flag = spot // (1 << (len(bits) - 1 - k)) % 2
        if not (isinstance(flag, int) and flag == 0):
            at[axis] = at[axis] + flag * bit * (1 - 2 * (at[axis] // bit % 2))
    return at["dp"] * nseq + at["seq"]


def fan(bits):
    return [sum(b for k, b in enumerate(bits) if (part >> (len(bits) - 1 - k)) & 1) for part in range(1 << len(bits))]


def combine_kernel(counts, slots, *refs):
    outs = refs[sum(counts) :]
    at = 0
    for n, (k, col) in zip(counts, slots):
        total = refs[at][...].astype(F32)
        for r in refs[at + 1 : at + n]:
            total += r[...].astype(F32)
        outs[k][:, col : col + total.shape[1]] = total.astype(outs[k].dtype)
        at += n


def combine(items, after=(), joined=()):
    steps = 2 if all(rows % 32 == 0 for _, _, rows, _ in items) else 1
    ins, specs, counts, slots, shapes, nbytes = [], [], [], [], [], 0
    for k, (arrays, lo, rows, dtype) in enumerate(items):
        block, cols = rows // steps, arrays[0][0].shape[1]
        arrays = [(a, off) for a, off in arrays if off <= lo < off + a.shape[0]]
        for a, off in arrays:
            ins.append(a)
            specs.append(pl.BlockSpec((block, cols), lambda i, at=(lo - off) // block: (at + i, 0)))
        counts.append(len(arrays))
        if k in joined:
            slots.append((len(shapes) - 1, shapes[-1][1]))
            shapes[-1] = (rows, shapes[-1][1] + cols, dtype)
        else:
            slots.append((len(shapes), 0))
            shapes.append((rows, cols, dtype))
        nbytes += rows * cols * 2 * (len(arrays) + 2)
    return call(
        functools.partial(combine_kernel, counts, slots),
        *ins,
        grid=(steps,),
        in_specs=specs,
        out_specs=[pl.BlockSpec((rows // steps, cols), lambda i: (i, 0)) for rows, cols, _ in shapes],
        out_shape=[jax.ShapeDtypeStruct((rows, cols), dtype) for rows, cols, dtype in shapes],
        name="combine",
        flops=nbytes,
        nbytes=nbytes,
        after=after,
    )


def last_kernel(counts, nseq, *refs):
    n = sum(counts)
    small_ref, outs = refs[n], refs[n + 1 :]
    combine_kernel(counts, [(0, 0), (0, refs[0].shape[1]), (1, 0)], *refs[:n], *outs[:2])
    d = small_ref.shape[1]
    me = lax.axis_index("dp") * nseq + lax.axis_index("seq")
    lines = [(k, 1) for k in (0, 1, 2, 3, 4, 4)] + [(5, 3), (8, outs[-1].shape[1] * d // outs[2].shape[1] // d)]
    for (at, rows), out in zip(lines, outs[2:]):
        flat = jnp.concatenate([small_ref[at + r : at + r + 1, :] for r in range(rows)], axis=1)
        flat = jnp.broadcast_to(flat, (8, rows * d))
        mine = out.shape[1]
        out[...] = pltpu.roll(flat, rows * d - me * mine, 1)[:1, :mine]


def last_sums(terms, small, ff, ndev, nseq):
    arrays = [a for term, *_ in terms for a, _ in term]
    rows = terms[0][2]
    d = small.shape[1]
    widths = [term[0][0].shape[1] for term, *_ in terms]
    shapes = [(rows, widths[0] + widths[1]), (rows, widths[2])] + [(1, d // ndev)] * 6 + [(1, 3 * d // ndev), (1, ff // ndev)]
    return call(
        functools.partial(last_kernel, [len(term) for term, *_ in terms], nseq),
        *arrays,
        small,
        grid=(1,),
        in_specs=[whole((rows, a.shape[1])) for a in arrays] + [whole(small.shape)],
        out_specs=[whole(shape) for shape in shapes],
        out_shape=[jax.ShapeDtypeStruct(shape, F32) for shape in shapes],
        name="last",
        flops=rows * d * 20,
        nbytes=rows * d * 40,
    )


class Halving:
    def __init__(self, send, keep, stages, sizes):
        self.keep, self.stages, self.sizes = keep, list(stages), sizes
        self.rows, self.got, self.ready = keep.shape[0], [], [send]

    def targets(self):
        axis, bits = self.stages[0]
        return [(axis, offset) for offset in fan(bits)[1:]]

    def permute(self):
        for part, (axis, offset) in zip(self.ready, self.targets()):
            self.got.append((lax.ppermute(part, axis, [(i, i ^ offset) for i in range(self.sizes[axis])]), 0))
        self.stages.pop(0)

    def sends(self, lo=0, hi=1, parts=1):
        size = self.ready[0].shape[0] // parts
        return [(a, lo * size, (hi - lo) * size, to) for a, to in zip(self.ready, self.targets())]

    def receive(self, arrays, lo=0, hi=1, parts=1, last=True):
        size = self.ready[0].shape[0] // parts
        self.got += [(a, lo * size) for a in arrays]
        if last:
            self.stages.pop(0)

    def items(self):
        arrays = [(self.keep, 0), *self.got]
        parts = 1 << len(self.stages[0][1])
        self.rows //= parts
        return [(arrays, k * self.rows, self.rows, BF16) for k in range(1, parts)]

    def rest(self):
        arrays = [(self.keep, 0), *self.got]
        return arrays, 0, self.rows, BF16


def advance(sums, after):
    groups = [r.items() for r in sums]
    outs = combine([item for group in groups for item in group], after)
    at = 0
    for r, group in zip(sums, groups):
        r.ready = outs[at : at + len(group)]
        at += len(group)
    return [outs[0]]


def unit_of(x):
    mean = jnp.mean(x, axis=-1, keepdims=True)
    c = x - mean
    inv = lax.rsqrt(jnp.mean(c * c, axis=-1, keepdims=True) + EPS)
    return c * inv, inv


def norm_kernel(x_ref, dy_ref, live_ref, g1, b1, g2, b2, a_ref, m_ref, grad_ref, sum_ref):
    u, _ = unit_of(x_ref[...].astype(F32))
    a_ref[...] = (u * g1[...] + b1[...]).astype(BF16)
    m_ref[...] = (u * g2[...] + b2[...]).astype(BF16)
    grad = dy_ref[...].astype(F32) * live_ref[...]
    grad_ref[...] = grad.astype(BF16)

    @pl.when(pl.program_id(0) == 0)
    def _():
        sum_ref[...] = jnp.zeros_like(sum_ref)

    sum_ref[...] += jnp.sum(grad, axis=0, keepdims=True)


def norms(x, dy, live, g1, b1, g2, b2, after=()):
    rows, d = x.shape
    tr = min(256, rows)
    row = pl.BlockSpec((tr, d), lambda i: (i, 0))
    return call(
        norm_kernel,
        x, dy, live, g1, b1, g2, b2,
        grid=(rows // tr,),
        in_specs=[row, row, pl.BlockSpec((tr, 1), lambda i: (i, 0))] + [whole((1, d))] * 4,
        out_specs=[row, row, row, whole((1, d))],
        out_shape=[jax.ShapeDtypeStruct((rows, d), BF16)] * 3 + [jax.ShapeDtypeStruct((1, d), F32)],
        flops=rows * d * 20, nbytes=rows * d * 10,
        name="norms",
        after=after,
    )


def mlp_kernel(m_ref, grad_ref, win_ref, bin_ref, wout_ref, out_ref, act_ref, dpre_ref, dm_ref, bsum_ref):
    pre = dot(m_ref[...], win_ref[...]) + bin_ref[...]
    cdf = 0.5 * (1.0 + lax.erf(pre * math.sqrt(0.5)))
    act = (pre * cdf).astype(BF16)
    act_ref[...] = act
    d_act = dot_t(grad_ref[...], wout_ref[...])
    slope = cdf + pre * (jnp.exp(-0.5 * pre * pre) * (1.0 / math.sqrt(2.0 * math.pi)))
    d_pre = (d_act * slope).astype(BF16)
    dpre_ref[...] = d_pre
    bsum_ref[...] = jnp.sum(d_pre.astype(F32), axis=0, keepdims=True)

    @pl.when(pl.program_id(0) == 0)
    def _():
        out_ref[...] = jnp.zeros_like(out_ref)
        dm_ref[...] = jnp.zeros_like(dm_ref)

    out_ref[...] += dot(act, wout_ref[...])
    dm_ref[...] += dot_t(d_pre, win_ref[...])


def mlp(m, grad, win, b_in, wout, after=(), sends=(), cid=None):
    rows, d = m.shape
    ff = win.shape[1]
    tf = 1024
    cols = pl.BlockSpec((rows, tf), lambda i: (0, i))
    line = pl.BlockSpec((1, tf), lambda i: (0, i))
    return call(
        mlp_kernel,
        m, grad, win, b_in, wout,
        grid=(ff // tf,),
        in_specs=[
            whole((rows, d)),
            whole((rows, d)),
            pl.BlockSpec((d, tf), lambda i: (0, i)),
            line,
            pl.BlockSpec((tf, d), lambda i: (i, 0)),
        ],
        out_specs=[whole((rows, d)), cols, cols, whole((rows, d)), line],
        out_shape=[
            jax.ShapeDtypeStruct((rows, d), F32),
            jax.ShapeDtypeStruct((rows, ff), BF16),
            jax.ShapeDtypeStruct((rows, ff), BF16),
            jax.ShapeDtypeStruct((rows, d), F32),
            jax.ShapeDtypeStruct((1, ff), F32),
        ],
        flops=8 * rows * d * ff, nbytes=4 * d * ff + 4 * rows * ff + 12 * rows * d, trans=rows * ff * 2,
        name="mlp",
        after=after,
        sends=sends,
        cid=cid,
    )


def turned(left, nat_ref, at):
    n = min(BLOCK, left.shape[1])
    eye = lax.broadcasted_iota(jnp.int32, (n, n), 0) == lax.broadcasted_iota(jnp.int32, (n, n), 1)
    eye = jnp.where(eye, 1.0, 0.0).astype(BF16)
    for c in range(0, left.shape[1], n):
        nat_ref[at + c : at + c + n, :] = dot_t(eye, left[:, c : c + n])


def placed(order, nat_ref, lt_ref):
    blocks = 1 << len(flat_bits(order[0]))
    size = nat_ref.shape[0] // blocks
    for b in range(blocks):
        rows = pl.ds(pl.multiple_of(source(b, *order) * size, size), size)
        lt_ref[b * size : (b + 1) * size, :] = nat_ref[rows, :].astype(BF16)


def wgrad_kernel(stacked, orders, steps, starts, per, *refs):
    n = len(starts)
    n_right = -(-sum(steps) // per)
    n_left = len(refs) - n_right - 3 * n - 2
    lefts, rights, refs = refs[:n_left], refs[n_left : n_left + n_right], refs[n_left + n_right :]
    outs, (nat_ref, lt_ref) = refs[:-2], refs[-2:]
    i = pl.program_id(0)

    @pl.when(i == 0)
    def _():
        row = col = 0
        for left in lefts:
            toks, width = left.shape
            turned(left[...], nat_ref.at[:, col : col + toks], row)
            if stacked:
                col += toks
            else:
                row += width

    for g in range(n):
        send_ref, keep_ref, bsum_ref = outs[3 * g : 3 * g + 3]

        @pl.when(i == starts[g])
        def _():
            placed(orders[g], nat_ref, lt_ref)

        for k, right_ref in enumerate(rights):
            first, end = max(starts[g], k * per), min(starts[g] + steps[g], (k + 1) * per)

            @pl.when((i >= first) & (i < end))
            def _():
                half = keep_ref.shape[0]
                right = right_ref[...]
                send_ref[...] = dot(lt_ref[half:, :], right).astype(BF16)
                keep_ref[...] = dot(lt_ref[:half, :], right).astype(BF16)
                bsum_ref[...] = jnp.sum(right.astype(F32), axis=0, keepdims=True)


def wgrad(groups, lefts, right, tn=512, after=(), sends=(), cid=None):
    rights = right if isinstance(right, list) else [right]
    toks, width = rights[0].shape
    stacked = lefts[0].shape[0] < toks
    per = width // tn
    d = lefts[0].shape[1] if stacked else sum(left.shape[1] for left in lefts)
    steps = [cols // tn for _, cols in groups]
    starts = [sum(steps[:g]) for g in range(len(groups))]
    out_specs, out_shape = [], []
    for (_, cols), first, n in zip(groups, starts, steps):
        at = lambda i, *_, first=first, n=n: (0, jnp.clip(i - first, 0, n - 1))
        out_specs += [pl.BlockSpec((d // 2, tn), at)] * 2 + [pl.BlockSpec((1, tn), at)]
        out_shape += [jax.ShapeDtypeStruct((d // 2, cols), BF16)] * 2 + [jax.ShapeDtypeStruct((1, cols), F32)]
    cols = sum(r.shape[1] for r in rights)
    return call(
        functools.partial(wgrad_kernel, stacked, [o for o, _ in groups], steps, starts, per if len(rights) > 1 else sum(steps)),
        *lefts,
        *rights,
        grid=(sum(steps),),
        in_specs=[
            *[whole(left.shape) for left in lefts],
            *[pl.BlockSpec((toks, tn), lambda i, *_, k=k: (0, jnp.clip(i - k * per, 0, per - 1))) for k in range(len(rights))],
        ],
        out_specs=out_specs,
        scratch=[pltpu.VMEM((d, toks), F32), pltpu.VMEM((d, toks), BF16)],
        out_shape=out_shape,
        flops=2 * toks * d * cols,
        nbytes=2 * toks * (d + cols) + 2 * d * cols,
        name="wgrad",
        after=after,
        sends=sends,
        cid=cid,
    )


def wgrad_rows_kernel(turns_n, orders, groups, *refs):
    n = len(groups)
    (left_ref, right_ref), refs = refs[:2], refs[2:]
    outs, (nat_ref, lt_ref) = refs[: 2 * n], refs[2 * n :]
    i = pl.program_id(0)
    tile = left_ref.shape[1]

    @pl.when(i < turns_n)
    def _():
        turned(left_ref[...], nat_ref, 0)
        lt_ref[pl.ds(pl.multiple_of(i * tile, tile), tile), :] = nat_ref[...].astype(lt_ref.dtype)

    for g, (first, steps, lo, cols) in enumerate(groups):
        send_ref, keep_ref = outs[2 * g : 2 * g + 2]
        rows = send_ref.shape[0]

        @pl.when((i >= first) & (i < first + steps))
        def _():
            total = 1 << len(flat_bits(orders[g][0]))
            blocks = total // steps
            size = rows // blocks
            for b in range(blocks):
                spot = ((i - first) * blocks + b + total // 2) % total
                at = pl.ds(pl.multiple_of(source(spot, *orders[g]) * size, size), size)
                nat_ref[b * size : (b + 1) * size, :] = lt_ref[at, :].astype(F32)
            out = dot(nat_ref[:rows, :].astype(BF16), right_ref[:, lo : lo + cols]).astype(BF16)

            @pl.when(i < first + steps // 2)
            def _():
                send_ref[...] = out

            @pl.when(i >= first + steps // 2)
            def _():
                keep_ref[...] = out


def wgrad_rows(groups, left, right, tile=1024, after=(), sends=(), cid=None):
    toks, d = right.shape
    rows = left.shape[1]
    n = rows // tile
    half = n // 2
    orders = [o for o, _ in groups]
    kind = BF16 if (rows >> len(flat_bits(orders[0][0]))) % 16 == 0 else F32
    cuts, out_specs, out_shape, lo = [], [], [], 0
    for g, (_, cols) in enumerate(groups):
        first = n * (g + 1)
        cuts.append((first, n, lo, cols))
        lo += cols
        out_specs.append(pl.BlockSpec((tile, cols), lambda i, *_, first=first: (jnp.clip(i - first, 0, half - 1), 0)))
        out_specs.append(pl.BlockSpec((tile, cols), lambda i, *_, first=first: (jnp.clip(i - first - half, 0, half - 1), 0)))
        out_shape += [jax.ShapeDtypeStruct((rows // 2, cols), BF16)] * 2
    return call(
        functools.partial(wgrad_rows_kernel, n, orders, cuts),
        left,
        right,
        grid=(n * (1 + len(groups)),),
        in_specs=[
            pl.BlockSpec((toks, tile), lambda i, *_: (0, jnp.minimum(i, n - 1))),
            pl.BlockSpec((toks, d), lambda i, *_: (0, 0)),
        ],
        out_specs=out_specs,
        scratch=[pltpu.VMEM((tile, toks), F32), pltpu.VMEM((rows, toks), kind)],
        out_shape=out_shape,
        flops=2 * toks * rows * d,
        nbytes=2 * (rows * (d + toks) + toks * d),
        name="wgrad_rows",
        after=after,
        sends=sends,
        cid=cid,
    )


def d_ctx_kernel(a_ref, w_ref, out_ref):
    out_ref[...] = dot_t(a_ref[...], w_ref[...]).astype(BF16)


def d_context(grad, w, tn=256, after=(), sends=(), cid=None):
    rows, d = grad.shape
    return call(
        d_ctx_kernel,
        grad, w,
        grid=(d // tn,),
        in_specs=[whole((rows, d)), pl.BlockSpec((tn, d), lambda i: (i, 0))],
        out_specs=[pl.BlockSpec((rows, tn), lambda i: (0, i))],
        out_shape=[jax.ShapeDtypeStruct((rows, d), BF16)],
        flops=2 * rows * d * d, nbytes=2 * d * (2 * rows + d),
        name="d_ctx",
        after=after,
        sends=sends,
        cid=cid,
    )


def lane_ids(rows):
    return lax.broadcasted_iota(jnp.int32, (rows, LANES), 1)


def turns():
    frm = lax.broadcasted_iota(jnp.int32, (LANES, LANES), 0)
    to = lax.broadcasted_iota(jnp.int32, (LANES, LANES), 1)
    half = ROT // 2
    within = frm % HEAD
    partner = jnp.where(within < half, frm + half, frm - half)
    rotated = within < ROT
    turned = (frm + HEAD) % LANES
    one = lambda hit: jnp.where(hit, 1.0, 0.0).astype(BF16)
    return one(turned == to), one(rotated & (partner == to)), one(rotated & ((partner + HEAD) % LANES == to))


def split(x):
    high = x.astype(BF16)
    return jnp.concatenate([high, (x - high.astype(F32)).astype(BF16)], axis=1)


def qkv_kernel(n, *refs):
    a_refs, (w_ref, bias_ref, cos_ref, sin_ref, q_ref, k_ref, v_ref) = refs[:n], refs[n:]
    turn, swap, swap_turn = turns()
    k_moves = jnp.concatenate([turn, swap_turn], axis=1)
    k_moves = jnp.concatenate([k_moves, k_moves], axis=0)
    q_moves = jnp.concatenate([swap, swap], axis=0)
    r = 0
    for a_ref in a_refs:
        rows = slice(r, r + a_ref.shape[0])
        r += a_ref.shape[0]
        first = lane_ids(a_ref.shape[0]) < HEAD
        packed = dot(a_ref[...], w_ref[...]) + bias_ref[...]
        cos, sin = cos_ref[rows, :], sin_ref[rows, :]
        for g in range(w_ref.shape[1] // PAIR):
            c = g * PAIR
            lanes = slice(g * LANES, (g + 1) * LANES)
            pa, pb, pc = packed[:, c : c + LANES], packed[:, c + LANES : c + 2 * LANES], packed[:, c + 2 * LANES : c + PAIR]
            both = dot(split(jnp.where(first, pc, pa)), k_moves)
            k_ref[rows, lanes] = (both[:, :LANES] * cos + both[:, LANES:] * sin).astype(BF16)
            v_ref[rows, lanes] = jnp.where(first, pb, pc).astype(BF16)
            if a_ref is a_refs[-1]:
                q = jnp.where(first, pa, pb)
                q_ref[:, lanes] = (q * cos + dot(split(q), q_moves) * sin).astype(BF16)


def qkv(pieces, w, bias, cos, sin, group=4, after=()):
    toks, d = pieces[-1].shape
    win = sum(p.shape[0] for p in pieces)
    cols = w.shape[1]
    out = pl.BlockSpec((win, group * LANES), lambda i: (0, i))
    return call(
        functools.partial(qkv_kernel, len(pieces)),
        *pieces, w, bias, cos, sin,
        grid=(cols // PAIR // group,),
        in_specs=[
            *[whole(p.shape) for p in pieces],
            pl.BlockSpec((d, group * PAIR), lambda i: (0, i)),
            pl.BlockSpec((1, group * PAIR), lambda i: (0, i)),
            whole((win, LANES)),
            whole((win, LANES)),
        ],
        out_specs=[pl.BlockSpec((toks, group * LANES), lambda i: (0, i)), out, out],
        out_shape=[jax.ShapeDtypeStruct((toks, cols // 3), BF16)] + [jax.ShapeDtypeStruct((win, cols // 3), BF16)] * 2,
        flops=2 * win * d * cols, nbytes=8 * win * d + 2 * d * cols,
        name="qkv",
        after=after,
    )


GROUP = 2
QB = 256


def attention_kernel(
    toks, win, start_ref, q_ref, k_ref, v_ref, do_ref, cos_ref, sin_ref, ctx_ref, dp_ref,
    k2, v2, kt, vt, s_ref, e_ref, dq_acc, dk_acc, dv_acc,
):
    nk = win // BLOCK
    halo = win - toks
    first = lane_ids(BLOCK) < HEAD
    first_q = lane_ids(QB) < HEAD
    zero = jnp.zeros((BLOCK, LANES), BF16)
    zero_q = jnp.zeros((QB, LANES), BF16)
    top = lax.broadcasted_iota(jnp.int32, (LANES, QB), 0) < HEAD
    groups = range(GROUP)
    lanes = [slice(g * LANES, (g + 1) * LANES) for g in groups]
    eye = lax.broadcasted_iota(jnp.int32, (LANES, LANES), 0) == lax.broadcasted_iota(jnp.int32, (LANES, LANES), 1)
    upper = lax.broadcasted_iota(jnp.int32, (LANES, LANES), 0) < HEAD
    eye0 = jnp.where(eye & upper, 1.0, 0.0).astype(BF16)
    eye1 = jnp.where(eye & ~upper, 1.0, 0.0).astype(BF16)

    def prepare(j, _):
        rows = pl.ds(pl.multiple_of(j * BLOCK, BLOCK), BLOCK)
        for g in groups:
            for src, two, tr in ((k_ref, k2, kt), (v_ref, v2, vt)):
                x = src[rows, lanes[g]]
                two[g, j, :BLOCK, :] = jnp.where(first, x, zero)
                two[g, j, BLOCK:, :] = jnp.where(first, zero, x)
                tr[g, j, :, :BLOCK] = dot_t(eye0, x).astype(BF16)
                tr[g, j, :, BLOCK:] = dot_t(eye1, x).astype(BF16)
        return 0

    lax.fori_loop(0, nk, prepare, 0)
    dk_acc[...] = jnp.zeros_like(dk_acc)
    dv_acc[...] = jnp.zeros_like(dv_acc)
    scale = HEAD**-0.5
    for i in range(toks // QB):
        rows = slice(i * QB, (i + 1) * QB)
        last = (halo + (i + 1) * QB) // BLOCK
        low = max(halo + i * QB - DOC_MOST + 1, 0) // BLOCK
        qs = [q_ref[rows, lanes[g]].astype(F32) * scale for g in groups]
        qts = [q.T.astype(BF16) for q in qs]
        qs = [q.astype(BF16) for q in qs]
        q2 = [jnp.concatenate([jnp.where(first_q, q, zero_q), jnp.where(first_q, zero_q, q)], axis=0) for q in qs]
        start = start_ref[:, rows]
        q_at = halo + i * QB + lax.broadcasted_iota(jnp.int32, (1, QB), 1)

        def scores(j, peaks):
            at = j * BLOCK + lax.broadcasted_iota(jnp.int32, (BLOCK, QB), 0)
            ok = (at >= start) & (at <= q_at)
            out = []
            for g in groups:
                s = dot(k2[g, j], qts[g])
                s0 = jnp.where(ok, s[:BLOCK], NEG)
                s1 = jnp.where(ok, s[BLOCK:], NEG)
                s_ref[g, j, :BLOCK, :] = s0
                s_ref[g, j, BLOCK:, :] = s1
                out.append(jnp.maximum(peaks[2 * g], jnp.max(s0, axis=0, keepdims=True)))
                out.append(jnp.maximum(peaks[2 * g + 1], jnp.max(s1, axis=0, keepdims=True)))
            return tuple(out)

        floor = jnp.full((1, QB), NEG, F32)
        peaks = lax.fori_loop(low, last, scores, (floor,) * (2 * GROUP), unroll=True)

        def weigh(j, carry):
            out = []
            for g in groups:
                t0, t1, acc = carry[3 * g : 3 * g + 3]
                e0 = jnp.exp(s_ref[g, j, :BLOCK, :] - peaks[2 * g])
                e1 = jnp.exp(s_ref[g, j, BLOCK:, :] - peaks[2 * g + 1])
                b0, b1 = e0.astype(BF16), e1.astype(BF16)
                e_ref[g, j, :BLOCK, :] = b0
                e_ref[g, j, BLOCK:, :] = b1
                acc = acc + dot(vt[g, j], jnp.concatenate([b0, b1], axis=0))
                out += [t0 + jnp.sum(e0, axis=0, keepdims=True), t1 + jnp.sum(e1, axis=0, keepdims=True), acc]
            return tuple(out)

        none = jnp.zeros((1, QB), F32)
        sums = lax.fori_loop(low, last, weigh, (none, none, jnp.zeros((LANES, QB), F32)) * GROUP, unroll=True)
        do_l, do2, d0, d1 = [], [], [], []
        for g in groups:
            t0, t1, acc = sums[3 * g : 3 * g + 3]
            share = jnp.where(top, 1.0 / t0, 1.0 / t1)
            ctx_t = acc * share
            ctx_ref[rows, lanes[g]] = ctx_t.T.astype(BF16)
            do_t = do_ref[rows, lanes[g]].astype(F32).T * share
            both = do_t * ctx_t
            d0.append(jnp.sum(both[:HEAD], axis=0, keepdims=True))
            d1.append(jnp.sum(both[HEAD:], axis=0, keepdims=True))
            do = do_t.T.astype(BF16)
            do_l.append(do_t.astype(BF16))
            do2.append(jnp.concatenate([jnp.where(first_q, do, zero_q), jnp.where(first_q, zero_q, do)], axis=0))

        def back(j, dqs):
            at = pl.ds(pl.multiple_of(j * BLOCK, BLOCK), BLOCK)
            out = []
            for g in groups:
                dp = dot(v2[g, j], do_l[g])
                e0, e1 = e_ref[g, j, :BLOCK, :], e_ref[g, j, BLOCK:, :]
                ds0 = (e0.astype(F32) * (dp[:BLOCK] - d0[g])).astype(BF16)
                ds1 = (e1.astype(F32) * (dp[BLOCK:] - d1[g])).astype(BF16)
                dv_acc[at, lanes[g]] += dot(jnp.concatenate([e0, e1], axis=1), do2[g])
                dk_acc[at, lanes[g]] += dot(jnp.concatenate([ds0, ds1], axis=1), q2[g])
                out.append(dqs[g] + dot(kt[g, j], jnp.concatenate([ds0, ds1], axis=0)))
            return tuple(out)

        dqs = lax.fori_loop(low, last, back, (jnp.zeros((LANES, QB), F32),) * GROUP, unroll=True)
        for g in groups:
            dq_acc[rows, lanes[g]] = dqs[g].T * scale

    turn, swap, swap_turn = turns()
    for j in range(nk):
        rows = slice(j * BLOCK, (j + 1) * BLOCK)
        cos, sin = cos_ref[rows, :], sin_ref[rows, :]
        for g in groups:
            dk = dk_acc[rows, lanes[g]].astype(BF16)
            dk = dot(dk, turn) * cos - dot(dk, swap_turn) * sin
            dv = dv_acc[rows, lanes[g]]
            if j * BLOCK >= halo:
                own = slice(j * BLOCK - halo, (j + 1) * BLOCK - halo)
                dq = dq_acc[own, lanes[g]]
                dq = dq * cos - dot(dq.astype(BF16), swap) * sin
            else:
                dq = jnp.zeros_like(dk)
            c = g * PAIR
            dp_ref[rows, c : c + LANES] = jnp.where(first, dq, dk).astype(BF16)
            dp_ref[rows, c + LANES : c + 2 * LANES] = jnp.where(first, dv, dq).astype(BF16)
            dp_ref[rows, c + 2 * LANES : c + PAIR] = jnp.where(first, dk, dv).astype(BF16)


def attention(start, q, k, v, d_ctx, cos, sin, pair, pairs, after=(), sends=(), cid=None):
    win, d = k.shape
    toks = d_ctx.shape[0]
    nk = win // BLOCK
    width = GROUP * LANES
    at = pair // GROUP
    own = pl.BlockSpec((toks, width), lambda i: (0, at + i))
    every = pl.BlockSpec((win, width), lambda i: (0, at + i))
    out = pairs * LANES
    return call(
        functools.partial(attention_kernel, toks, win),
        start,
        q,
        k,
        v,
        d_ctx,
        cos,
        sin,
        grid=(pairs // GROUP,),
        in_specs=[whole((1, toks)), own, every, every, own, whole((win, LANES)), whole((win, LANES))],
        out_specs=[pl.BlockSpec((toks, width), lambda i: (0, i)), pl.BlockSpec((win, GROUP * PAIR), lambda i: (0, i))],
        out_shape=[jax.ShapeDtypeStruct((toks, out), BF16), jax.ShapeDtypeStruct((win, 3 * out), BF16)],
        scratch=[
            pltpu.VMEM((GROUP, nk, 2 * BLOCK, LANES), BF16),
            pltpu.VMEM((GROUP, nk, 2 * BLOCK, LANES), BF16),
            pltpu.VMEM((GROUP, nk, LANES, 2 * BLOCK), BF16),
            pltpu.VMEM((GROUP, nk, LANES, 2 * BLOCK), BF16),
            pltpu.VMEM((GROUP, nk, 2 * BLOCK, QB), F32),
            pltpu.VMEM((GROUP, nk, 2 * BLOCK, QB), BF16),
            pltpu.VMEM((toks, width), F32),
            pltpu.VMEM((win, width), F32),
            pltpu.VMEM((win, width), F32),
        ],
        flops=pairs * toks * DOC_MOST * 4 * 6 * LANES,
        nbytes=14 * win * out,
        trans=pairs * 2 * toks * DOC_MOST,
        name="attention",
        after=after,
        sends=sends,
        cid=cid,
    )


def tail_kernel(cfg, *refs):
    ndp, nseq, halos, n_pieces, n_dp, n_ctx, joins, last_c = cfg
    refs = list(refs)
    take = lambda n: [refs.pop(0) for _ in range(n)]
    dp_rows, (w_ref,) = take(n_dp), take(1)
    n_late = n_dp - 2 + n_pieces + n_ctx + 3
    late = take(n_late)
    mlp_ref, wd_ref, bias_ref, g1, g2 = take(5)
    gsum_ref, qsum_ref, isum_ref = take(3)
    left_q, own_q = take(2)
    hidden_ref, grad_in_ref, small = take(3)
    owns = take(3)
    last_gots = [take(len(fan(last_c)) - 1) for _ in owns]
    nat, lt, own_acc, far, far_got = take(5)
    group_bufs = [take(6), take(6), [None, own_q.at[0], None, left_q, *take(2)]]
    bsum_ref, small_got = take(2)
    held = take(n_late)
    send_sem, recv_sem, late_sem = refs
    loads = [pltpu.make_async_copy(a, b, late_sem.at[k]) for k, (a, b) in enumerate(zip(late, held))]
    held = list(held)
    take_held = lambda n: [held.pop(0) for _ in range(n)]
    dp_cols, pieces, ctxs = take_held(n_dp - 2), take_held(n_pieces), take_held(n_ctx)
    grad_ref, x_ref, d_mlp_ref = held
    first_loads = n_dp - 2 + n_pieces
    toks, d = x_ref.shape
    me_dp, me_seq = lax.axis_index("dp"), lax.axis_index("seq")
    dp_bits = stage_bits(ndp)
    core, cross = fan(dp_bits[:1]), fan(dp_bits[1:])
    across = fan(last_c)

    def device(axis, offset):
        return (me_dp ^ offset, me_seq) if axis == "dp" else (me_dp, me_seq ^ offset)

    behind = (me_dp, lax.rem(me_seq + nseq - 1, nseq))
    ahead = (me_dp, lax.rem(me_seq + 1, nseq))
    names = {}

    def copy(name, src, dst, to):
        k = names.setdefault(name, len(names))
        return pltpu.make_async_remote_copy(
            src_ref=src,
            dst_ref=dst,
            send_sem=send_sem.at[k],
            recv_sem=recv_sem.at[k],
            device_id=to,
            device_id_type=pl.DeviceIdType.MESH,
        )

    half = toks // 2

    def far_copy(k, c):
        rows = pl.ds(c * half, half)
        return copy(("far", k, c), far.at[k, rows], far_got.at[k, rows], behind)


    def first(n):
        send, _, got, *_ = group_bufs[n]
        return copy(("core", n), send, got, device("dp", core[1]))

    def second(n):
        _, _, _, out, into, _ = group_bufs[n]
        start = 1 if n < 2 else 0
        return [copy(("cross", n, k), out.at[k - start], into.at[k - 1], device("dp", cross[k])) for k in range(1, len(cross))]

    def third(n):
        out, got = group_bufs[n][5], last_gots[(n + 1) % 3]
        return [copy(("across", n, k), out.at[k - 1], got[k - 1], device("seq", across[k])) for k in range(1, len(across))]

    def to_second(n):
        _, keep, got, out, _, _ = group_bufs[n]
        first(n).wait()
        rows = out.shape[1]
        for k, c in enumerate(second(n), 1):
            at = slice(k * rows, (k + 1) * rows)
            out[k - 1] = (keep[at, :].astype(F32) + got[at, :].astype(F32)).astype(BF16)
            c.start()

    def to_third(n):
        _, keep, got, _, into, out = group_bufs[n]
        for c in second(n):
            c.wait()
        own = owns[(n + 1) % 3]
        rows = own.shape[0]
        copies = third(n)
        for k in reversed(range(len(across))):
            at = slice(k * rows, (k + 1) * rows)
            total = keep[at, :].astype(F32)
            if got is not None:
                total += got[at, :].astype(F32)
            for b in range(len(cross) - 1):
                total += into[b, at, :].astype(F32)
            if k:
                out[k - 1] = total.astype(out.dtype)
                copies[k - 1].start()
            else:
                own[...] = total

    def pass_on(k, c):
        far_copy(k - 1, c).wait()
        rows = pl.ds(c * half, half)
        far[k, rows] = (far[k, rows].astype(F32) + far_got[k - 1, rows].astype(F32)).astype(BF16)
        far_copy(k, c).start()

    def back(rows=slice(None)):
        total, at = None, 0
        for a_ref in dp_rows:
            n = a_ref.shape[1]
            term = dot_t(a_ref[rows, :], w_ref[:, at : at + n])
            total, at = term if total is None else total + term, at + n
        return total

    step = [0]
    pid = pl.program_id(0)

    def phase(fn):
        pl.when(pid == step[0])(fn)
        step[0] += 1

    for k in range(halos):

        def do_far(k=k):
            if k == 0:
                offsets = [("dp", o) for o in (*core[1:], *cross[1:])] + [("seq", o) for o in across[1:]]
                greet([device(*o) for o in offsets] + [behind, ahead])
                for c in loads + second(2):
                    c.start()
            for c in range(2):
                rows = slice(c * half, (c + 1) * half)
                far[k, rows] = back(rows).astype(BF16)
                if k == 0:
                    far_copy(0, c).start()

        phase(do_far)

    def do_columns():
        for c in loads[:first_loads]:
            c.wait()
        col = 0
        for left in pieces:
            n = left.shape[0]
            turned(left[...], nat.at[:, :n], 0)
            placed((short_order(ndp, nseq), nseq), nat.at[:, :n], lt.at[:, col : col + n])
            col += n
        send, keep = group_bufs[0][:2]
        half, at = keep.shape[0], 0
        for right_ref in dp_cols:
            right = right_ref[...]
            n = right.shape[1]
            send[:, at : at + n] = dot(lt[half:, :], right).astype(BF16)
            keep[:, at : at + n] = dot(lt[:half, :], right).astype(BF16)
            bsum_ref[:, at : at + n] = jnp.sum(right.astype(F32), axis=0, keepdims=True)
            at += n
        first(0).start()
        if halos > 1:
            pass_on(1, 0)

    phase(do_columns)

    def do_dense():
        for c in loads[first_loads:]:
            c.wait()
        at = 0
        for ctx in ctxs:
            turned(ctx[...], nat, at)
            at += ctx.shape[1]
        placed((short_order(ndp, nseq), nseq), nat, lt.at[:, :toks])
        send, keep = group_bufs[1][:2]
        half = keep.shape[0]
        send[...] = dot(lt[half:, :toks], grad_ref[...]).astype(BF16)
        first(1).start()
        keep[...] = dot(lt[:half, :toks], grad_ref[...]).astype(BF16)
        to_second(0)
        to_third(2)

    phase(do_dense)

    def do_own():
        own_acc[...] = back()
        if halos > 1:
            pass_on(1, 1)
        to_second(1)

    phase(do_own)
    for t in range(joins):

        def do_join(t=t):
            cols = hidden_ref.shape[1]
            at = slice(t * cols, (t + 1) * cols)
            total, row = x_ref[:, at].astype(F32) + mlp_ref[...] + bias_ref[:, at], 0
            for ctx in ctxs:
                n = ctx.shape[1]
                total += dot(ctx[...], wd_ref[row : row + n, :])
                row += n
            hidden_ref[...] = total.astype(BF16)

        phase(do_join)

    def do_rest():
        for k in range(2, halos):
            for c in range(2):
                pass_on(k, c)
        to_third(0)
        to_third(1)
        small[...] = jnp.zeros_like(small)
        rows = min(128, half)
        for r in range(0, toks, rows):
            if r % half == 0:
                far_copy(halos - 1, r // half).wait()
            at = slice(r, r + rows)
            u, inv = unit_of(x_ref[at, :].astype(F32))
            d1 = own_acc[at, :] + far_got[halos - 1, at, :].astype(F32)
            d2 = d_mlp_ref[at, :]
            e = d1 * g1[...] + d2 * g2[...]
            dx = inv * (e - jnp.mean(e, axis=-1, keepdims=True) - u * jnp.mean(e * u, axis=-1, keepdims=True))
            grad_in_ref[at, :] = grad_ref[at, :].astype(F32) + dx
            for k, v in enumerate((d1 * u, d1, d2 * u, d2)):
                small[k : k + 1, :] += jnp.sum(v, axis=0, keepdims=True)
        small[4:5, :] = gsum_ref[...]
        row = 5
        for parts in ((qsum_ref, bsum_ref), (isum_ref,)):
            flat = jnp.concatenate([p[...] for p in parts], axis=1)
            for c in range(0, flat.shape[1], d):
                small[row : row + 1, :] = flat[:, c : c + d]
                row += 1
        used = 0
        for axis, offsets in (("dp", core), ("dp", cross), ("seq", across)):
            copies = []
            for o in offsets[1:]:
                copies.append(copy(("small", used), small, small_got.at[used], device(axis, o)))
                copies[-1].start()
                used += 1
            for c in copies:
                c.wait()
            total = small[...]
            for k in range(used - len(copies), used):
                total += small_got[k]
            small[...] = total
        for c in third(0) + third(1) + third(2):
            c.wait()

    phase(do_rest)


def tail(dps, w, pieces, ctxs, grad, x, mlp_out, d_mlp, w_d, bias, g1, g2, sums, left_q, ndp, nseq, halos, after=()):
    toks, d = x.shape
    depth = w.shape[1]
    joins = 4
    own_at = halos + 2
    dp_bits, seq_bits = stage_bits(ndp), stage_bits(nseq)
    cross, across = 1 << len(dp_bits[1:]), 1 << len(seq_bits)
    tile = d // joins
    once = lambda shape: pl.BlockSpec(shape, lambda i: (0,) * len(shape), pipeline_mode=pl.Buffered(1))
    piece_at = lambda i: (jnp.where(i < halos, i, jnp.where(i < own_at, halos - 1, halos)), 0)
    join_at = lambda i: (0, jnp.clip(i - own_at - 1, 0, joins - 1))
    hbm = pl.BlockSpec(memory_space=pl.ANY)
    cut_up = lambda a, n: a.reshape(n, a.shape[0] // n, a.shape[1])
    left_q = cut_up(left_q, cross)
    late = [*dps[2:], *pieces, *ctxs, grad, x, d_mlp]
    ins = [*dps, w, *late, mlp_out, w_d, bias, g1, g2, *sums, left_q, left_q]
    in_specs = (
        [pl.BlockSpec((toks, a.shape[1]), piece_at) for a in dps]
        + [once(w.shape)]
        + [hbm] * len(late)
        + [pl.BlockSpec((toks, tile), join_at), pl.BlockSpec((d, tile), join_at)]
        + [once((1, d))] * 3
        + [once(v.shape) for v in sums]
        + [hbm, once((1, *left_q.shape[1:]))]
    )
    rest = sum(a.shape[1] for a in dps[2:])
    lines = 4 + sum(v.shape[1] for v in sums) // d + 1
    lines += -lines % 8
    widths = [left_q.shape[2], rest, d]
    left = d // 2 // cross // across
    kind = BF16 if left % 16 == 0 else F32
    out_shape = [
        jax.ShapeDtypeStruct((toks, d), BF16),
        jax.ShapeDtypeStruct((toks, d), F32),
        jax.ShapeDtypeStruct((lines, d), F32),
        *[jax.ShapeDtypeStruct((left, n), F32) for n in widths],
        *[jax.ShapeDtypeStruct((left, n), kind) for n in widths for _ in range(across - 1)],
    ]
    fixed = lambda shape: pl.BlockSpec(shape, lambda i: (0,) * len(shape))
    out_specs = (
        [pl.BlockSpec((toks, tile), join_at), fixed((toks, d))]
        + [fixed((lines, d))]
        + [fixed((left, n)) for n in widths]
        + [hbm] * (len(widths) * (across - 1))
    )
    scratch = [
        pltpu.VMEM((d, toks), F32),
        pltpu.VMEM((d, toks * (halos + 1)), BF16),
        pltpu.VMEM((toks, d), F32),
        pltpu.VMEM((halos, toks, d), BF16),
        pltpu.VMEM((halos, toks, d), BF16),
    ]
    for n in widths[1:]:
        scratch += [pltpu.VMEM((d // 2, n), BF16)] * 3
        scratch += [pltpu.VMEM((cross - 1, d // 2 // cross, n), BF16)] * 2
        scratch += [pltpu.VMEM((across - 1, left, n), kind)]
    scratch += [pltpu.VMEM((cross - 1, *left_q.shape[1:]), BF16), pltpu.VMEM((across - 1, left, widths[0]), kind)]
    scratch += [pltpu.VMEM((1, rest), F32), pltpu.VMEM((1 + cross - 1 + across - 1, lines, d), F32)]
    scratch += [pltpu.VMEM(a.shape, a.dtype) for a in late]
    copies = 2 * halos + 4 * (1 + cross - 1 + across - 1)
    scratch += [pltpu.SemaphoreType.DMA((copies,))] * 2 + [pltpu.SemaphoreType.DMA((len(late),))]
    cfg = (ndp, nseq, halos, len(pieces), len(dps), len(ctxs), joins, seq_bits)
    n = len(ins)

    def body(*refs):
        tail_kernel(cfg, *refs[:n], *refs[n + len(after) :])

    outs = pl.pallas_call(
        body,
        grid_spec=pltpu.PrefetchScalarGridSpec(
            num_scalar_prefetch=0,
            grid=(own_at + 1 + joins + 1,),
            in_specs=in_specs + [hbm] * len(after),
            out_specs=out_specs,
            scratch_shapes=scratch,
        ),
        out_shape=out_shape,
        compiler_params=pltpu.CompilerParams(vmem_limit_bytes=63 * MIB, collective_id=1, has_side_effects=True),
        cost_estimate=pl.CostEstimate(flops=20 * toks * d * depth, bytes_accessed=40 * toks * d, transcendentals=0),
        name="tail",
    )(*ins, *after)
    outs = list(outs)
    main, own, outs = outs[:3], outs[3:6], outs[6:]
    terms = []
    for a in own:
        terms.append(([(v, 0) for v in (a, *outs[: across - 1])], 0, left, F32))
        outs = outs[across - 1 :]
    return main, terms


def shards(
    hidden_in,
    doc_lengths,
    ln1_gain,
    ln1_bias,
    ln2_gain,
    ln2_bias,
    qkv_weight,
    qkv_bias,
    dense_weight,
    dense_bias,
    fc_in_weight,
    fc_in_bias,
    fc_out_weight,
    fc_out_bias,
    out_grad,
):
    _, toks, d = hidden_in.shape
    ff = fc_in_weight.shape[1]
    ndp, nseq = lax.axis_size("dp"), lax.axis_size("seq")
    ndev = ndp * nseq
    sizes = {"dp": ndp, "seq": nseq}
    me_dp, me_seq = lax.axis_index("dp"), lax.axis_index("seq")
    row = lambda v: v.reshape(1, -1)

    halos = min(-(-(DOC_MOST - 1) // toks), nseq - 1)
    halos = max(halos, 1)
    win = (halos + 1) * toks
    base = (me_seq - halos) * toks
    lengths = doc_lengths.reshape(-1)
    docs = lengths.shape[0]
    doc = jnp.arange(docs, dtype=jnp.int32)
    ends = jnp.sum(jnp.where(doc[None, :] <= doc[:, None], lengths[None, :], 0), axis=1)
    at = base + jnp.arange(win, dtype=jnp.int32)
    begin = jnp.max(jnp.where(at[:, None] >= ends[None, :], ends[None, :], 0), axis=1)
    doc_pos = at - begin
    live = (at[halos * toks :] < ends[docs - 2]).astype(F32).reshape(toks, 1)
    start = (begin - base)[halos * toks :]
    lane = jnp.arange(LANES, dtype=jnp.int32) % HEAD
    half = ROT // 2
    freq = 10000.0 ** (-(2.0 * (lane % half).astype(F32)) / ROT)
    angle = doc_pos.astype(F32)[:, None] * freq[None, :]
    cos = jnp.where(lane < ROT, jnp.cos(angle), 1.0)
    sin = jnp.where(lane < half, -1.0, jnp.where(lane < ROT, 1.0, 0.0)) * jnp.sin(angle)

    x = hidden_in.reshape(toks, d)
    a_own, m_own, grad, grad_sum = norms(
        x, out_grad.reshape(toks, d), live, row(ln1_gain), row(ln1_bias), row(ln2_gain), row(ln2_bias)
    )

    ahead = [(i, (i + 1) % nseq) for i in range(nseq)]
    on = ("ring", 1, nseq)
    fine = toks // 4 % LANES == 0
    cut = toks * 3 // 4 if fine else toks
    mlp_out, act, d_pre, d_mlp, b_in_sum, near = mlp(
        m_own, grad, fc_in_weight, row(fc_in_bias), fc_out_weight, sends=[(a_own, 0, cut, on)], cid=2
    )
    near, far = [near], []
    two = halos > 1

    orders = [stage_order(ndp, nseq, kind) for kind in range(3)]
    srcs = [(o, nseq) for o in orders]
    in_cut, out_cut = ff * 5 // 8, d // 4
    sends = [(a_own, cut, toks - cut, on)] if fine else []
    if two:
        sends.append((near[0], 0, toks // 4 if fine else toks // 2, on))
    s0, k0, line, s1, k1, _, *got = wgrad(
        [(srcs[0], in_cut), (srcs[2], ff - in_cut)], [m_own], d_pre, sends=sends, cid=3 if sends else None
    )
    near += got[:1] if fine else []
    far += got[-1:] if two else []
    early = [Halving(s0, k0, orders[0], sizes), Halving(s1, k1, orders[2], sizes)]
    s2, k2, s3, k3, *got = wgrad_rows(
        [(srcs[2], out_cut), (srcs[1], d - out_cut)],
        act,
        grad,
        after=[line],
        sends=[send for r in early for send in r.sends()]
        + ([(near[0], far[0].shape[0], toks // 2, on)] if two else []),
        cid=4,
    )
    for r in early:
        r.receive([got.pop(0)])
    far += got
    late = [Halving(s2, k2, orders[2], sizes), Halving(s3, k3, orders[1], sizes)]
    fc = early + late
    d_ctx, *got = d_context(
        grad,
        dense_weight,
        sends=[send for r in late for send in r.sends()] + ([(near[1], 0, toks - cut, on)] if two and fine else []),
        cid=5,
    )
    for r in late:
        r.receive([got.pop(0)])
    far += got
    pieces = [*far, *near, a_own]
    for k in range(2, halos):
        far = [lax.ppermute(jnp.concatenate(far, axis=0), "seq", ahead)]
        pieces = far + pieces
    last = advance(fc, [d_ctx])
    for r in fc:
        r.permute()
    q, k, v = qkv(pieces, qkv_weight, row(qkv_bias), cos, sin, after=last)

    order_c = short_order(ndp, nseq)
    src_c = (order_c, nseq)
    pairs = d // LANES
    quarter = pairs // 4

    def part(at, n, sums=(), **more):
        sends = [send for r in sums for send in r.sends()]
        ctx, dp, *got = attention(
            row(start), q, k, v, d_ctx, cos, sin, at * quarter, n * quarter, sends=sends, cid=6 + at if sends else None, **more
        )
        for r in sums:
            r.receive([got.pop(0) for _ in r.targets()])
        return ctx, dp

    ctx_a, dp_a = part(0, 1)
    advance(fc, [ctx_a])
    ctx_b, dp_b = part(1, 1, fc)
    advance(fc, [ctx_b])
    qa_send, qa_keep, b_qkv_a, *got = wgrad(
        [(src_c, dp_a.shape[1] * 2)], pieces, [dp_a, dp_b], tn=dp_a.shape[1], sends=[send for r in fc for send in r.sends()], cid=10
    )
    for r in fc:
        r.receive([got.pop(0) for _ in r.targets()])
    r_qa = Halving(qa_send, qa_keep, order_c, sizes)
    last = advance(fc, [b_qkv_a])
    while len(fc[0].stages) > 1:
        for r in fc:
            r.permute()
        last = advance(fc, last)
    ctx_c, dp_c = part(2, 2, [*fc, r_qa])
    left_q, g_in, g_out = combine([r_qa.rest(), *[(*r.rest()[:3], F32) for r in fc]], [ctx_c], joined=(2, 4))
    main, terms = tail(
        [dp_a, dp_b, dp_c],
        qkv_weight,
        pieces,
        [ctx_a, ctx_b, ctx_c],
        grad,
        x,
        mlp_out,
        d_mlp,
        dense_weight,
        row(dense_bias + fc_out_bias),
        row(ln1_gain),
        row(ln2_gain),
        [grad_sum, b_qkv_a, b_in_sum],
        left_q,
        ndp,
        nseq,
        halos,
    )
    hidden_out, grad_in, small = main
    g_qkv, g_dense, *parts = last_sums(terms, small, ff, ndev, nseq)
    o1g, o1b, o2g, o2b, o_db, o_ob, o_qb, o_ib = (v.reshape(-1) for v in parts)
    return (
        hidden_out.reshape(hidden_in.shape),
        grad_in.reshape(hidden_in.shape),
        o1g,
        o1b,
        o2g,
        o2b,
        g_qkv,
        o_qb,
        g_dense,
        o_db,
        g_in,
        o_ib,
        g_out,
        o_ob,
    )


def solution(mesh):
    both = P(("dp", "seq"))
    rows = P(("dp", "seq"), None)
    toks = P("dp", "seq", None)
    return jax.shard_map(
        shards,
        mesh=mesh,
        in_specs=(toks, P("dp", None)) + (P(),) * 12 + (toks,),
        out_specs=(toks, toks, both, both, both, both, rows, both, rows, both, rows, both, rows, both),
        check_vma=False,
    )
```

```python
import functools
import math

import jax
import jax.numpy as jnp
from jax import lax
from jax.experimental import pallas as pl
from jax.experimental.pallas import tpu as pltpu
from jax.sharding import PartitionSpec as P

HEADS = 16
HEAD = 64
ROT = 16
DOC_MOST = 1024
EPS = 1e-05
NEG = -1e30
LANES = 128
PAIR = 3 * LANES
BLOCK = 256
F32 = jnp.float32
BF16 = jnp.bfloat16
MIB = 1 << 20
VMEM_MIB = 56


def dot(a, b):
    return lax.dot_general(a, b, (((1,), (0,)), ((), ())), preferred_element_type=F32)


def dot_t(a, b):
    return lax.dot_general(a, b, (((1,), (1,)), ((), ())), preferred_element_type=F32)


def whole(shape):
    return pl.BlockSpec(shape, lambda *_: (0,) * len(shape))


def place(to):
    at = {"dp": lax.axis_index("dp"), "seq": lax.axis_index("seq")}
    if to[0] == "ring":
        at["seq"] = lax.rem(at["seq"] + to[1] + to[2], to[2])
    else:
        at[to[0]] = at[to[0]] ^ to[1]
    return (at["dp"], at["seq"])


def both_ways(targets):
    back = [("ring", -to[1], to[2]) for to in targets if to[0] == "ring"]
    return [place(to) for to in sorted({*targets, *back})]


def greet(devices):
    barrier = pltpu.get_barrier_semaphore()
    for device in devices:
        pl.semaphore_signal(barrier, inc=1, device_id=device, device_id_type=pl.DeviceIdType.MESH)
    pl.semaphore_wait(barrier, len(devices))


def call(kernel, *args, grid, in_specs, out_specs, out_shape, name, flops, nbytes, trans=0, scalars=0, scratch=(), after=(), sends=(), cid=None):
    n, n_out, m = scalars + len(in_specs), len(out_specs), len(sends)

    def body(*refs):
        refs = list(refs)
        ins, _, srcs = refs[:n], refs[n : n + len(after)], refs[n + len(after) :][:m]
        rest = refs[n + len(after) + m :]
        outs, gots, own = rest[:n_out], rest[n_out : n_out + m], rest[n_out + m :]
        if not m:
            kernel(*ins, *outs, *own)
            return
        *own, send_sem, recv_sem = own

        def copy(k):
            _, lo, rows, to = sends[k]
            return pltpu.make_async_remote_copy(
                src_ref=srcs[k].at[pl.ds(lo, rows)],
                dst_ref=gots[k],
                send_sem=send_sem.at[k],
                recv_sem=recv_sem.at[k],
                device_id=place(to),
                device_id_type=pl.DeviceIdType.MESH,
            )

        @pl.when(pl.program_id(0) == 0)
        def _():
            greet(both_ways([to for *_, to in sends]))
            for k in range(m):
                copy(k).start()

        kernel(*ins, *outs, *own)

        @pl.when(pl.program_id(0) == grid[0] - 1)
        def _():
            for k in range(m):
                copy(k).wait()

    hbm = pl.BlockSpec(memory_space=pl.ANY)
    more = dict(collective_id=cid, has_side_effects=True) if m else {}
    sems = [pltpu.SemaphoreType.DMA((m,))] * 2 if m else []
    return pl.pallas_call(
        body,
        grid_spec=pltpu.PrefetchScalarGridSpec(
            num_scalar_prefetch=scalars,
            grid=grid,
            in_specs=[*in_specs, *[hbm] * (len(after) + m)],
            out_specs=[*out_specs, *[hbm] * m],
            scratch_shapes=[*scratch, *sems],
        ),
        out_shape=[*out_shape, *[jax.ShapeDtypeStruct((rows, a.shape[1]), a.dtype) for a, _, rows, _ in sends]],
        compiler_params=pltpu.CompilerParams(vmem_limit_bytes=VMEM_MIB * MIB, **more),
        cost_estimate=pl.CostEstimate(flops=int(flops), bytes_accessed=int(nbytes), transcendentals=int(trans)),
        name=name,
    )(*args, *after, *[a for a, *_ in sends])


def stage_bits(size):
    return [1 << b for b in range(size.bit_length() - 1)]


def stage_order(ndp, nseq, kind):
    dp_bits = [("dp", [b]) for b in stage_bits(ndp)]
    seq_bits = [("seq", [b]) for b in stage_bits(nseq)]
    cycle = [*dp_bits[1:], *seq_bits[:1]]
    kind = min(kind, len(cycle) - 1)
    at = (0, len(cycle) - 1, 1)[kind] if kind else 0
    return dp_bits[:1] + cycle[at:] + cycle[:at] + seq_bits[1:]


def short_order(ndp, nseq):
    dp_bits = stage_bits(ndp)
    return [("dp", dp_bits[:1]), ("dp", dp_bits[1:]), ("seq", stage_bits(nseq))]


def flat_bits(stages):
    return [(axis, bit) for axis, bits in stages for bit in bits]


def source(spot, stages, nseq):
    at = {"dp": lax.axis_index("dp"), "seq": lax.axis_index("seq")}
    bits = flat_bits(stages)
    for k, (axis, bit) in enumerate(bits):
        flag = spot // (1 << (len(bits) - 1 - k)) % 2
        if not (isinstance(flag, int) and flag == 0):
            at[axis] = at[axis] + flag * bit * (1 - 2 * (at[axis] // bit % 2))
    return at["dp"] * nseq + at["seq"]


def fan(bits):
    return [sum(b for k, b in enumerate(bits) if (part >> (len(bits) - 1 - k)) & 1) for part in range(1 << len(bits))]


def combine_kernel(counts, slots, *refs):
    outs = refs[sum(counts) :]
    at = 0
    for n, (k, col) in zip(counts, slots):
        total = refs[at][...].astype(F32)
        for r in refs[at + 1 : at + n]:
            total += r[...].astype(F32)
        outs[k][:, col : col + total.shape[1]] = total.astype(outs[k].dtype)
        at += n


def combine(items, after=(), joined=()):
    steps = 2 if all(rows % 32 == 0 for _, _, rows, _ in items) else 1
    ins, specs, counts, slots, shapes, nbytes = [], [], [], [], [], 0
    for k, (arrays, lo, rows, dtype) in enumerate(items):
        block, cols = rows // steps, arrays[0][0].shape[1]
        arrays = [(a, off) for a, off in arrays if off <= lo < off + a.shape[0]]
        for a, off in arrays:
            ins.append(a)
            specs.append(pl.BlockSpec((block, cols), lambda i, at=(lo - off) // block: (at + i, 0)))
        counts.append(len(arrays))
        if k in joined:
            slots.append((len(shapes) - 1, shapes[-1][1]))
            shapes[-1] = (rows, shapes[-1][1] + cols, dtype)
        else:
            slots.append((len(shapes), 0))
            shapes.append((rows, cols, dtype))
        nbytes += rows * cols * 2 * (len(arrays) + 2)
    return call(
        functools.partial(combine_kernel, counts, slots),
        *ins,
        grid=(steps,),
        in_specs=specs,
        out_specs=[pl.BlockSpec((rows // steps, cols), lambda i: (i, 0)) for rows, cols, _ in shapes],
        out_shape=[jax.ShapeDtypeStruct((rows, cols), dtype) for rows, cols, dtype in shapes],
        name="combine",
        flops=nbytes,
        nbytes=nbytes,
        after=after,
    )


def last_kernel(counts, nseq, *refs):
    n = sum(counts)
    small_ref, outs = refs[n], refs[n + 1 :]
    combine_kernel(counts, [(0, 0), (0, refs[0].shape[1]), (1, 0)], *refs[:n], *outs[:2])
    d = small_ref.shape[1]
    me = lax.axis_index("dp") * nseq + lax.axis_index("seq")
    lines = [(k, 1) for k in (0, 1, 2, 3, 4, 4)] + [(5, 3), (8, outs[-1].shape[1] * d // outs[2].shape[1] // d)]
    for (at, rows), out in zip(lines, outs[2:]):
        flat = jnp.concatenate([small_ref[at + r : at + r + 1, :] for r in range(rows)], axis=1)
        flat = jnp.broadcast_to(flat, (8, rows * d))
        mine = out.shape[1]
        out[...] = pltpu.roll(flat, rows * d - me * mine, 1)[:1, :mine]


def last_sums(terms, small, ff, ndev, nseq):
    arrays = [a for term, *_ in terms for a, _ in term]
    rows = terms[0][2]
    d = small.shape[1]
    widths = [term[0][0].shape[1] for term, *_ in terms]
    shapes = [(rows, widths[0] + widths[1]), (rows, widths[2])] + [(1, d // ndev)] * 6 + [(1, 3 * d // ndev), (1, ff // ndev)]
    return call(
        functools.partial(last_kernel, [len(term) for term, *_ in terms], nseq),
        *arrays,
        small,
        grid=(1,),
        in_specs=[whole((rows, a.shape[1])) for a in arrays] + [whole(small.shape)],
        out_specs=[whole(shape) for shape in shapes],
        out_shape=[jax.ShapeDtypeStruct(shape, F32) for shape in shapes],
        name="last",
        flops=rows * d * 20,
        nbytes=rows * d * 40,
    )


class Halving:
    def __init__(self, send, keep, stages, sizes):
        self.keep, self.stages, self.sizes = keep, list(stages), sizes
        self.rows, self.got, self.ready = keep.shape[0], [], [send]

    def targets(self):
        axis, bits = self.stages[0]
        return [(axis, offset) for offset in fan(bits)[1:]]

    def permute(self):
        for part, (axis, offset) in zip(self.ready, self.targets()):
            self.got.append((lax.ppermute(part, axis, [(i, i ^ offset) for i in range(self.sizes[axis])]), 0))
        self.stages.pop(0)

    def sends(self, lo=0, hi=1, parts=1):
        size = self.ready[0].shape[0] // parts
        return [(a, lo * size, (hi - lo) * size, to) for a, to in zip(self.ready, self.targets())]

    def receive(self, arrays, lo=0, hi=1, parts=1, last=True):
        size = self.ready[0].shape[0] // parts
        self.got += [(a, lo * size) for a in arrays]
        if last:
            self.stages.pop(0)

    def items(self):
        arrays = [(self.keep, 0), *self.got]
        parts = 1 << len(self.stages[0][1])
        self.rows //= parts
        return [(arrays, k * self.rows, self.rows, BF16) for k in range(1, parts)]

    def rest(self):
        arrays = [(self.keep, 0), *self.got]
        return arrays, 0, self.rows, BF16


def advance(sums, after):
    groups = [r.items() for r in sums]
    outs = combine([item for group in groups for item in group], after)
    at = 0
    for r, group in zip(sums, groups):
        r.ready = outs[at : at + len(group)]
        at += len(group)
    return [outs[0]]


def unit_of(x):
    mean = jnp.mean(x, axis=-1, keepdims=True)
    c = x - mean
    inv = lax.rsqrt(jnp.mean(c * c, axis=-1, keepdims=True) + EPS)
    return c * inv, inv


def norm_kernel(len_ref, x_ref, dy_ref, g1, b1, g2, b2, a_ref, m_ref, grad_ref, sum_ref):
    u, _ = unit_of(x_ref[...].astype(F32))
    a_ref[...] = (u * g1[...] + b1[...]).astype(BF16)
    m_ref[...] = (u * g2[...] + b2[...]).astype(BF16)
    rows = x_ref.shape[0]
    toks = rows * pl.num_programs(0)
    at = lax.axis_index("seq") * toks + pl.program_id(0) * rows + lax.broadcasted_iota(jnp.int32, (rows, 1), 0)
    text = sum(len_ref[k] for k in range(len_ref.shape[0] - 1))
    grad = dy_ref[...].astype(F32) * jnp.where(at < text, 1.0, 0.0)
    grad_ref[...] = grad.astype(BF16)

    @pl.when(pl.program_id(0) == 0)
    def _():
        sum_ref[...] = jnp.zeros_like(sum_ref)

    sum_ref[...] += jnp.sum(grad, axis=0, keepdims=True)


def norms(lengths, x, dy, g1, b1, g2, b2, after=()):
    rows, d = x.shape
    tr = min(256, rows)
    row = pl.BlockSpec((tr, d), lambda i, *_: (i, 0))
    return call(
        norm_kernel,
        lengths,
        x,
        dy,
        g1,
        b1,
        g2,
        b2,
        scalars=1,
        grid=(rows // tr,),
        in_specs=[row, row] + [whole((1, d))] * 4,
        out_specs=[row, row, row, whole((1, d))],
        out_shape=[jax.ShapeDtypeStruct((rows, d), BF16)] * 3 + [jax.ShapeDtypeStruct((1, d), F32)],
        flops=rows * d * 20, nbytes=rows * d * 10,
        name="norms",
        after=after,
    )


def mlp_kernel(m_ref, grad_ref, win_ref, bin_ref, wout_ref, out_ref, act_ref, dpre_ref, dm_ref, bsum_ref):
    pre = dot(m_ref[...], win_ref[...]) + bin_ref[...]
    cdf = 0.5 * (1.0 + lax.erf(pre * math.sqrt(0.5)))
    act = (pre * cdf).astype(BF16)
    act_ref[...] = act
    d_act = dot_t(grad_ref[...], wout_ref[...])
    slope = cdf + pre * (jnp.exp(-0.5 * pre * pre) * (1.0 / math.sqrt(2.0 * math.pi)))
    d_pre = (d_act * slope).astype(BF16)
    dpre_ref[...] = d_pre
    bsum_ref[...] = jnp.sum(d_pre.astype(F32), axis=0, keepdims=True)

    @pl.when(pl.program_id(0) == 0)
    def _():
        out_ref[...] = jnp.zeros_like(out_ref)
        dm_ref[...] = jnp.zeros_like(dm_ref)

    out_ref[...] += dot(act, wout_ref[...])
    dm_ref[...] += dot_t(d_pre, win_ref[...])


def mlp(m, grad, win, b_in, wout, after=(), sends=(), cid=None):
    rows, d = m.shape
    ff = win.shape[1]
    tf = 1024
    cols = pl.BlockSpec((rows, tf), lambda i: (0, i))
    line = pl.BlockSpec((1, tf), lambda i: (0, i))
    return call(
        mlp_kernel,
        m, grad, win, b_in, wout,
        grid=(ff // tf,),
        in_specs=[
            whole((rows, d)),
            whole((rows, d)),
            pl.BlockSpec((d, tf), lambda i: (0, i)),
            line,
            pl.BlockSpec((tf, d), lambda i: (i, 0)),
        ],
        out_specs=[whole((rows, d)), cols, cols, whole((rows, d)), line],
        out_shape=[
            jax.ShapeDtypeStruct((rows, d), F32),
            jax.ShapeDtypeStruct((rows, ff), BF16),
            jax.ShapeDtypeStruct((rows, ff), BF16),
            jax.ShapeDtypeStruct((rows, d), F32),
            jax.ShapeDtypeStruct((1, ff), F32),
        ],
        flops=8 * rows * d * ff, nbytes=4 * d * ff + 4 * rows * ff + 12 * rows * d, trans=rows * ff * 2,
        name="mlp",
        after=after,
        sends=sends,
        cid=cid,
    )


def turned(left, nat_ref, at):
    n = min(BLOCK, left.shape[1])
    eye = lax.broadcasted_iota(jnp.int32, (n, n), 0) == lax.broadcasted_iota(jnp.int32, (n, n), 1)
    eye = jnp.where(eye, 1.0, 0.0).astype(BF16)
    for c in range(0, left.shape[1], n):
        nat_ref[at + c : at + c + n, :] = dot_t(eye, left[:, c : c + n])


def placed(order, nat_ref, lt_ref):
    blocks = 1 << len(flat_bits(order[0]))
    size = nat_ref.shape[0] // blocks
    for b in range(blocks):
        rows = pl.ds(pl.multiple_of(source(b, *order) * size, size), size)
        lt_ref[b * size : (b + 1) * size, :] = nat_ref[rows, :].astype(BF16)


def wgrad_kernel(stacked, orders, steps, starts, per, *refs):
    n = len(starts)
    n_right = -(-sum(steps) // per)
    n_left = len(refs) - n_right - 3 * n - 2
    lefts, rights, refs = refs[:n_left], refs[n_left : n_left + n_right], refs[n_left + n_right :]
    outs, (nat_ref, lt_ref) = refs[:-2], refs[-2:]
    i = pl.program_id(0)

    @pl.when(i == 0)
    def _():
        row = col = 0
        for left in lefts:
            toks, width = left.shape
            turned(left[...], nat_ref.at[:, col : col + toks], row)
            if stacked:
                col += toks
            else:
                row += width

    for g in range(n):
        send_ref, keep_ref, bsum_ref = outs[3 * g : 3 * g + 3]

        @pl.when(i == starts[g])
        def _():
            placed(orders[g], nat_ref, lt_ref)

        for k, right_ref in enumerate(rights):
            first, end = max(starts[g], k * per), min(starts[g] + steps[g], (k + 1) * per)

            @pl.when((i >= first) & (i < end))
            def _():
                half = keep_ref.shape[0]
                right = right_ref[...]
                send_ref[...] = dot(lt_ref[half:, :], right).astype(BF16)
                keep_ref[...] = dot(lt_ref[:half, :], right).astype(BF16)
                bsum_ref[...] = jnp.sum(right.astype(F32), axis=0, keepdims=True)


def wgrad(groups, lefts, right, tn=512, after=(), sends=(), cid=None):
    rights = right if isinstance(right, list) else [right]
    toks, width = rights[0].shape
    stacked = lefts[0].shape[0] < toks
    per = width // tn
    d = lefts[0].shape[1] if stacked else sum(left.shape[1] for left in lefts)
    steps = [cols // tn for _, cols in groups]
    starts = [sum(steps[:g]) for g in range(len(groups))]
    out_specs, out_shape = [], []
    for (_, cols), first, n in zip(groups, starts, steps):
        at = lambda i, *_, first=first, n=n: (0, jnp.clip(i - first, 0, n - 1))
        out_specs += [pl.BlockSpec((d // 2, tn), at)] * 2 + [pl.BlockSpec((1, tn), at)]
        out_shape += [jax.ShapeDtypeStruct((d // 2, cols), BF16)] * 2 + [jax.ShapeDtypeStruct((1, cols), F32)]
    cols = sum(r.shape[1] for r in rights)
    return call(
        functools.partial(wgrad_kernel, stacked, [o for o, _ in groups], steps, starts, per if len(rights) > 1 else sum(steps)),
        *lefts,
        *rights,
        grid=(sum(steps),),
        in_specs=[
            *[whole(left.shape) for left in lefts],
            *[pl.BlockSpec((toks, tn), lambda i, *_, k=k: (0, jnp.clip(i - k * per, 0, per - 1))) for k in range(len(rights))],
        ],
        out_specs=out_specs,
        scratch=[pltpu.VMEM((d, toks), F32), pltpu.VMEM((d, toks), BF16)],
        out_shape=out_shape,
        flops=2 * toks * d * cols,
        nbytes=2 * toks * (d + cols) + 2 * d * cols,
        name="wgrad",
        after=after,
        sends=sends,
        cid=cid,
    )


def wgrad_rows_kernel(turns_n, orders, groups, *refs):
    n = len(groups)
    (left_ref, right_ref), refs = refs[:2], refs[2:]
    outs, (nat_ref, lt_ref) = refs[: 2 * n], refs[2 * n :]
    i = pl.program_id(0)
    tile = left_ref.shape[1]

    @pl.when(i < turns_n)
    def _():
        turned(left_ref[...], nat_ref, 0)
        lt_ref[pl.ds(pl.multiple_of(i * tile, tile), tile), :] = nat_ref[...].astype(lt_ref.dtype)

    for g, (first, steps, lo, cols) in enumerate(groups):
        send_ref, keep_ref = outs[2 * g : 2 * g + 2]
        rows = send_ref.shape[0]

        @pl.when((i >= first) & (i < first + steps))
        def _():
            total = 1 << len(flat_bits(orders[g][0]))
            blocks = total // steps
            size = rows // blocks
            for b in range(blocks):
                spot = ((i - first) * blocks + b + total // 2) % total
                at = pl.ds(pl.multiple_of(source(spot, *orders[g]) * size, size), size)
                nat_ref[b * size : (b + 1) * size, :] = lt_ref[at, :].astype(F32)
            out = dot(nat_ref[:rows, :].astype(BF16), right_ref[:, lo : lo + cols]).astype(BF16)

            @pl.when(i < first + steps // 2)
            def _():
                send_ref[...] = out

            @pl.when(i >= first + steps // 2)
            def _():
                keep_ref[...] = out


def wgrad_rows(groups, left, right, tile=1024, after=(), sends=(), cid=None):
    toks, d = right.shape
    rows = left.shape[1]
    n = rows // tile
    half = n // 2
    orders = [o for o, _ in groups]
    kind = BF16 if (rows >> len(flat_bits(orders[0][0]))) % 16 == 0 else F32
    cuts, out_specs, out_shape, lo = [], [], [], 0
    for g, (_, cols) in enumerate(groups):
        first = n * (g + 1)
        cuts.append((first, n, lo, cols))
        lo += cols
        out_specs.append(pl.BlockSpec((tile, cols), lambda i, *_, first=first: (jnp.clip(i - first, 0, half - 1), 0)))
        out_specs.append(pl.BlockSpec((tile, cols), lambda i, *_, first=first: (jnp.clip(i - first - half, 0, half - 1), 0)))
        out_shape += [jax.ShapeDtypeStruct((rows // 2, cols), BF16)] * 2
    return call(
        functools.partial(wgrad_rows_kernel, n, orders, cuts),
        left,
        right,
        grid=(n * (1 + len(groups)),),
        in_specs=[
            pl.BlockSpec((toks, tile), lambda i, *_: (0, jnp.minimum(i, n - 1))),
            pl.BlockSpec((toks, d), lambda i, *_: (0, 0)),
        ],
        out_specs=out_specs,
        scratch=[pltpu.VMEM((tile, toks), F32), pltpu.VMEM((rows, toks), kind)],
        out_shape=out_shape,
        flops=2 * toks * rows * d,
        nbytes=2 * (rows * (d + toks) + toks * d),
        name="wgrad_rows",
        after=after,
        sends=sends,
        cid=cid,
    )


def document_start(len_ref, at):
    begin, end = jnp.zeros_like(at), 0
    for k in range(len_ref.shape[0]):
        end = end + len_ref[k]
        begin = jnp.where(at >= end, end, begin)
    return begin


def d_ctx_kernel(halos, nseq, len_ref, a_ref, w_ref, out_ref, cos_ref, sin_ref, start_ref):
    out_ref[...] = dot_t(a_ref[...], w_ref[...]).astype(BF16)
    toks, rows = a_ref.shape[0], cos_ref.shape[0]
    me = lax.axis_index("seq")
    base = (me - halos) * toks
    at = base + pl.program_id(0) * rows + lax.broadcasted_iota(jnp.int32, (rows, LANES), 0)
    lane = lane_ids(rows) % HEAD
    half = ROT // 2
    freq = jnp.zeros((rows, LANES), F32)
    for k in range(half):
        freq = jnp.where(lane % half == k, 10000.0 ** (-(2.0 * k) / ROT), freq)
    angle = (at - document_start(len_ref, at)).astype(F32) * freq
    cos_ref[...] = jnp.where(lane < ROT, jnp.cos(angle), 1.0)
    sin = jnp.sin(angle)
    sin_ref[...] = jnp.where(lane < half, -sin, jnp.where(lane < ROT, sin, 0.0))
    own = me * toks + lax.broadcasted_iota(jnp.int32, (1, toks), 1)
    start_ref[...] = document_start(len_ref, own) - base


def d_context(lengths, grad, w, halos, nseq, tn=256, after=(), sends=(), cid=None):
    rows, d = grad.shape
    win = rows * (halos + 1)
    steps = d // tn
    table = pl.BlockSpec((win // steps, LANES), lambda i, *_: (i, 0))
    return call(
        functools.partial(d_ctx_kernel, halos, nseq),
        lengths,
        grad,
        w,
        scalars=1,
        grid=(steps,),
        in_specs=[whole((rows, d)), pl.BlockSpec((tn, d), lambda i, *_: (i, 0))],
        out_specs=[pl.BlockSpec((rows, tn), lambda i, *_: (0, i)), table, table, whole((1, rows))],
        out_shape=[
            jax.ShapeDtypeStruct((rows, d), BF16),
            jax.ShapeDtypeStruct((win, LANES), F32),
            jax.ShapeDtypeStruct((win, LANES), F32),
            jax.ShapeDtypeStruct((1, rows), jnp.int32),
        ],
        flops=2 * rows * d * d,
        nbytes=2 * d * (2 * rows + d),
        name="d_ctx",
        after=after,
        sends=sends,
        cid=cid,
    )


def lane_ids(rows):
    return lax.broadcasted_iota(jnp.int32, (rows, LANES), 1)


def turns():
    frm = lax.broadcasted_iota(jnp.int32, (LANES, LANES), 0)
    to = lax.broadcasted_iota(jnp.int32, (LANES, LANES), 1)
    half = ROT // 2
    within = frm % HEAD
    partner = jnp.where(within < half, frm + half, frm - half)
    rotated = within < ROT
    turned = (frm + HEAD) % LANES
    one = lambda hit: jnp.where(hit, 1.0, 0.0).astype(BF16)
    return one(turned == to), one(rotated & (partner == to)), one(rotated & ((partner + HEAD) % LANES == to))


def split(x):
    high = x.astype(BF16)
    return jnp.concatenate([high, (x - high.astype(F32)).astype(BF16)], axis=1)


def qkv_kernel(n, *refs):
    a_refs, (w_ref, bias_ref, cos_ref, sin_ref, q_ref, k_ref, v_ref) = refs[:n], refs[n:]
    turn, swap, swap_turn = turns()
    k_moves = jnp.concatenate([turn, swap_turn], axis=1)
    k_moves = jnp.concatenate([k_moves, k_moves], axis=0)
    q_moves = jnp.concatenate([swap, swap], axis=0)
    r = 0
    for a_ref in a_refs:
        rows = slice(r, r + a_ref.shape[0])
        r += a_ref.shape[0]
        first = lane_ids(a_ref.shape[0]) < HEAD
        packed = dot(a_ref[...], w_ref[...]) + bias_ref[...]
        cos, sin = cos_ref[rows, :], sin_ref[rows, :]
        for g in range(w_ref.shape[1] // PAIR):
            c = g * PAIR
            lanes = slice(g * LANES, (g + 1) * LANES)
            pa, pb, pc = packed[:, c : c + LANES], packed[:, c + LANES : c + 2 * LANES], packed[:, c + 2 * LANES : c + PAIR]
            both = dot(split(jnp.where(first, pc, pa)), k_moves)
            k_ref[rows, lanes] = (both[:, :LANES] * cos + both[:, LANES:] * sin).astype(BF16)
            v_ref[rows, lanes] = jnp.where(first, pb, pc).astype(BF16)
            if a_ref is a_refs[-1]:
                q = jnp.where(first, pa, pb)
                q_ref[:, lanes] = (q * cos + dot(split(q), q_moves) * sin).astype(BF16)


def qkv(pieces, w, bias, cos, sin, group=4, after=()):
    toks, d = pieces[-1].shape
    win = sum(p.shape[0] for p in pieces)
    cols = w.shape[1]
    out = pl.BlockSpec((win, group * LANES), lambda i: (0, i))
    return call(
        functools.partial(qkv_kernel, len(pieces)),
        *pieces, w, bias, cos, sin,
        grid=(cols // PAIR // group,),
        in_specs=[
            *[whole(p.shape) for p in pieces],
            pl.BlockSpec((d, group * PAIR), lambda i: (0, i)),
            pl.BlockSpec((1, group * PAIR), lambda i: (0, i)),
            whole((win, LANES)),
            whole((win, LANES)),
        ],
        out_specs=[pl.BlockSpec((toks, group * LANES), lambda i: (0, i)), out, out],
        out_shape=[jax.ShapeDtypeStruct((toks, cols // 3), BF16)] + [jax.ShapeDtypeStruct((win, cols // 3), BF16)] * 2,
        flops=2 * win * d * cols, nbytes=8 * win * d + 2 * d * cols,
        name="qkv",
        after=after,
    )


GROUP = 2
QB = 256


def attention_kernel(
    toks, win, start_ref, q_ref, k_ref, v_ref, do_ref, cos_ref, sin_ref, ctx_ref, dp_ref,
    k2, v2, kt, vt, s_ref, e_ref, dq_acc, dk_acc, dv_acc,
):
    nk = win // BLOCK
    halo = win - toks
    first = lane_ids(BLOCK) < HEAD
    first_q = lane_ids(QB) < HEAD
    zero = jnp.zeros((BLOCK, LANES), BF16)
    zero_q = jnp.zeros((QB, LANES), BF16)
    top = lax.broadcasted_iota(jnp.int32, (LANES, QB), 0) < HEAD
    groups = range(GROUP)
    lanes = [slice(g * LANES, (g + 1) * LANES) for g in groups]
    eye = lax.broadcasted_iota(jnp.int32, (LANES, LANES), 0) == lax.broadcasted_iota(jnp.int32, (LANES, LANES), 1)
    upper = lax.broadcasted_iota(jnp.int32, (LANES, LANES), 0) < HEAD
    eye0 = jnp.where(eye & upper, 1.0, 0.0).astype(BF16)
    eye1 = jnp.where(eye & ~upper, 1.0, 0.0).astype(BF16)

    def prepare(j, _):
        rows = pl.ds(pl.multiple_of(j * BLOCK, BLOCK), BLOCK)
        for g in groups:
            for src, two, tr in ((k_ref, k2, kt), (v_ref, v2, vt)):
                x = src[rows, lanes[g]]
                two[g, j, :BLOCK, :] = jnp.where(first, x, zero)
                two[g, j, BLOCK:, :] = jnp.where(first, zero, x)
                tr[g, j, :, :BLOCK] = dot_t(eye0, x).astype(BF16)
                tr[g, j, :, BLOCK:] = dot_t(eye1, x).astype(BF16)
        return 0

    lax.fori_loop(0, nk, prepare, 0)
    dk_acc[...] = jnp.zeros_like(dk_acc)
    dv_acc[...] = jnp.zeros_like(dv_acc)
    scale = HEAD**-0.5
    for i in range(toks // QB):
        rows = slice(i * QB, (i + 1) * QB)
        last = (halo + (i + 1) * QB) // BLOCK
        low = max(halo + i * QB - DOC_MOST + 1, 0) // BLOCK
        qs = [q_ref[rows, lanes[g]].astype(F32) * scale for g in groups]
        qts = [q.T.astype(BF16) for q in qs]
        qs = [q.astype(BF16) for q in qs]
        q2 = [jnp.concatenate([jnp.where(first_q, q, zero_q), jnp.where(first_q, zero_q, q)], axis=0) for q in qs]
        start = start_ref[:, rows]
        q_at = halo + i * QB + lax.broadcasted_iota(jnp.int32, (1, QB), 1)

        def scores(j, peaks):
            at = j * BLOCK + lax.broadcasted_iota(jnp.int32, (BLOCK, QB), 0)
            ok = (at >= start) & (at <= q_at)
            out = []
            for g in groups:
                s = dot(k2[g, j], qts[g])
                s0 = jnp.where(ok, s[:BLOCK], NEG)
                s1 = jnp.where(ok, s[BLOCK:], NEG)
                s_ref[g, j, :BLOCK, :] = s0
                s_ref[g, j, BLOCK:, :] = s1
                out.append(jnp.maximum(peaks[2 * g], jnp.max(s0, axis=0, keepdims=True)))
                out.append(jnp.maximum(peaks[2 * g + 1], jnp.max(s1, axis=0, keepdims=True)))
            return tuple(out)

        floor = jnp.full((1, QB), NEG, F32)
        peaks = lax.fori_loop(low, last, scores, (floor,) * (2 * GROUP), unroll=True)

        def weigh(j, carry):
            out = []
            for g in groups:
                t0, t1, acc = carry[3 * g : 3 * g + 3]
                e0 = jnp.exp(s_ref[g, j, :BLOCK, :] - peaks[2 * g])
                e1 = jnp.exp(s_ref[g, j, BLOCK:, :] - peaks[2 * g + 1])
                b0, b1 = e0.astype(BF16), e1.astype(BF16)
                e_ref[g, j, :BLOCK, :] = b0
                e_ref[g, j, BLOCK:, :] = b1
                acc = acc + dot(vt[g, j], jnp.concatenate([b0, b1], axis=0))
                out += [t0 + jnp.sum(e0, axis=0, keepdims=True), t1 + jnp.sum(e1, axis=0, keepdims=True), acc]
            return tuple(out)

        none = jnp.zeros((1, QB), F32)
        sums = lax.fori_loop(low, last, weigh, (none, none, jnp.zeros((LANES, QB), F32)) * GROUP, unroll=True)
        do_l, do2, d0, d1 = [], [], [], []
        for g in groups:
            t0, t1, acc = sums[3 * g : 3 * g + 3]
            share = jnp.where(top, 1.0 / t0, 1.0 / t1)
            ctx_t = acc * share
            ctx_ref[rows, lanes[g]] = ctx_t.T.astype(BF16)
            do_t = do_ref[rows, lanes[g]].astype(F32).T * share
            both = do_t * ctx_t
            d0.append(jnp.sum(both[:HEAD], axis=0, keepdims=True))
            d1.append(jnp.sum(both[HEAD:], axis=0, keepdims=True))
            do = do_t.T.astype(BF16)
            do_l.append(do_t.astype(BF16))
            do2.append(jnp.concatenate([jnp.where(first_q, do, zero_q), jnp.where(first_q, zero_q, do)], axis=0))

        def back(j, dqs):
            at = pl.ds(pl.multiple_of(j * BLOCK, BLOCK), BLOCK)
            out = []
            for g in groups:
                dp = dot(v2[g, j], do_l[g])
                e0, e1 = e_ref[g, j, :BLOCK, :], e_ref[g, j, BLOCK:, :]
                ds0 = (e0.astype(F32) * (dp[:BLOCK] - d0[g])).astype(BF16)
                ds1 = (e1.astype(F32) * (dp[BLOCK:] - d1[g])).astype(BF16)
                dv_acc[at, lanes[g]] += dot(jnp.concatenate([e0, e1], axis=1), do2[g])
                dk_acc[at, lanes[g]] += dot(jnp.concatenate([ds0, ds1], axis=1), q2[g])
                out.append(dqs[g] + dot(kt[g, j], jnp.concatenate([ds0, ds1], axis=0)))
            return tuple(out)

        dqs = lax.fori_loop(low, last, back, (jnp.zeros((LANES, QB), F32),) * GROUP, unroll=True)
        for g in groups:
            dq_acc[rows, lanes[g]] = dqs[g].T * scale

    turn, swap, swap_turn = turns()
    for j in range(nk):
        rows = slice(j * BLOCK, (j + 1) * BLOCK)
        cos, sin = cos_ref[rows, :], sin_ref[rows, :]
        for g in groups:
            dk = dk_acc[rows, lanes[g]].astype(BF16)
            dk = dot(dk, turn) * cos - dot(dk, swap_turn) * sin
            dv = dv_acc[rows, lanes[g]]
            if j * BLOCK >= halo:
                own = slice(j * BLOCK - halo, (j + 1) * BLOCK - halo)
                dq = dq_acc[own, lanes[g]]
                dq = dq * cos - dot(dq.astype(BF16), swap) * sin
            else:
                dq = jnp.zeros_like(dk)
            c = g * PAIR
            dp_ref[rows, c : c + LANES] = jnp.where(first, dq, dk).astype(BF16)
            dp_ref[rows, c + LANES : c + 2 * LANES] = jnp.where(first, dv, dq).astype(BF16)
            dp_ref[rows, c + 2 * LANES : c + PAIR] = jnp.where(first, dk, dv).astype(BF16)


def attention(start, q, k, v, d_ctx, cos, sin, pair, pairs, after=(), sends=(), cid=None):
    win, d = k.shape
    toks = d_ctx.shape[0]
    nk = win // BLOCK
    width = GROUP * LANES
    at = pair // GROUP
    own = pl.BlockSpec((toks, width), lambda i: (0, at + i))
    every = pl.BlockSpec((win, width), lambda i: (0, at + i))
    out = pairs * LANES
    return call(
        functools.partial(attention_kernel, toks, win),
        start,
        q,
        k,
        v,
        d_ctx,
        cos,
        sin,
        grid=(pairs // GROUP,),
        in_specs=[whole((1, toks)), own, every, every, own, whole((win, LANES)), whole((win, LANES))],
        out_specs=[pl.BlockSpec((toks, width), lambda i: (0, i)), pl.BlockSpec((win, GROUP * PAIR), lambda i: (0, i))],
        out_shape=[jax.ShapeDtypeStruct((toks, out), BF16), jax.ShapeDtypeStruct((win, 3 * out), BF16)],
        scratch=[
            pltpu.VMEM((GROUP, nk, 2 * BLOCK, LANES), BF16),
            pltpu.VMEM((GROUP, nk, 2 * BLOCK, LANES), BF16),
            pltpu.VMEM((GROUP, nk, LANES, 2 * BLOCK), BF16),
            pltpu.VMEM((GROUP, nk, LANES, 2 * BLOCK), BF16),
            pltpu.VMEM((GROUP, nk, 2 * BLOCK, QB), F32),
            pltpu.VMEM((GROUP, nk, 2 * BLOCK, QB), BF16),
            pltpu.VMEM((toks, width), F32),
            pltpu.VMEM((win, width), F32),
            pltpu.VMEM((win, width), F32),
        ],
        flops=pairs * toks * DOC_MOST * 4 * 6 * LANES,
        nbytes=14 * win * out,
        trans=pairs * 2 * toks * DOC_MOST,
        name="attention",
        after=after,
        sends=sends,
        cid=cid,
    )


def tail_kernel(cfg, *refs):
    ndp, nseq, halos, n_pieces, n_dp, n_ctx, joins, last_c = cfg
    refs = list(refs)
    take = lambda n: [refs.pop(0) for _ in range(n)]
    dp_rows, (w_ref,) = take(n_dp), take(1)
    n_late = n_dp - 2 + n_pieces + n_ctx + 3
    late = take(n_late)
    mlp_ref, wd_ref, bias_ref, g1, g2 = take(5)
    gsum_ref, qsum_ref, isum_ref = take(3)
    left_q, own_q = take(2)
    hidden_ref, grad_in_ref, small = take(3)
    owns = take(3)
    last_gots = [take(len(fan(last_c)) - 1) for _ in owns]
    nat, lt, own_acc, far, far_got = take(5)
    group_bufs = [take(6), take(6), [None, own_q.at[0], None, left_q, *take(2)]]
    bsum_ref, small_got = take(2)
    held = take(n_late)
    send_sem, recv_sem, late_sem = refs
    loads = [pltpu.make_async_copy(a, b, late_sem.at[k]) for k, (a, b) in enumerate(zip(late, held))]
    held = list(held)
    take_held = lambda n: [held.pop(0) for _ in range(n)]
    dp_cols, pieces, ctxs = take_held(n_dp - 2), take_held(n_pieces), take_held(n_ctx)
    grad_ref, x_ref, d_mlp_ref = held
    first_loads = n_dp - 2 + n_pieces
    toks, d = x_ref.shape
    me_dp, me_seq = lax.axis_index("dp"), lax.axis_index("seq")
    dp_bits = stage_bits(ndp)
    core, cross = fan(dp_bits[:1]), fan(dp_bits[1:])
    across = fan(last_c)

    def device(axis, offset):
        return (me_dp ^ offset, me_seq) if axis == "dp" else (me_dp, me_seq ^ offset)

    behind = (me_dp, lax.rem(me_seq + nseq - 1, nseq))
    ahead = (me_dp, lax.rem(me_seq + 1, nseq))
    names = {}

    def copy(name, src, dst, to):
        k = names.setdefault(name, len(names))
        return pltpu.make_async_remote_copy(
            src_ref=src,
            dst_ref=dst,
            send_sem=send_sem.at[k],
            recv_sem=recv_sem.at[k],
            device_id=to,
            device_id_type=pl.DeviceIdType.MESH,
        )

    half = toks // 2

    def far_copy(k, c):
        rows = pl.ds(c * half, half)
        return copy(("far", k, c), far.at[k, rows], far_got.at[k, rows], behind)


    def first(n):
        send, _, got, *_ = group_bufs[n]
        return copy(("core", n), send, got, device("dp", core[1]))

    def second(n):
        _, _, _, out, into, _ = group_bufs[n]
        start = 1 if n < 2 else 0
        return [copy(("cross", n, k), out.at[k - start], into.at[k - 1], device("dp", cross[k])) for k in range(1, len(cross))]

    def third(n):
        out, got = group_bufs[n][5], last_gots[(n + 1) % 3]
        return [copy(("across", n, k), out.at[k - 1], got[k - 1], device("seq", across[k])) for k in range(1, len(across))]

    def to_second(n):
        _, keep, got, out, _, _ = group_bufs[n]
        first(n).wait()
        rows = out.shape[1]
        for k, c in enumerate(second(n), 1):
            at = slice(k * rows, (k + 1) * rows)
            out[k - 1] = (keep[at, :].astype(F32) + got[at, :].astype(F32)).astype(BF16)
            c.start()

    def to_third(n):
        _, keep, got, _, into, out = group_bufs[n]
        for c in second(n):
            c.wait()
        own = owns[(n + 1) % 3]
        rows = own.shape[0]
        copies = third(n)
        for k in reversed(range(len(across))):
            at = slice(k * rows, (k + 1) * rows)
            total = keep[at, :].astype(F32)
            if got is not None:
                total += got[at, :].astype(F32)
            for b in range(len(cross) - 1):
                total += into[b, at, :].astype(F32)
            if k:
                out[k - 1] = total.astype(out.dtype)
                copies[k - 1].start()
            else:
                own[...] = total

    def pass_on(k, c):
        far_copy(k - 1, c).wait()
        rows = pl.ds(c * half, half)
        far[k, rows] = (far[k, rows].astype(F32) + far_got[k - 1, rows].astype(F32)).astype(BF16)
        far_copy(k, c).start()

    def back(rows=slice(None)):
        total, at = None, 0
        for a_ref in dp_rows:
            n = a_ref.shape[1]
            term = dot_t(a_ref[rows, :], w_ref[:, at : at + n])
            total, at = term if total is None else total + term, at + n
        return total

    step = [0]
    pid = pl.program_id(0)

    def phase(fn):
        pl.when(pid == step[0])(fn)
        step[0] += 1

    for k in range(halos):

        def do_far(k=k):
            if k == 0:
                offsets = [("dp", o) for o in (*core[1:], *cross[1:])] + [("seq", o) for o in across[1:]]
                greet([device(*o) for o in offsets] + [behind, ahead])
                for c in loads + second(2):
                    c.start()
            for c in range(2):
                rows = slice(c * half, (c + 1) * half)
                far[k, rows] = back(rows).astype(BF16)
                if k == 0:
                    far_copy(0, c).start()

        phase(do_far)

    def do_columns():
        for c in loads[:first_loads]:
            c.wait()
        col = 0
        for left in pieces:
            n = left.shape[0]
            turned(left[...], nat.at[:, :n], 0)
            placed((short_order(ndp, nseq), nseq), nat.at[:, :n], lt.at[:, col : col + n])
            col += n
        send, keep = group_bufs[0][:2]
        half, at = keep.shape[0], 0
        for right_ref in dp_cols:
            right = right_ref[...]
            n = right.shape[1]
            send[:, at : at + n] = dot(lt[half:, :], right).astype(BF16)
            keep[:, at : at + n] = dot(lt[:half, :], right).astype(BF16)
            bsum_ref[:, at : at + n] = jnp.sum(right.astype(F32), axis=0, keepdims=True)
            at += n
        first(0).start()
        if halos > 1:
            pass_on(1, 0)

    phase(do_columns)

    def do_dense():
        for c in loads[first_loads:]:
            c.wait()
        at = 0
        for ctx in ctxs:
            turned(ctx[...], nat, at)
            at += ctx.shape[1]
        placed((short_order(ndp, nseq), nseq), nat, lt.at[:, :toks])
        send, keep = group_bufs[1][:2]
        half = keep.shape[0]
        send[...] = dot(lt[half:, :toks], grad_ref[...]).astype(BF16)
        first(1).start()
        keep[...] = dot(lt[:half, :toks], grad_ref[...]).astype(BF16)
        to_second(0)

    phase(do_dense)

    def do_own():
        own_acc[...] = back()
        if halos > 1:
            pass_on(1, 1)
        to_second(1)

    phase(do_own)
    for t in range(joins):

        def do_join(t=t):
            cols = hidden_ref.shape[1]
            at = slice(t * cols, (t + 1) * cols)
            total, row = x_ref[:, at].astype(F32) + mlp_ref[...] + bias_ref[:, at], 0
            for ctx in ctxs:
                n = ctx.shape[1]
                total += dot(ctx[...], wd_ref[row : row + n, :])
                row += n
            hidden_ref[...] = total.astype(BF16)

        phase(do_join)

    def do_rest():
        for k in range(2, halos):
            for c in range(2):
                pass_on(k, c)
        small[...] = jnp.zeros_like(small)
        rows = min(128, half)
        for r in range(0, toks, rows):
            if r % half == 0:
                far_copy(halos - 1, r // half).wait()
                if r == 0:
                    for n in (2, 0, 1):
                        to_third(n)
            at = slice(r, r + rows)
            u, inv = unit_of(x_ref[at, :].astype(F32))
            d1 = own_acc[at, :] + far_got[halos - 1, at, :].astype(F32)
            d2 = d_mlp_ref[at, :]
            e = d1 * g1[...] + d2 * g2[...]
            dx = inv * (e - jnp.mean(e, axis=-1, keepdims=True) - u * jnp.mean(e * u, axis=-1, keepdims=True))
            grad_in_ref[at, :] = grad_ref[at, :].astype(F32) + dx
            for k, v in enumerate((d1 * u, d1, d2 * u, d2)):
                small[k : k + 1, :] += jnp.sum(v, axis=0, keepdims=True)
        small[4:5, :] = gsum_ref[...]
        row = 5
        for parts in ((qsum_ref, bsum_ref), (isum_ref,)):
            flat = jnp.concatenate([p[...] for p in parts], axis=1)
            for c in range(0, flat.shape[1], d):
                small[row : row + 1, :] = flat[:, c : c + d]
                row += 1
        used = 0
        for axis, offsets in (("dp", core), ("dp", cross), ("seq", across)):
            copies = []
            for o in offsets[1:]:
                copies.append(copy(("small", used), small, small_got.at[used], device(axis, o)))
                copies[-1].start()
                used += 1
            for c in copies:
                c.wait()
            total = small[...]
            for k in range(used - len(copies), used):
                total += small_got[k]
            small[...] = total
        for c in third(0) + third(1) + third(2):
            c.wait()

    phase(do_rest)


def tail(dps, w, pieces, ctxs, grad, x, mlp_out, d_mlp, w_d, bias, g1, g2, sums, left_q, ndp, nseq, halos, after=()):
    toks, d = x.shape
    depth = w.shape[1]
    joins = 4
    own_at = halos + 2
    dp_bits, seq_bits = stage_bits(ndp), stage_bits(nseq)
    cross, across = 1 << len(dp_bits[1:]), 1 << len(seq_bits)
    tile = d // joins
    once = lambda shape: pl.BlockSpec(shape, lambda i: (0,) * len(shape), pipeline_mode=pl.Buffered(1))
    piece_at = lambda i: (jnp.where(i < halos, i, jnp.where(i < own_at, halos - 1, halos)), 0)
    join_at = lambda i: (0, jnp.clip(i - own_at - 1, 0, joins - 1))
    hbm = pl.BlockSpec(memory_space=pl.ANY)
    cut_up = lambda a, n: a.reshape(n, a.shape[0] // n, a.shape[1])
    left_q = cut_up(left_q, cross)
    late = [*dps[2:], *pieces, *ctxs, grad, x, d_mlp]
    ins = [*dps, w, *late, mlp_out, w_d, bias, g1, g2, *sums, left_q, left_q]
    in_specs = (
        [pl.BlockSpec((toks, a.shape[1]), piece_at) for a in dps]
        + [once(w.shape)]
        + [hbm] * len(late)
        + [pl.BlockSpec((toks, tile), join_at), pl.BlockSpec((d, tile), join_at)]
        + [once((1, d))] * 3
        + [once(v.shape) for v in sums]
        + [hbm, once((1, *left_q.shape[1:]))]
    )
    rest = sum(a.shape[1] for a in dps[2:])
    lines = 4 + sum(v.shape[1] for v in sums) // d + 1
    lines += -lines % 8
    widths = [left_q.shape[2], rest, d]
    left = d // 2 // cross // across
    kind = BF16 if left % 16 == 0 else F32
    out_shape = [
        jax.ShapeDtypeStruct((toks, d), BF16),
        jax.ShapeDtypeStruct((toks, d), F32),
        jax.ShapeDtypeStruct((lines, d), F32),
        *[jax.ShapeDtypeStruct((left, n), F32) for n in widths],
        *[jax.ShapeDtypeStruct((left, n), kind) for n in widths for _ in range(across - 1)],
    ]
    fixed = lambda shape: pl.BlockSpec(shape, lambda i: (0,) * len(shape))
    out_specs = (
        [pl.BlockSpec((toks, tile), join_at), fixed((toks, d))]
        + [fixed((lines, d))]
        + [fixed((left, n)) for n in widths]
        + [hbm] * (len(widths) * (across - 1))
    )
    scratch = [
        pltpu.VMEM((d, toks), F32),
        pltpu.VMEM((d, toks * (halos + 1)), BF16),
        pltpu.VMEM((toks, d), F32),
        pltpu.VMEM((halos, toks, d), BF16),
        pltpu.VMEM((halos, toks, d), BF16),
    ]
    for n in widths[1:]:
        scratch += [pltpu.VMEM((d // 2, n), BF16)] * 3
        scratch += [pltpu.VMEM((cross - 1, d // 2 // cross, n), BF16)] * 2
        scratch += [pltpu.VMEM((across - 1, left, n), kind)]
    scratch += [pltpu.VMEM((cross - 1, *left_q.shape[1:]), BF16), pltpu.VMEM((across - 1, left, widths[0]), kind)]
    scratch += [pltpu.VMEM((1, rest), F32), pltpu.VMEM((1 + cross - 1 + across - 1, lines, d), F32)]
    scratch += [pltpu.VMEM(a.shape, a.dtype) for a in late]
    copies = 2 * halos + 4 * (1 + cross - 1 + across - 1)
    scratch += [pltpu.SemaphoreType.DMA((copies,))] * 2 + [pltpu.SemaphoreType.DMA((len(late),))]
    cfg = (ndp, nseq, halos, len(pieces), len(dps), len(ctxs), joins, seq_bits)
    n = len(ins)

    def body(*refs):
        tail_kernel(cfg, *refs[:n], *refs[n + len(after) :])

    outs = pl.pallas_call(
        body,
        grid_spec=pltpu.PrefetchScalarGridSpec(
            num_scalar_prefetch=0,
            grid=(own_at + 1 + joins + 1,),
            in_specs=in_specs + [hbm] * len(after),
            out_specs=out_specs,
            scratch_shapes=scratch,
        ),
        out_shape=out_shape,
        compiler_params=pltpu.CompilerParams(vmem_limit_bytes=63 * MIB, collective_id=1, has_side_effects=True),
        cost_estimate=pl.CostEstimate(flops=20 * toks * d * depth, bytes_accessed=40 * toks * d, transcendentals=0),
        name="tail",
    )(*ins, *after)
    outs = list(outs)
    main, own, outs = outs[:3], outs[3:6], outs[6:]
    terms = []
    for a in own:
        terms.append(([(v, 0) for v in (a, *outs[: across - 1])], 0, left, F32))
        outs = outs[across - 1 :]
    return main, terms


def shards(
    hidden_in,
    doc_lengths,
    ln1_gain,
    ln1_bias,
    ln2_gain,
    ln2_bias,
    qkv_weight,
    qkv_bias,
    dense_weight,
    dense_bias,
    fc_in_weight,
    fc_in_bias,
    fc_out_weight,
    fc_out_bias,
    out_grad,
):
    _, toks, d = hidden_in.shape
    ff = fc_in_weight.shape[1]
    ndp, nseq = lax.axis_size("dp"), lax.axis_size("seq")
    ndev = ndp * nseq
    sizes = {"dp": ndp, "seq": nseq}
    me_dp, me_seq = lax.axis_index("dp"), lax.axis_index("seq")
    row = lambda v: v.reshape(1, -1)

    halos = max(min(-(-(DOC_MOST - 1) // toks), nseq - 1), 1)
    lengths = doc_lengths.reshape(-1)
    x = hidden_in.reshape(toks, d)
    a_own, m_own, grad, grad_sum = norms(
        lengths, x, out_grad.reshape(toks, d), row(ln1_gain), row(ln1_bias), row(ln2_gain), row(ln2_bias)
    )

    ahead = [(i, (i + 1) % nseq) for i in range(nseq)]
    on = ("ring", 1, nseq)
    fine = toks // 4 % LANES == 0
    cut = toks * 3 // 4 if fine else toks
    mlp_out, act, d_pre, d_mlp, b_in_sum, near = mlp(
        m_own, grad, fc_in_weight, row(fc_in_bias), fc_out_weight, sends=[(a_own, 0, cut, on)], cid=2
    )
    near, far = [near], []
    two = halos > 1

    orders = [stage_order(ndp, nseq, kind) for kind in range(3)]
    srcs = [(o, nseq) for o in orders]
    in_cut, out_cut = ff * 5 // 8, d // 4
    sends = [(a_own, cut, toks - cut, on)] if fine else []
    if two:
        sends.append((near[0], 0, toks // 4 if fine else toks // 2, on))
    s0, k0, line, s1, k1, _, *got = wgrad(
        [(srcs[0], in_cut), (srcs[2], ff - in_cut)], [m_own], d_pre, sends=sends, cid=3 if sends else None
    )
    near += got[:1] if fine else []
    far += got[-1:] if two else []
    early = [Halving(s0, k0, orders[0], sizes), Halving(s1, k1, orders[2], sizes)]
    s2, k2, s3, k3, *got = wgrad_rows(
        [(srcs[2], out_cut), (srcs[1], d - out_cut)],
        act,
        grad,
        after=[line],
        sends=[send for r in early for send in r.sends()]
        + ([(near[0], far[0].shape[0], toks // 2, on)] if two else []),
        cid=4,
    )
    for r in early:
        r.receive([got.pop(0)])
    far += got
    late = [Halving(s2, k2, orders[2], sizes), Halving(s3, k3, orders[1], sizes)]
    fc = early + late
    d_ctx, cos, sin, start, *got = d_context(
        lengths,
        grad,
        dense_weight,
        halos,
        nseq,
        sends=[send for r in late for send in r.sends()] + ([(near[1], 0, toks - cut, on)] if two and fine else []),
        cid=5,
    )
    for r in late:
        r.receive([got.pop(0)])
    far += got
    pieces = [*far, *near, a_own]
    for k in range(2, halos):
        far = [lax.ppermute(jnp.concatenate(far, axis=0), "seq", ahead)]
        pieces = far + pieces
    last = advance(fc, [d_ctx])
    for r in fc:
        r.permute()
    q, k, v = qkv(pieces, qkv_weight, row(qkv_bias), cos, sin, after=last)

    order_c = short_order(ndp, nseq)
    src_c = (order_c, nseq)
    pairs = d // LANES
    quarter = pairs // 4

    def part(at, n, sums=(), **more):
        sends = [send for r in sums for send in r.sends()]
        ctx, dp, *got = attention(
            start, q, k, v, d_ctx, cos, sin, at * quarter, n * quarter, sends=sends, cid=6 + at if sends else None, **more
        )
        for r in sums:
            r.receive([got.pop(0) for _ in r.targets()])
        return ctx, dp

    ctx_a, dp_a = part(0, 1)
    advance(fc, [ctx_a])
    ctx_b, dp_b = part(1, 1, fc)
    advance(fc, [ctx_b])
    qa_send, qa_keep, b_qkv_a, *got = wgrad(
        [(src_c, dp_a.shape[1] * 2)], pieces, [dp_a, dp_b], tn=dp_a.shape[1], sends=[send for r in fc for send in r.sends()], cid=10
    )
    for r in fc:
        r.receive([got.pop(0) for _ in r.targets()])
    r_qa = Halving(qa_send, qa_keep, order_c, sizes)
    last = advance(fc, [b_qkv_a])
    while len(fc[0].stages) > 1:
        for r in fc:
            r.permute()
        last = advance(fc, last)
    ctx_c, dp_c = part(2, 2, [*fc, r_qa])
    left_q, g_in, g_out = combine([r_qa.rest(), *[(*r.rest()[:3], F32) for r in fc]], [ctx_c], joined=(2, 4))
    main, terms = tail(
        [dp_a, dp_b, dp_c],
        qkv_weight,
        pieces,
        [ctx_a, ctx_b, ctx_c],
        grad,
        x,
        mlp_out,
        d_mlp,
        dense_weight,
        row(dense_bias + fc_out_bias),
        row(ln1_gain),
        row(ln2_gain),
        [grad_sum, b_qkv_a, b_in_sum],
        left_q,
        ndp,
        nseq,
        halos,
    )
    hidden_out, grad_in, small = main
    g_qkv, g_dense, *parts = last_sums(terms, small, ff, ndev, nseq)
    o1g, o1b, o2g, o2b, o_db, o_ob, o_qb, o_ib = (v.reshape(-1) for v in parts)
    return (
        hidden_out.reshape(hidden_in.shape),
        grad_in.reshape(hidden_in.shape),
        o1g,
        o1b,
        o2g,
        o2b,
        g_qkv,
        o_qb,
        g_dense,
        o_db,
        g_in,
        o_ib,
        g_out,
        o_ob,
    )


def solution(mesh):
    both = P(("dp", "seq"))
    rows = P(("dp", "seq"), None)
    toks = P("dp", "seq", None)
    return jax.shard_map(
        shards,
        mesh=mesh,
        in_specs=(toks, P("dp", None)) + (P(),) * 12 + (toks,),
        out_specs=(toks, toks, both, both, both, both, rows, both, rows, both, rows, both, rows, both),
        check_vma=False,
    )
```

```python
import functools
import math

import jax
import jax.numpy as jnp
from jax import lax
from jax.experimental import pallas as pl
from jax.experimental.pallas import tpu as pltpu
from jax.sharding import PartitionSpec as P

HEADS = 16
HEAD = 64
ROT = 16
DOC_MOST = 1024
EPS = 1e-05
NEG = -1e30
LANES = 128
PAIR = 3 * LANES
BLOCK = 256
F32 = jnp.float32
BF16 = jnp.bfloat16
MIB = 1 << 20
VMEM_MIB = 56


def dot(a, b):
    return lax.dot_general(a, b, (((1,), (0,)), ((), ())), preferred_element_type=F32)


def dot_t(a, b):
    return lax.dot_general(a, b, (((1,), (1,)), ((), ())), preferred_element_type=F32)


def whole(shape):
    return pl.BlockSpec(shape, lambda *_: (0,) * len(shape))


def place(to):
    at = {"dp": lax.axis_index("dp"), "seq": lax.axis_index("seq")}
    if to[0] == "ring":
        at["seq"] = lax.rem(at["seq"] + to[1] + to[2], to[2])
    else:
        at[to[0]] = at[to[0]] ^ to[1]
    return (at["dp"], at["seq"])


def both_ways(targets):
    back = [("ring", -to[1], to[2]) for to in targets if to[0] == "ring"]
    return [place(to) for to in sorted({*targets, *back})]


def greet(devices):
    barrier = pltpu.get_barrier_semaphore()
    for device in devices:
        pl.semaphore_signal(barrier, inc=1, device_id=device, device_id_type=pl.DeviceIdType.MESH)
    pl.semaphore_wait(barrier, len(devices))


def call(kernel, *args, grid, in_specs, out_specs, out_shape, name, flops, nbytes, trans=0, scalars=0, scratch=(), after=(), sends=(), cid=None):
    n, n_out, m = scalars + len(in_specs), len(out_specs), len(sends)

    def body(*refs):
        refs = list(refs)
        ins, _, srcs = refs[:n], refs[n : n + len(after)], refs[n + len(after) :][:m]
        rest = refs[n + len(after) + m :]
        outs, gots, own = rest[:n_out], rest[n_out : n_out + m], rest[n_out + m :]
        if not m:
            kernel(*ins, *outs, *own)
            return
        *own, send_sem, recv_sem = own

        def copy(k):
            _, lo, rows, to = sends[k]
            return pltpu.make_async_remote_copy(
                src_ref=srcs[k].at[pl.ds(lo, rows)],
                dst_ref=gots[k],
                send_sem=send_sem.at[k],
                recv_sem=recv_sem.at[k],
                device_id=place(to),
                device_id_type=pl.DeviceIdType.MESH,
            )

        @pl.when(pl.program_id(0) == 0)
        def _():
            greet(both_ways([to for *_, to in sends]))
            for k in range(m):
                copy(k).start()

        kernel(*ins, *outs, *own)

        @pl.when(pl.program_id(0) == grid[0] - 1)
        def _():
            for k in range(m):
                copy(k).wait()

    hbm = pl.BlockSpec(memory_space=pl.ANY)
    more = dict(collective_id=cid, has_side_effects=True) if m else {}
    sems = [pltpu.SemaphoreType.DMA((m,))] * 2 if m else []
    return pl.pallas_call(
        body,
        grid_spec=pltpu.PrefetchScalarGridSpec(
            num_scalar_prefetch=scalars,
            grid=grid,
            in_specs=[*in_specs, *[hbm] * (len(after) + m)],
            out_specs=[*out_specs, *[hbm] * m],
            scratch_shapes=[*scratch, *sems],
        ),
        out_shape=[*out_shape, *[jax.ShapeDtypeStruct((rows, a.shape[1]), a.dtype) for a, _, rows, _ in sends]],
        compiler_params=pltpu.CompilerParams(vmem_limit_bytes=VMEM_MIB * MIB, **more),
        cost_estimate=pl.CostEstimate(flops=int(flops), bytes_accessed=int(nbytes), transcendentals=int(trans)),
        name=name,
    )(*args, *after, *[a for a, *_ in sends])


def stage_bits(size):
    return [1 << b for b in range(size.bit_length() - 1)]


def stage_order(ndp, nseq, kind):
    dp_bits = [("dp", [b]) for b in stage_bits(ndp)]
    seq_bits = [("seq", [b]) for b in stage_bits(nseq)]
    cycle = [*dp_bits[1:], *seq_bits[:1]]
    kind = min(kind, len(cycle) - 1)
    at = (0, len(cycle) - 1, 1)[kind] if kind else 0
    return dp_bits[:1] + cycle[at:] + cycle[:at] + seq_bits[1:]


def short_order(ndp, nseq):
    dp_bits = stage_bits(ndp)
    return [("dp", dp_bits[:1]), ("dp", dp_bits[1:]), ("seq", stage_bits(nseq))]


def flat_bits(stages):
    return [(axis, bit) for axis, bits in stages for bit in bits]


def source(spot, stages, nseq):
    at = {"dp": lax.axis_index("dp"), "seq": lax.axis_index("seq")}
    bits = flat_bits(stages)
    for k, (axis, bit) in enumerate(bits):
        flag = spot // (1 << (len(bits) - 1 - k)) % 2
        if not (isinstance(flag, int) and flag == 0):
            at[axis] = at[axis] + flag * bit * (1 - 2 * (at[axis] // bit % 2))
    return at["dp"] * nseq + at["seq"]


def fan(bits):
    return [sum(b for k, b in enumerate(bits) if (part >> (len(bits) - 1 - k)) & 1) for part in range(1 << len(bits))]


def combine_kernel(counts, slots, *refs):
    outs = refs[sum(counts) :]
    at = 0
    for n, (k, col) in zip(counts, slots):
        total = refs[at][...].astype(F32)
        for r in refs[at + 1 : at + n]:
            total += r[...].astype(F32)
        outs[k][:, col : col + total.shape[1]] = total.astype(outs[k].dtype)
        at += n


def combine(items, after=(), joined=()):
    steps = 2 if all(rows % 32 == 0 for _, _, rows, _ in items) else 1
    ins, specs, counts, slots, shapes, nbytes = [], [], [], [], [], 0
    for k, (arrays, lo, rows, dtype) in enumerate(items):
        block, cols = rows // steps, arrays[0][0].shape[1]
        arrays = [(a, off) for a, off in arrays if off <= lo < off + a.shape[0]]
        for a, off in arrays:
            ins.append(a)
            specs.append(pl.BlockSpec((block, cols), lambda i, at=(lo - off) // block: (at + i, 0)))
        counts.append(len(arrays))
        if k in joined:
            slots.append((len(shapes) - 1, shapes[-1][1]))
            shapes[-1] = (rows, shapes[-1][1] + cols, dtype)
        else:
            slots.append((len(shapes), 0))
            shapes.append((rows, cols, dtype))
        nbytes += rows * cols * 2 * (len(arrays) + 2)
    return call(
        functools.partial(combine_kernel, counts, slots),
        *ins,
        grid=(steps,),
        in_specs=specs,
        out_specs=[pl.BlockSpec((rows // steps, cols), lambda i: (i, 0)) for rows, cols, _ in shapes],
        out_shape=[jax.ShapeDtypeStruct((rows, cols), dtype) for rows, cols, dtype in shapes],
        name="combine",
        flops=nbytes,
        nbytes=nbytes,
        after=after,
    )


def last_kernel(counts, nseq, *refs):
    n = sum(counts)
    small_ref, done_ref, kept_ref, *outs = refs[n:]
    kept_ref[...] = done_ref[...]
    combine_kernel(counts, [(0, 0), (0, refs[0].shape[1]), (1, 0)], *refs[:n], *outs[:2])
    d = small_ref.shape[1]
    me = lax.axis_index("dp") * nseq + lax.axis_index("seq")
    lines = [(k, 1) for k in (0, 1, 2, 3, 4, 4)] + [(5, 3), (8, outs[-1].shape[1] * d // outs[2].shape[1] // d)]
    for (at, rows), out in zip(lines, outs[2:]):
        flat = jnp.concatenate([small_ref[at + r : at + r + 1, :] for r in range(rows)], axis=1)
        flat = jnp.broadcast_to(flat, (8, rows * d))
        mine = out.shape[1]
        out[...] = pltpu.roll(flat, rows * d - me * mine, 1)[:1, :mine]


def last_sums(terms, small, done, ff, ndev, nseq):
    arrays = [a for term, *_ in terms for a, _ in term]
    rows = terms[0][2]
    d = small.shape[1]
    widths = [term[0][0].shape[1] for term, *_ in terms]
    shapes = [(rows, widths[0] + widths[1]), (rows, widths[2])] + [(1, d // ndev)] * 6 + [(1, 3 * d // ndev), (1, ff // ndev)]
    return call(
        functools.partial(last_kernel, [len(term) for term, *_ in terms], nseq),
        *arrays,
        small,
        done,
        grid=(1,),
        in_specs=[whole((rows, a.shape[1])) for a in arrays] + [whole(small.shape), whole(done.shape)],
        out_specs=[whole(done.shape)] + [whole(shape) for shape in shapes],
        out_shape=[jax.ShapeDtypeStruct(done.shape, done.dtype)] + [jax.ShapeDtypeStruct(shape, F32) for shape in shapes],
        name="last",
        flops=rows * d * 20,
        nbytes=rows * d * 40,
    )


class Halving:
    def __init__(self, send, keep, stages, sizes):
        self.keep, self.stages, self.sizes = keep, list(stages), sizes
        self.rows, self.got, self.ready = keep.shape[0], [], [send]

    def targets(self):
        axis, bits = self.stages[0]
        return [(axis, offset) for offset in fan(bits)[1:]]

    def permute(self):
        for part, (axis, offset) in zip(self.ready, self.targets()):
            self.got.append((lax.ppermute(part, axis, [(i, i ^ offset) for i in range(self.sizes[axis])]), 0))
        self.stages.pop(0)

    def sends(self, lo=0, hi=1, parts=1):
        size = self.ready[0].shape[0] // parts
        return [(a, lo * size, (hi - lo) * size, to) for a, to in zip(self.ready, self.targets())]

    def receive(self, arrays, lo=0, hi=1, parts=1, last=True):
        size = self.ready[0].shape[0] // parts
        self.got += [(a, lo * size) for a in arrays]
        if last:
            self.stages.pop(0)

    def items(self):
        arrays = [(self.keep, 0), *self.got]
        parts = 1 << len(self.stages[0][1])
        self.rows //= parts
        return [(arrays, k * self.rows, self.rows, BF16) for k in range(1, parts)]

    def rest(self):
        arrays = [(self.keep, 0), *self.got]
        return arrays, 0, self.rows, BF16


def advance(sums, after):
    groups = [r.items() for r in sums]
    outs = combine([item for group in groups for item in group], after)
    at = 0
    for r, group in zip(sums, groups):
        r.ready = outs[at : at + len(group)]
        at += len(group)
    return [outs[0]]


def unit_of(x):
    mean = jnp.mean(x, axis=-1, keepdims=True)
    c = x - mean
    inv = lax.rsqrt(jnp.mean(c * c, axis=-1, keepdims=True) + EPS)
    return c * inv, inv


def norm_kernel(len_ref, x_ref, dy_ref, g1, b1, g2, b2, a_ref, m_ref, grad_ref, sum_ref):
    u, _ = unit_of(x_ref[...].astype(F32))
    a_ref[...] = (u * g1[...] + b1[...]).astype(BF16)
    m_ref[...] = (u * g2[...] + b2[...]).astype(BF16)
    rows = x_ref.shape[0]
    toks = rows * pl.num_programs(0)
    at = lax.axis_index("seq") * toks + pl.program_id(0) * rows + lax.broadcasted_iota(jnp.int32, (rows, 1), 0)
    text = sum(len_ref[k] for k in range(len_ref.shape[0] - 1))
    grad = dy_ref[...].astype(F32) * jnp.where(at < text, 1.0, 0.0)
    grad_ref[...] = grad.astype(BF16)

    @pl.when(pl.program_id(0) == 0)
    def _():
        sum_ref[...] = jnp.zeros_like(sum_ref)

    sum_ref[...] += jnp.sum(grad, axis=0, keepdims=True)


def norms(lengths, x, dy, g1, b1, g2, b2, after=()):
    rows, d = x.shape
    tr = min(256, rows)
    row = pl.BlockSpec((tr, d), lambda i, *_: (i, 0))
    return call(
        norm_kernel,
        lengths,
        x,
        dy,
        g1,
        b1,
        g2,
        b2,
        scalars=1,
        grid=(rows // tr,),
        in_specs=[row, row] + [whole((1, d))] * 4,
        out_specs=[row, row, row, whole((1, d))],
        out_shape=[jax.ShapeDtypeStruct((rows, d), BF16)] * 3 + [jax.ShapeDtypeStruct((1, d), F32)],
        flops=rows * d * 20, nbytes=rows * d * 10,
        name="norms",
        after=after,
    )


def mlp_kernel(m_ref, grad_ref, win_ref, bin_ref, wout_ref, out_ref, act_ref, dpre_ref, dm_ref, bsum_ref):
    pre = dot(m_ref[...], win_ref[...]) + bin_ref[...]
    cdf = 0.5 * (1.0 + lax.erf(pre * math.sqrt(0.5)))
    act = (pre * cdf).astype(BF16)
    act_ref[...] = act
    d_act = dot_t(grad_ref[...], wout_ref[...])
    slope = cdf + pre * (jnp.exp(-0.5 * pre * pre) * (1.0 / math.sqrt(2.0 * math.pi)))
    d_pre = (d_act * slope).astype(BF16)
    dpre_ref[...] = d_pre
    bsum_ref[...] = jnp.sum(d_pre.astype(F32), axis=0, keepdims=True)

    @pl.when(pl.program_id(0) == 0)
    def _():
        out_ref[...] = jnp.zeros_like(out_ref)
        dm_ref[...] = jnp.zeros_like(dm_ref)

    out_ref[...] += dot(act, wout_ref[...])
    dm_ref[...] += dot_t(d_pre, win_ref[...])


def mlp(m, grad, win, b_in, wout, after=(), sends=(), cid=None):
    rows, d = m.shape
    ff = win.shape[1]
    tf = 1024
    cols = pl.BlockSpec((rows, tf), lambda i: (0, i))
    line = pl.BlockSpec((1, tf), lambda i: (0, i))
    return call(
        mlp_kernel,
        m, grad, win, b_in, wout,
        grid=(ff // tf,),
        in_specs=[
            whole((rows, d)),
            whole((rows, d)),
            pl.BlockSpec((d, tf), lambda i: (0, i)),
            line,
            pl.BlockSpec((tf, d), lambda i: (i, 0)),
        ],
        out_specs=[whole((rows, d)), cols, cols, whole((rows, d)), line],
        out_shape=[
            jax.ShapeDtypeStruct((rows, d), F32),
            jax.ShapeDtypeStruct((rows, ff), BF16),
            jax.ShapeDtypeStruct((rows, ff), BF16),
            jax.ShapeDtypeStruct((rows, d), F32),
            jax.ShapeDtypeStruct((1, ff), F32),
        ],
        flops=8 * rows * d * ff, nbytes=4 * d * ff + 4 * rows * ff + 12 * rows * d, trans=rows * ff * 2,
        name="mlp",
        after=after,
        sends=sends,
        cid=cid,
    )


def turned(left, nat_ref, at):
    n = min(BLOCK, left.shape[1])
    eye = lax.broadcasted_iota(jnp.int32, (n, n), 0) == lax.broadcasted_iota(jnp.int32, (n, n), 1)
    eye = jnp.where(eye, 1.0, 0.0).astype(BF16)
    for c in range(0, left.shape[1], n):
        nat_ref[at + c : at + c + n, :] = dot_t(eye, left[:, c : c + n])


def placed(order, nat_ref, lt_ref):
    blocks = 1 << len(flat_bits(order[0]))
    size = nat_ref.shape[0] // blocks
    for b in range(blocks):
        rows = pl.ds(pl.multiple_of(source(b, *order) * size, size), size)
        lt_ref[b * size : (b + 1) * size, :] = nat_ref[rows, :].astype(BF16)


def wgrad_kernel(stacked, orders, steps, starts, per, *refs):
    n = len(starts)
    n_right = -(-sum(steps) // per)
    n_left = len(refs) - n_right - 3 * n - 2
    lefts, rights, refs = refs[:n_left], refs[n_left : n_left + n_right], refs[n_left + n_right :]
    outs, (nat_ref, lt_ref) = refs[:-2], refs[-2:]
    i = pl.program_id(0)

    @pl.when(i == 0)
    def _():
        row = col = 0
        for left in lefts:
            toks, width = left.shape
            turned(left[...], nat_ref.at[:, col : col + toks], row)
            if stacked:
                col += toks
            else:
                row += width

    for g in range(n):
        send_ref, keep_ref, bsum_ref = outs[3 * g : 3 * g + 3]

        @pl.when(i == starts[g])
        def _():
            placed(orders[g], nat_ref, lt_ref)

        for k, right_ref in enumerate(rights):
            first, end = max(starts[g], k * per), min(starts[g] + steps[g], (k + 1) * per)

            @pl.when((i >= first) & (i < end))
            def _():
                half = keep_ref.shape[0]
                right = right_ref[...]
                send_ref[...] = dot(lt_ref[half:, :], right).astype(BF16)
                keep_ref[...] = dot(lt_ref[:half, :], right).astype(BF16)
                bsum_ref[...] = jnp.sum(right.astype(F32), axis=0, keepdims=True)


def wgrad(groups, lefts, right, tn=512, after=(), sends=(), cid=None):
    rights = right if isinstance(right, list) else [right]
    toks, width = rights[0].shape
    stacked = lefts[0].shape[0] < toks
    per = width // tn
    d = lefts[0].shape[1] if stacked else sum(left.shape[1] for left in lefts)
    steps = [cols // tn for _, cols in groups]
    starts = [sum(steps[:g]) for g in range(len(groups))]
    out_specs, out_shape = [], []
    for (_, cols), first, n in zip(groups, starts, steps):
        at = lambda i, *_, first=first, n=n: (0, jnp.clip(i - first, 0, n - 1))
        out_specs += [pl.BlockSpec((d // 2, tn), at)] * 2 + [pl.BlockSpec((1, tn), at)]
        out_shape += [jax.ShapeDtypeStruct((d // 2, cols), BF16)] * 2 + [jax.ShapeDtypeStruct((1, cols), F32)]
    cols = sum(r.shape[1] for r in rights)
    return call(
        functools.partial(wgrad_kernel, stacked, [o for o, _ in groups], steps, starts, per if len(rights) > 1 else sum(steps)),
        *lefts,
        *rights,
        grid=(sum(steps),),
        in_specs=[
            *[whole(left.shape) for left in lefts],
            *[pl.BlockSpec((toks, tn), lambda i, *_, k=k: (0, jnp.clip(i - k * per, 0, per - 1))) for k in range(len(rights))],
        ],
        out_specs=out_specs,
        scratch=[pltpu.VMEM((d, toks), F32), pltpu.VMEM((d, toks), BF16)],
        out_shape=out_shape,
        flops=2 * toks * d * cols,
        nbytes=2 * toks * (d + cols) + 2 * d * cols,
        name="wgrad",
        after=after,
        sends=sends,
        cid=cid,
    )


def wgrad_rows_kernel(turns_n, orders, groups, *refs):
    n = len(groups)
    (left_ref, right_ref), refs = refs[:2], refs[2:]
    outs, (nat_ref, lt_ref) = refs[: 2 * n], refs[2 * n :]
    i = pl.program_id(0)
    tile = left_ref.shape[1]

    @pl.when(i < turns_n)
    def _():
        turned(left_ref[...], nat_ref, 0)
        lt_ref[pl.ds(pl.multiple_of(i * tile, tile), tile), :] = nat_ref[...].astype(lt_ref.dtype)

    for g, (first, steps, lo, cols) in enumerate(groups):
        send_ref, keep_ref = outs[2 * g : 2 * g + 2]
        rows = send_ref.shape[0]

        @pl.when((i >= first) & (i < first + steps))
        def _():
            total = 1 << len(flat_bits(orders[g][0]))
            blocks = total // steps
            size = rows // blocks
            for b in range(blocks):
                spot = ((i - first) * blocks + b + total // 2) % total
                at = pl.ds(pl.multiple_of(source(spot, *orders[g]) * size, size), size)
                nat_ref[b * size : (b + 1) * size, :] = lt_ref[at, :].astype(F32)
            out = dot(nat_ref[:rows, :].astype(BF16), right_ref[:, lo : lo + cols]).astype(BF16)

            @pl.when(i < first + steps // 2)
            def _():
                send_ref[...] = out

            @pl.when(i >= first + steps // 2)
            def _():
                keep_ref[...] = out


def wgrad_rows(groups, left, right, tile=1024, after=(), sends=(), cid=None):
    toks, d = right.shape
    rows = left.shape[1]
    n = rows // tile
    half = n // 2
    orders = [o for o, _ in groups]
    kind = BF16 if (rows >> len(flat_bits(orders[0][0]))) % 16 == 0 else F32
    cuts, out_specs, out_shape, lo = [], [], [], 0
    for g, (_, cols) in enumerate(groups):
        first = n * (g + 1)
        cuts.append((first, n, lo, cols))
        lo += cols
        out_specs.append(pl.BlockSpec((tile, cols), lambda i, *_, first=first: (jnp.clip(i - first, 0, half - 1), 0)))
        out_specs.append(pl.BlockSpec((tile, cols), lambda i, *_, first=first: (jnp.clip(i - first - half, 0, half - 1), 0)))
        out_shape += [jax.ShapeDtypeStruct((rows // 2, cols), BF16)] * 2
    return call(
        functools.partial(wgrad_rows_kernel, n, orders, cuts),
        left,
        right,
        grid=(n * (1 + len(groups)),),
        in_specs=[
            pl.BlockSpec((toks, tile), lambda i, *_: (0, jnp.minimum(i, n - 1))),
            pl.BlockSpec((toks, d), lambda i, *_: (0, 0)),
        ],
        out_specs=out_specs,
        scratch=[pltpu.VMEM((tile, toks), F32), pltpu.VMEM((rows, toks), kind)],
        out_shape=out_shape,
        flops=2 * toks * rows * d,
        nbytes=2 * (rows * (d + toks) + toks * d),
        name="wgrad_rows",
        after=after,
        sends=sends,
        cid=cid,
    )


def document_start(len_ref, at):
    begin, end = jnp.zeros_like(at), 0
    for k in range(len_ref.shape[0]):
        end = end + len_ref[k]
        begin = jnp.where(at >= end, end, begin)
    return begin


def d_ctx_kernel(halos, nseq, len_ref, a_ref, w_ref, out_ref, cos_ref, sin_ref, start_ref):
    out_ref[...] = dot_t(a_ref[...], w_ref[...]).astype(BF16)
    toks, rows = a_ref.shape[0], cos_ref.shape[0]
    me = lax.axis_index("seq")
    base = (me - halos) * toks
    at = base + pl.program_id(0) * rows + lax.broadcasted_iota(jnp.int32, (rows, LANES), 0)
    lane = lane_ids(rows) % HEAD
    half = ROT // 2
    freq = jnp.zeros((rows, LANES), F32)
    for k in range(half):
        freq = jnp.where(lane % half == k, 10000.0 ** (-(2.0 * k) / ROT), freq)
    angle = (at - document_start(len_ref, at)).astype(F32) * freq
    cos_ref[...] = jnp.where(lane < ROT, jnp.cos(angle), 1.0)
    sin = jnp.sin(angle)
    sin_ref[...] = jnp.where(lane < half, -sin, jnp.where(lane < ROT, sin, 0.0))
    own = me * toks + lax.broadcasted_iota(jnp.int32, (1, toks), 1)
    start_ref[...] = document_start(len_ref, own) - base


def d_context(lengths, grad, w, halos, nseq, tn=256, after=(), sends=(), cid=None):
    rows, d = grad.shape
    win = rows * (halos + 1)
    steps = d // tn
    table = pl.BlockSpec((win // steps, LANES), lambda i, *_: (i, 0))
    return call(
        functools.partial(d_ctx_kernel, halos, nseq),
        lengths,
        grad,
        w,
        scalars=1,
        grid=(steps,),
        in_specs=[whole((rows, d)), pl.BlockSpec((tn, d), lambda i, *_: (i, 0))],
        out_specs=[pl.BlockSpec((rows, tn), lambda i, *_: (0, i)), table, table, whole((1, rows))],
        out_shape=[
            jax.ShapeDtypeStruct((rows, d), BF16),
            jax.ShapeDtypeStruct((win, LANES), F32),
            jax.ShapeDtypeStruct((win, LANES), F32),
            jax.ShapeDtypeStruct((1, rows), jnp.int32),
        ],
        flops=2 * rows * d * d,
        nbytes=2 * d * (2 * rows + d),
        name="d_ctx",
        after=after,
        sends=sends,
        cid=cid,
    )


def lane_ids(rows):
    return lax.broadcasted_iota(jnp.int32, (rows, LANES), 1)


def turns():
    frm = lax.broadcasted_iota(jnp.int32, (LANES, LANES), 0)
    to = lax.broadcasted_iota(jnp.int32, (LANES, LANES), 1)
    half = ROT // 2
    within = frm % HEAD
    partner = jnp.where(within < half, frm + half, frm - half)
    rotated = within < ROT
    turned = (frm + HEAD) % LANES
    one = lambda hit: jnp.where(hit, 1.0, 0.0).astype(BF16)
    return one(turned == to), one(rotated & (partner == to)), one(rotated & ((partner + HEAD) % LANES == to))


def split(x):
    high = x.astype(BF16)
    return jnp.concatenate([high, (x - high.astype(F32)).astype(BF16)], axis=1)


def qkv_kernel(n, *refs):
    a_refs, (w_ref, bias_ref, cos_ref, sin_ref, q_ref, k_ref, v_ref) = refs[:n], refs[n:]
    turn, swap, swap_turn = turns()
    k_moves = jnp.concatenate([turn, swap_turn], axis=1)
    k_moves = jnp.concatenate([k_moves, k_moves], axis=0)
    q_moves = jnp.concatenate([swap, swap], axis=0)
    r = 0
    for a_ref in a_refs:
        rows = slice(r, r + a_ref.shape[0])
        r += a_ref.shape[0]
        first = lane_ids(a_ref.shape[0]) < HEAD
        packed = dot(a_ref[...], w_ref[...]) + bias_ref[...]
        cos, sin = cos_ref[rows, :], sin_ref[rows, :]
        for g in range(w_ref.shape[1] // PAIR):
            c = g * PAIR
            lanes = slice(g * LANES, (g + 1) * LANES)
            pa, pb, pc = packed[:, c : c + LANES], packed[:, c + LANES : c + 2 * LANES], packed[:, c + 2 * LANES : c + PAIR]
            both = dot(split(jnp.where(first, pc, pa)), k_moves)
            k_ref[rows, lanes] = (both[:, :LANES] * cos + both[:, LANES:] * sin).astype(BF16)
            v_ref[rows, lanes] = jnp.where(first, pb, pc).astype(BF16)
            if a_ref is a_refs[-1]:
                q = jnp.where(first, pa, pb)
                q_ref[:, lanes] = (q * cos + dot(split(q), q_moves) * sin).astype(BF16)


def qkv(pieces, w, bias, cos, sin, group=4, after=()):
    toks, d = pieces[-1].shape
    win = sum(p.shape[0] for p in pieces)
    cols = w.shape[1]
    out = pl.BlockSpec((win, group * LANES), lambda i: (0, i))
    return call(
        functools.partial(qkv_kernel, len(pieces)),
        *pieces, w, bias, cos, sin,
        grid=(cols // PAIR // group,),
        in_specs=[
            *[whole(p.shape) for p in pieces],
            pl.BlockSpec((d, group * PAIR), lambda i: (0, i)),
            pl.BlockSpec((1, group * PAIR), lambda i: (0, i)),
            whole((win, LANES)),
            whole((win, LANES)),
        ],
        out_specs=[pl.BlockSpec((toks, group * LANES), lambda i: (0, i)), out, out],
        out_shape=[jax.ShapeDtypeStruct((toks, cols // 3), BF16)] + [jax.ShapeDtypeStruct((win, cols // 3), BF16)] * 2,
        flops=2 * win * d * cols, nbytes=8 * win * d + 2 * d * cols,
        name="qkv",
        after=after,
    )


GROUP = 2
QB = 256


def attention_kernel(
    toks, win, start_ref, q_ref, k_ref, v_ref, do_ref, cos_ref, sin_ref, ctx_ref, dp_ref,
    k2, v2, kt, vt, s_ref, e_ref, dq_acc, dk_acc, dv_acc,
):
    nk = win // BLOCK
    halo = win - toks
    first = lane_ids(BLOCK) < HEAD
    first_q = lane_ids(QB) < HEAD
    zero = jnp.zeros((BLOCK, LANES), BF16)
    zero_q = jnp.zeros((QB, LANES), BF16)
    top = lax.broadcasted_iota(jnp.int32, (LANES, QB), 0) < HEAD
    groups = range(GROUP)
    lanes = [slice(g * LANES, (g + 1) * LANES) for g in groups]
    eye = lax.broadcasted_iota(jnp.int32, (LANES, LANES), 0) == lax.broadcasted_iota(jnp.int32, (LANES, LANES), 1)
    upper = lax.broadcasted_iota(jnp.int32, (LANES, LANES), 0) < HEAD
    eye0 = jnp.where(eye & upper, 1.0, 0.0).astype(BF16)
    eye1 = jnp.where(eye & ~upper, 1.0, 0.0).astype(BF16)

    def prepare(j, _):
        rows = pl.ds(pl.multiple_of(j * BLOCK, BLOCK), BLOCK)
        for g in groups:
            for src, two, tr in ((k_ref, k2, kt), (v_ref, v2, vt)):
                x = src[rows, lanes[g]]
                two[g, j, :BLOCK, :] = jnp.where(first, x, zero)
                two[g, j, BLOCK:, :] = jnp.where(first, zero, x)
                tr[g, j, :, :BLOCK] = dot_t(eye0, x).astype(BF16)
                tr[g, j, :, BLOCK:] = dot_t(eye1, x).astype(BF16)
        return 0

    lax.fori_loop(0, nk, prepare, 0)
    dk_acc[...] = jnp.zeros_like(dk_acc)
    dv_acc[...] = jnp.zeros_like(dv_acc)
    scale = HEAD**-0.5
    for i in range(toks // QB):
        rows = slice(i * QB, (i + 1) * QB)
        last = (halo + (i + 1) * QB) // BLOCK
        low = max(halo + i * QB - DOC_MOST + 1, 0) // BLOCK
        qs = [q_ref[rows, lanes[g]].astype(F32) * scale for g in groups]
        qts = [q.T.astype(BF16) for q in qs]
        qs = [q.astype(BF16) for q in qs]
        q2 = [jnp.concatenate([jnp.where(first_q, q, zero_q), jnp.where(first_q, zero_q, q)], axis=0) for q in qs]
        start = start_ref[:, rows]
        q_at = halo + i * QB + lax.broadcasted_iota(jnp.int32, (1, QB), 1)

        def scores(j, peaks):
            at = j * BLOCK + lax.broadcasted_iota(jnp.int32, (BLOCK, QB), 0)
            ok = (at >= start) & (at <= q_at)
            out = []
            for g in groups:
                s = dot(k2[g, j], qts[g])
                s0 = jnp.where(ok, s[:BLOCK], NEG)
                s1 = jnp.where(ok, s[BLOCK:], NEG)
                s_ref[g, j, :BLOCK, :] = s0
                s_ref[g, j, BLOCK:, :] = s1
                out.append(jnp.maximum(peaks[2 * g], jnp.max(s0, axis=0, keepdims=True)))
                out.append(jnp.maximum(peaks[2 * g + 1], jnp.max(s1, axis=0, keepdims=True)))
            return tuple(out)

        floor = jnp.full((1, QB), NEG, F32)
        peaks = lax.fori_loop(low, last, scores, (floor,) * (2 * GROUP), unroll=True)

        def weigh(j, carry):
            out = []
            for g in groups:
                t0, t1, acc = carry[3 * g : 3 * g + 3]
                e0 = jnp.exp(s_ref[g, j, :BLOCK, :] - peaks[2 * g])
                e1 = jnp.exp(s_ref[g, j, BLOCK:, :] - peaks[2 * g + 1])
                b0, b1 = e0.astype(BF16), e1.astype(BF16)
                e_ref[g, j, :BLOCK, :] = b0
                e_ref[g, j, BLOCK:, :] = b1
                acc = acc + dot(vt[g, j], jnp.concatenate([b0, b1], axis=0))
                out += [t0 + jnp.sum(e0, axis=0, keepdims=True), t1 + jnp.sum(e1, axis=0, keepdims=True), acc]
            return tuple(out)

        none = jnp.zeros((1, QB), F32)
        sums = lax.fori_loop(low, last, weigh, (none, none, jnp.zeros((LANES, QB), F32)) * GROUP, unroll=True)
        do_l, do2, d0, d1 = [], [], [], []
        for g in groups:
            t0, t1, acc = sums[3 * g : 3 * g + 3]
            share = jnp.where(top, 1.0 / t0, 1.0 / t1)
            ctx_t = acc * share
            ctx_ref[rows, lanes[g]] = ctx_t.T.astype(BF16)
            do_t = do_ref[rows, lanes[g]].astype(F32).T * share
            both = do_t * ctx_t
            d0.append(jnp.sum(both[:HEAD], axis=0, keepdims=True))
            d1.append(jnp.sum(both[HEAD:], axis=0, keepdims=True))
            do = do_t.T.astype(BF16)
            do_l.append(do_t.astype(BF16))
            do2.append(jnp.concatenate([jnp.where(first_q, do, zero_q), jnp.where(first_q, zero_q, do)], axis=0))

        def back(j, dqs):
            at = pl.ds(pl.multiple_of(j * BLOCK, BLOCK), BLOCK)
            out = []
            for g in groups:
                dp = dot(v2[g, j], do_l[g])
                e0, e1 = e_ref[g, j, :BLOCK, :], e_ref[g, j, BLOCK:, :]
                ds0 = (e0.astype(F32) * (dp[:BLOCK] - d0[g])).astype(BF16)
                ds1 = (e1.astype(F32) * (dp[BLOCK:] - d1[g])).astype(BF16)
                dv_acc[at, lanes[g]] += dot(jnp.concatenate([e0, e1], axis=1), do2[g])
                dk_acc[at, lanes[g]] += dot(jnp.concatenate([ds0, ds1], axis=1), q2[g])
                out.append(dqs[g] + dot(kt[g, j], jnp.concatenate([ds0, ds1], axis=0)))
            return tuple(out)

        dqs = lax.fori_loop(low, last, back, (jnp.zeros((LANES, QB), F32),) * GROUP, unroll=True)
        for g in groups:
            dq_acc[rows, lanes[g]] = dqs[g].T * scale

    turn, swap, swap_turn = turns()
    for j in range(nk):
        rows = slice(j * BLOCK, (j + 1) * BLOCK)
        cos, sin = cos_ref[rows, :], sin_ref[rows, :]
        for g in groups:
            dk = dk_acc[rows, lanes[g]].astype(BF16)
            dk = dot(dk, turn) * cos - dot(dk, swap_turn) * sin
            dv = dv_acc[rows, lanes[g]]
            if j * BLOCK >= halo:
                own = slice(j * BLOCK - halo, (j + 1) * BLOCK - halo)
                dq = dq_acc[own, lanes[g]]
                dq = dq * cos - dot(dq.astype(BF16), swap) * sin
            else:
                dq = jnp.zeros_like(dk)
            c = g * PAIR
            dp_ref[rows, c : c + LANES] = jnp.where(first, dq, dk).astype(BF16)
            dp_ref[rows, c + LANES : c + 2 * LANES] = jnp.where(first, dv, dq).astype(BF16)
            dp_ref[rows, c + 2 * LANES : c + PAIR] = jnp.where(first, dk, dv).astype(BF16)


def attention(start, q, k, v, d_ctx, cos, sin, pair, pairs, after=(), sends=(), cid=None):
    win, d = k.shape
    toks = d_ctx.shape[0]
    nk = win // BLOCK
    width = GROUP * LANES
    at = pair // GROUP
    own = pl.BlockSpec((toks, width), lambda i: (0, at + i))
    every = pl.BlockSpec((win, width), lambda i: (0, at + i))
    out = pairs * LANES
    return call(
        functools.partial(attention_kernel, toks, win),
        start,
        q,
        k,
        v,
        d_ctx,
        cos,
        sin,
        grid=(pairs // GROUP,),
        in_specs=[whole((1, toks)), own, every, every, own, whole((win, LANES)), whole((win, LANES))],
        out_specs=[pl.BlockSpec((toks, width), lambda i: (0, i)), pl.BlockSpec((win, GROUP * PAIR), lambda i: (0, i))],
        out_shape=[jax.ShapeDtypeStruct((toks, out), BF16), jax.ShapeDtypeStruct((win, 3 * out), BF16)],
        scratch=[
            pltpu.VMEM((GROUP, nk, 2 * BLOCK, LANES), BF16),
            pltpu.VMEM((GROUP, nk, 2 * BLOCK, LANES), BF16),
            pltpu.VMEM((GROUP, nk, LANES, 2 * BLOCK), BF16),
            pltpu.VMEM((GROUP, nk, LANES, 2 * BLOCK), BF16),
            pltpu.VMEM((GROUP, nk, 2 * BLOCK, QB), F32),
            pltpu.VMEM((GROUP, nk, 2 * BLOCK, QB), BF16),
            pltpu.VMEM((toks, width), F32),
            pltpu.VMEM((win, width), F32),
            pltpu.VMEM((win, width), F32),
        ],
        flops=pairs * toks * DOC_MOST * 4 * 6 * LANES,
        nbytes=14 * win * out,
        trans=pairs * 2 * toks * DOC_MOST,
        name="attention",
        after=after,
        sends=sends,
        cid=cid,
    )


def tail_kernel(cfg, *refs):
    ndp, nseq, halos, n_pieces, n_dp, n_ctx, joins, last_c = cfg
    refs = list(refs)
    take = lambda n: [refs.pop(0) for _ in range(n)]
    dp_rows, (w_ref,) = take(n_dp), take(1)
    n_late = n_dp - 2 + n_pieces + n_ctx + 3
    late = take(n_late)
    mlp_ref, wd_ref, bias_ref, g1, g2 = take(5)
    gsum_ref, qsum_ref, isum_ref = take(3)
    left_q, own_q = take(2)
    hidden_ref, grad_in_ref, small = take(3)
    owns = take(3)
    last_gots = [take(len(fan(last_c)) - 1) for _ in owns]
    nat, lt, own_acc, far, far_got = take(5)
    group_bufs = [take(6), take(6), [None, own_q.at[0], None, left_q, *take(2)]]
    bsum_ref, small_got = take(2)
    held = take(n_late)
    send_sem, recv_sem, late_sem = refs
    loads = [pltpu.make_async_copy(a, b, late_sem.at[k]) for k, (a, b) in enumerate(zip(late, held))]
    held = list(held)
    take_held = lambda n: [held.pop(0) for _ in range(n)]
    dp_cols, pieces, ctxs = take_held(n_dp - 2), take_held(n_pieces), take_held(n_ctx)
    grad_ref, x_ref, d_mlp_ref = held
    first_loads = n_dp - 2 + n_pieces
    toks, d = x_ref.shape
    me_dp, me_seq = lax.axis_index("dp"), lax.axis_index("seq")
    dp_bits = stage_bits(ndp)
    core, cross = fan(dp_bits[:1]), fan(dp_bits[1:])
    across, everyone = fan(last_c), fan(dp_bits)

    def device(axis, offset):
        return (me_dp ^ offset, me_seq) if axis == "dp" else (me_dp, me_seq ^ offset)

    behind = (me_dp, lax.rem(me_seq + nseq - 1, nseq))
    ahead = (me_dp, lax.rem(me_seq + 1, nseq))
    names = {}

    def copy(name, src, dst, to):
        k = names.setdefault(name, len(names))
        return pltpu.make_async_remote_copy(
            src_ref=src,
            dst_ref=dst,
            send_sem=send_sem.at[k],
            recv_sem=recv_sem.at[k],
            device_id=to,
            device_id_type=pl.DeviceIdType.MESH,
        )

    half = toks // 2

    def far_copy(k, c):
        rows = pl.ds(c * half, half)
        return copy(("far", k, c), far.at[k, rows], far_got.at[k, rows], behind)


    def first(n):
        send, _, got, *_ = group_bufs[n]
        return copy(("core", n), send, got, device("dp", core[1]))

    def second(n):
        _, _, _, out, into, _ = group_bufs[n]
        start = 1 if n < 2 else 0
        return [copy(("cross", n, k), out.at[k - start], into.at[k - 1], device("dp", cross[k])) for k in range(1, len(cross))]

    def third(n):
        out, got = group_bufs[n][5], last_gots[(n + 1) % 3]
        return [copy(("across", n, k), out.at[k - 1], got[k - 1], device("seq", across[k])) for k in range(1, len(across))]

    def to_second(n):
        _, keep, got, out, _, _ = group_bufs[n]
        first(n).wait()
        rows = out.shape[1]
        for k, c in enumerate(second(n), 1):
            at = slice(k * rows, (k + 1) * rows)
            out[k - 1] = (keep[at, :].astype(F32) + got[at, :].astype(F32)).astype(BF16)
            c.start()

    def to_third(n):
        _, keep, got, _, into, out = group_bufs[n]
        for c in second(n):
            c.wait()
        own = owns[(n + 1) % 3]
        rows = own.shape[0]
        copies = third(n)
        for k in reversed(range(len(across))):
            at = slice(k * rows, (k + 1) * rows)
            total = keep[at, :].astype(F32)
            if got is not None:
                total += got[at, :].astype(F32)
            for b in range(len(cross) - 1):
                total += into[b, at, :].astype(F32)
            if k:
                out[k - 1] = total.astype(out.dtype)
                copies[k - 1].start()
            else:
                own[...] = total

    def pass_on(k, c):
        far_copy(k - 1, c).wait()
        rows = pl.ds(c * half, half)
        far[k, rows] = (far[k, rows].astype(F32) + far_got[k - 1, rows].astype(F32)).astype(BF16)
        far_copy(k, c).start()

    def back(rows=slice(None)):
        total, at = None, 0
        for a_ref in dp_rows:
            n = a_ref.shape[1]
            term = dot_t(a_ref[rows, :], w_ref[:, at : at + n])
            total, at = term if total is None else total + term, at + n
        return total

    step = [0]
    pid = pl.program_id(0)

    def phase(fn):
        pl.when(pid == step[0])(fn)
        step[0] += 1

    for k in range(halos):

        def do_far(k=k):
            if k == 0:
                offsets = [("dp", o) for o in everyone[1:]] + [("seq", o) for o in across[1:]]
                greet([device(*o) for o in offsets] + [behind, ahead])
                for c in loads + second(2):
                    c.start()
            for c in range(2):
                rows = slice(c * half, (c + 1) * half)
                far[k, rows] = back(rows).astype(BF16)
                if k == 0:
                    far_copy(0, c).start()

        phase(do_far)

    def do_columns():
        for c in loads[:first_loads]:
            c.wait()
        col = 0
        for left in pieces:
            n = left.shape[0]
            turned(left[...], nat.at[:, :n], 0)
            placed((short_order(ndp, nseq), nseq), nat.at[:, :n], lt.at[:, col : col + n])
            col += n
        send, keep = group_bufs[0][:2]
        half, at = keep.shape[0], 0
        for right_ref in dp_cols:
            right = right_ref[...]
            n = right.shape[1]
            send[:, at : at + n] = dot(lt[half:, :], right).astype(BF16)
            keep[:, at : at + n] = dot(lt[:half, :], right).astype(BF16)
            bsum_ref[:, at : at + n] = jnp.sum(right.astype(F32), axis=0, keepdims=True)
            at += n
        first(0).start()
        if halos > 1:
            pass_on(1, 0)

    phase(do_columns)

    def do_dense():
        for c in loads[first_loads:]:
            c.wait()
        at = 0
        for ctx in ctxs:
            turned(ctx[...], nat, at)
            at += ctx.shape[1]
        placed((short_order(ndp, nseq), nseq), nat, lt.at[:, :toks])
        send, keep = group_bufs[1][:2]
        half = keep.shape[0]
        send[...] = dot(lt[half:, :toks], grad_ref[...]).astype(BF16)
        first(1).start()
        keep[...] = dot(lt[:half, :toks], grad_ref[...]).astype(BF16)
        to_second(0)

    phase(do_dense)

    def do_own():
        own_acc[...] = back()
        if halos > 1:
            pass_on(1, 1)
        to_second(1)
        to_third(2)

    phase(do_own)
    for t in range(joins):

        def do_join(t=t):
            cols = hidden_ref.shape[1]
            at = slice(t * cols, (t + 1) * cols)
            total, row = x_ref[:, at].astype(F32) + mlp_ref[...] + bias_ref[:, at], 0
            for ctx in ctxs:
                n = ctx.shape[1]
                total += dot(ctx[...], wd_ref[row : row + n, :])
                row += n
            hidden_ref[...] = total.astype(BF16)

        phase(do_join)

    def do_rest():
        for k in range(2, halos):
            for c in range(2):
                pass_on(k, c)
        to_third(0)
        to_third(1)
        small[...] = jnp.zeros_like(small)
        rows = min(128, half)
        for r in range(0, toks, rows):
            if r % half == 0:
                far_copy(halos - 1, r // half).wait()
            at = slice(r, r + rows)
            u, inv = unit_of(x_ref[at, :].astype(F32))
            d1 = own_acc[at, :] + far_got[halos - 1, at, :].astype(F32)
            d2 = d_mlp_ref[at, :]
            e = d1 * g1[...] + d2 * g2[...]
            dx = inv * (e - jnp.mean(e, axis=-1, keepdims=True) - u * jnp.mean(e * u, axis=-1, keepdims=True))
            grad_in_ref[at, :] = grad_ref[at, :].astype(F32) + dx
            for k, v in enumerate((d1 * u, d1, d2 * u, d2)):
                small[k : k + 1, :] += jnp.sum(v, axis=0, keepdims=True)
        small[4:5, :] = gsum_ref[...]
        row = 5
        for parts in ((qsum_ref, bsum_ref), (isum_ref,)):
            flat = jnp.concatenate([p[...] for p in parts], axis=1)
            for c in range(0, flat.shape[1], d):
                small[row : row + 1, :] = flat[:, c : c + d]
                row += 1
        used = 0
        for axis, offsets in (("dp", everyone), ("seq", across)):
            copies = []
            for o in offsets[1:]:
                copies.append(copy(("small", used), small, small_got.at[used], device(axis, o)))
                copies[-1].start()
                used += 1
            for c in copies:
                c.wait()
            total = small[...]
            for k in range(used - len(copies), used):
                total += small_got[k]
            small[...] = total
        for c in third(0) + third(1) + third(2):
            c.wait()

    phase(do_rest)


def tail(dps, w, pieces, ctxs, grad, x, mlp_out, d_mlp, w_d, bias, g1, g2, sums, left_q, ndp, nseq, halos, after=()):
    toks, d = x.shape
    depth = w.shape[1]
    joins = 4
    own_at = halos + 2
    dp_bits, seq_bits = stage_bits(ndp), stage_bits(nseq)
    cross, across = 1 << len(dp_bits[1:]), 1 << len(seq_bits)
    tile = d // joins
    once = lambda shape: pl.BlockSpec(shape, lambda i: (0,) * len(shape), pipeline_mode=pl.Buffered(1))
    piece_at = lambda i: (jnp.where(i < halos, i, jnp.where(i < own_at, halos - 1, halos)), 0)
    join_at = lambda i: (0, jnp.clip(i - own_at - 1, 0, joins - 1))
    hbm = pl.BlockSpec(memory_space=pl.ANY)
    cut_up = lambda a, n: a.reshape(n, a.shape[0] // n, a.shape[1])
    left_q = cut_up(left_q, cross)
    late = [*dps[2:], *pieces, *ctxs, grad, x, d_mlp]
    ins = [*dps, w, *late, mlp_out, w_d, bias, g1, g2, *sums, left_q, left_q]
    in_specs = (
        [pl.BlockSpec((toks, a.shape[1]), piece_at) for a in dps]
        + [once(w.shape)]
        + [hbm] * len(late)
        + [pl.BlockSpec((toks, tile), join_at), pl.BlockSpec((d, tile), join_at)]
        + [once((1, d))] * 3
        + [once(v.shape) for v in sums]
        + [hbm, once((1, *left_q.shape[1:]))]
    )
    rest = sum(a.shape[1] for a in dps[2:])
    lines = 4 + sum(v.shape[1] for v in sums) // d + 1
    lines += -lines % 8
    widths = [left_q.shape[2], rest, d]
    left = d // 2 // cross // across
    kind = BF16 if left % 16 == 0 else F32
    out_shape = [
        jax.ShapeDtypeStruct((toks, d), BF16),
        jax.ShapeDtypeStruct((toks, d), F32),
        jax.ShapeDtypeStruct((lines, d), F32),
        *[jax.ShapeDtypeStruct((left, n), F32) for n in widths],
        *[jax.ShapeDtypeStruct((left, n), kind) for n in widths for _ in range(across - 1)],
    ]
    fixed = lambda shape: pl.BlockSpec(shape, lambda i: (0,) * len(shape))
    out_specs = (
        [pl.BlockSpec((toks, tile), join_at), fixed((toks, d))]
        + [fixed((lines, d))]
        + [fixed((left, n)) for n in widths]
        + [hbm] * (len(widths) * (across - 1))
    )
    scratch = [
        pltpu.VMEM((d, toks), F32),
        pltpu.VMEM((d, toks * (halos + 1)), BF16),
        pltpu.VMEM((toks, d), F32),
        pltpu.VMEM((halos, toks, d), BF16),
        pltpu.VMEM((halos, toks, d), BF16),
    ]
    for n in widths[1:]:
        scratch += [pltpu.VMEM((d // 2, n), BF16)] * 3
        scratch += [pltpu.VMEM((cross - 1, d // 2 // cross, n), BF16)] * 2
        scratch += [pltpu.VMEM((across - 1, left, n), kind)]
    scratch += [pltpu.VMEM((cross - 1, *left_q.shape[1:]), BF16), pltpu.VMEM((across - 1, left, widths[0]), kind)]
    scratch += [pltpu.VMEM((1, rest), F32), pltpu.VMEM((ndp - 1 + across - 1, lines, d), F32)]
    scratch += [pltpu.VMEM(a.shape, a.dtype) for a in late]
    copies = 2 * halos + 3 * (1 + cross - 1 + across - 1) + (ndp - 1 + across - 1)
    scratch += [pltpu.SemaphoreType.DMA((copies,))] * 2 + [pltpu.SemaphoreType.DMA((len(late),))]
    cfg = (ndp, nseq, halos, len(pieces), len(dps), len(ctxs), joins, seq_bits)
    n = len(ins)

    def body(*refs):
        tail_kernel(cfg, *refs[:n], *refs[n + len(after) :])

    outs = pl.pallas_call(
        body,
        grid_spec=pltpu.PrefetchScalarGridSpec(
            num_scalar_prefetch=0,
            grid=(own_at + 1 + joins + 1,),
            in_specs=in_specs + [hbm] * len(after),
            out_specs=out_specs,
            scratch_shapes=scratch,
        ),
        out_shape=out_shape,
        compiler_params=pltpu.CompilerParams(vmem_limit_bytes=63 * MIB, collective_id=1, has_side_effects=True),
        cost_estimate=pl.CostEstimate(flops=20 * toks * d * depth, bytes_accessed=40 * toks * d, transcendentals=0),
        name="tail",
    )(*ins, *after)
    outs = list(outs)
    main, own, outs = outs[:3], outs[3:6], outs[6:]
    terms = []
    for a in own:
        terms.append(([(v, 0) for v in (a, *outs[: across - 1])], 0, left, F32))
        outs = outs[across - 1 :]
    return main, terms


def shards(
    hidden_in,
    doc_lengths,
    ln1_gain,
    ln1_bias,
    ln2_gain,
    ln2_bias,
    qkv_weight,
    qkv_bias,
    dense_weight,
    dense_bias,
    fc_in_weight,
    fc_in_bias,
    fc_out_weight,
    fc_out_bias,
    out_grad,
):
    _, toks, d = hidden_in.shape
    ff = fc_in_weight.shape[1]
    ndp, nseq = lax.axis_size("dp"), lax.axis_size("seq")
    ndev = ndp * nseq
    sizes = {"dp": ndp, "seq": nseq}
    me_dp, me_seq = lax.axis_index("dp"), lax.axis_index("seq")
    row = lambda v: v.reshape(1, -1)

    halos = max(min(-(-(DOC_MOST - 1) // toks), nseq - 1), 1)
    lengths = doc_lengths.reshape(-1)
    x = hidden_in.reshape(toks, d)
    a_own, m_own, grad, grad_sum = norms(
        lengths, x, out_grad.reshape(toks, d), row(ln1_gain), row(ln1_bias), row(ln2_gain), row(ln2_bias)
    )

    ahead = [(i, (i + 1) % nseq) for i in range(nseq)]
    on = ("ring", 1, nseq)
    fine = toks // 4 % LANES == 0
    cut = toks * 3 // 4 if fine else toks
    mlp_out, act, d_pre, d_mlp, b_in_sum, near = mlp(
        m_own, grad, fc_in_weight, row(fc_in_bias), fc_out_weight, sends=[(a_own, 0, cut, on)], cid=2
    )
    near, far = [near], []
    two = halos > 1

    orders = [stage_order(ndp, nseq, kind) for kind in range(3)]
    srcs = [(o, nseq) for o in orders]
    in_cut, out_cut = ff * 5 // 8, d // 4
    sends = [(a_own, cut, toks - cut, on)] if fine else []
    if two:
        sends.append((near[0], 0, toks // 4 if fine else toks // 2, on))
    s0, k0, line, s1, k1, _, *got = wgrad(
        [(srcs[0], in_cut), (srcs[2], ff - in_cut)], [m_own], d_pre, sends=sends, cid=3 if sends else None
    )
    near += got[:1] if fine else []
    far += got[-1:] if two else []
    early = [Halving(s0, k0, orders[0], sizes), Halving(s1, k1, orders[2], sizes)]
    s2, k2, s3, k3, *got = wgrad_rows(
        [(srcs[2], out_cut), (srcs[1], d - out_cut)],
        act,
        grad,
        after=[line],
        sends=[send for r in early for send in r.sends()]
        + ([(near[0], far[0].shape[0], toks // 2, on)] if two else []),
        cid=4,
    )
    for r in early:
        r.receive([got.pop(0)])
    far += got
    late = [Halving(s2, k2, orders[2], sizes), Halving(s3, k3, orders[1], sizes)]
    fc = early + late
    d_ctx, cos, sin, start, *got = d_context(
        lengths,
        grad,
        dense_weight,
        halos,
        nseq,
        sends=[send for r in late for send in r.sends()] + ([(near[1], 0, toks - cut, on)] if two and fine else []),
        cid=5,
    )
    for r in late:
        r.receive([got.pop(0)])
    far += got
    pieces = [*far, *near, a_own]
    for k in range(2, halos):
        far = [lax.ppermute(jnp.concatenate(far, axis=0), "seq", ahead)]
        pieces = far + pieces
    last = advance(fc, [d_ctx])
    for r in fc:
        r.permute()
    q, k, v = qkv(pieces, qkv_weight, row(qkv_bias), cos, sin, after=last)

    order_c = short_order(ndp, nseq)
    src_c = (order_c, nseq)
    pairs = d // LANES
    quarter = pairs // 4

    def part(at, n, sums=(), **more):
        sends = [send for r in sums for send in r.sends()]
        ctx, dp, *got = attention(
            start, q, k, v, d_ctx, cos, sin, at * quarter, n * quarter, sends=sends, cid=6 + at if sends else None, **more
        )
        for r in sums:
            r.receive([got.pop(0) for _ in r.targets()])
        return ctx, dp

    ctx_a, dp_a = part(0, 1)
    advance(fc, [ctx_a])
    ctx_b, dp_b = part(1, 1, fc)
    advance(fc, [ctx_b])
    qa_send, qa_keep, b_qkv_a, *got = wgrad(
        [(src_c, dp_a.shape[1] * 2)], pieces, [dp_a, dp_b], tn=dp_a.shape[1], sends=[send for r in fc for send in r.sends()], cid=10
    )
    for r in fc:
        r.receive([got.pop(0) for _ in r.targets()])
    r_qa = Halving(qa_send, qa_keep, order_c, sizes)
    last = advance(fc, [b_qkv_a])
    while len(fc[0].stages) > 1:
        for r in fc:
            r.permute()
        last = advance(fc, last)
    ctx_c, dp_c = part(2, 2, [*fc, r_qa])
    left_q, g_in, g_out = combine([r_qa.rest(), *[(*r.rest()[:3], F32) for r in fc]], [ctx_c], joined=(2, 4))
    main, terms = tail(
        [dp_a, dp_b, dp_c],
        qkv_weight,
        pieces,
        [ctx_a, ctx_b, ctx_c],
        grad,
        x,
        mlp_out,
        d_mlp,
        dense_weight,
        row(dense_bias + fc_out_bias),
        row(ln1_gain),
        row(ln2_gain),
        [grad_sum, b_qkv_a, b_in_sum],
        left_q,
        ndp,
        nseq,
        halos,
    )
    hidden_out, grad_in, small = main
    hidden_out, g_qkv, g_dense, *parts = last_sums(terms, small, hidden_out, ff, ndev, nseq)
    o1g, o1b, o2g, o2b, o_db, o_ob, o_qb, o_ib = (v.reshape(-1) for v in parts)
    return (
        hidden_out.reshape(hidden_in.shape),
        grad_in.reshape(hidden_in.shape),
        o1g,
        o1b,
        o2g,
        o2b,
        g_qkv,
        o_qb,
        g_dense,
        o_db,
        g_in,
        o_ib,
        g_out,
        o_ob,
    )


def solution(mesh):
    both = P(("dp", "seq"))
    rows = P(("dp", "seq"), None)
    toks = P("dp", "seq", None)
    return jax.shard_map(
        shards,
        mesh=mesh,
        in_specs=(toks, P("dp", None)) + (P(),) * 12 + (toks,),
        out_specs=(toks, toks, both, both, both, both, rows, both, rows, both, rows, both, rows, both),
        check_vma=False,
    )
```

```python
import functools
import math

import jax
import jax.numpy as jnp
from jax import lax
from jax.experimental import pallas as pl
from jax.experimental.pallas import tpu as pltpu
from jax.sharding import PartitionSpec as P

HEADS = 16
HEAD = 64
ROT = 16
DOC_MOST = 1024
EPS = 1e-05
NEG = -1e30
LANES = 128
PAIR = 3 * LANES
BLOCK = 256
F32 = jnp.float32
BF16 = jnp.bfloat16
MIB = 1 << 20
VMEM_MIB = 56


def dot(a, b):
    return lax.dot_general(a, b, (((1,), (0,)), ((), ())), preferred_element_type=F32)


def dot_t(a, b):
    return lax.dot_general(a, b, (((1,), (1,)), ((), ())), preferred_element_type=F32)


def whole(shape):
    return pl.BlockSpec(shape, lambda *_: (0,) * len(shape))


def place(to):
    at = {"dp": lax.axis_index("dp"), "seq": lax.axis_index("seq")}
    if to[0] == "ring":
        at["seq"] = lax.rem(at["seq"] + to[1] + to[2], to[2])
    else:
        at[to[0]] = at[to[0]] ^ to[1]
    return (at["dp"], at["seq"])


def both_ways(targets):
    back = [("ring", -to[1], to[2]) for to in targets if to[0] == "ring"]
    return [place(to) for to in sorted({*targets, *back})]


def greet(devices):
    barrier = pltpu.get_barrier_semaphore()
    for device in devices:
        pl.semaphore_signal(barrier, inc=1, device_id=device, device_id_type=pl.DeviceIdType.MESH)
    pl.semaphore_wait(barrier, len(devices))


def call(kernel, *args, grid, in_specs, out_specs, out_shape, name, flops, nbytes, trans=0, scalars=0, scratch=(), after=(), sends=(), cid=None):
    n, n_out, m = scalars + len(in_specs), len(out_specs), len(sends)

    def body(*refs):
        refs = list(refs)
        ins, _, srcs = refs[:n], refs[n : n + len(after)], refs[n + len(after) :][:m]
        rest = refs[n + len(after) + m :]
        outs, gots, own = rest[:n_out], rest[n_out : n_out + m], rest[n_out + m :]
        if not m:
            kernel(*ins, *outs, *own)
            return
        *own, send_sem, recv_sem = own

        def copy(k):
            _, lo, rows, to = sends[k]
            return pltpu.make_async_remote_copy(
                src_ref=srcs[k].at[pl.ds(lo, rows)],
                dst_ref=gots[k],
                send_sem=send_sem.at[k],
                recv_sem=recv_sem.at[k],
                device_id=place(to),
                device_id_type=pl.DeviceIdType.MESH,
            )

        @pl.when(pl.program_id(0) == 0)
        def _():
            greet(both_ways([to for *_, to in sends]))
            for k in range(m):
                copy(k).start()

        kernel(*ins, *outs, *own)

        @pl.when(pl.program_id(0) == grid[0] - 1)
        def _():
            for k in range(m):
                copy(k).wait()

    hbm = pl.BlockSpec(memory_space=pl.ANY)
    more = dict(collective_id=cid, has_side_effects=True) if m else {}
    sems = [pltpu.SemaphoreType.DMA((m,))] * 2 if m else []
    return pl.pallas_call(
        body,
        grid_spec=pltpu.PrefetchScalarGridSpec(
            num_scalar_prefetch=scalars,
            grid=grid,
            in_specs=[*in_specs, *[hbm] * (len(after) + m)],
            out_specs=[*out_specs, *[hbm] * m],
            scratch_shapes=[*scratch, *sems],
        ),
        out_shape=[*out_shape, *[jax.ShapeDtypeStruct((rows, a.shape[1]), a.dtype) for a, _, rows, _ in sends]],
        compiler_params=pltpu.CompilerParams(vmem_limit_bytes=VMEM_MIB * MIB, **more),
        cost_estimate=pl.CostEstimate(flops=int(flops), bytes_accessed=int(nbytes), transcendentals=int(trans)),
        name=name,
    )(*args, *after, *[a for a, *_ in sends])


def stage_bits(size):
    return [1 << b for b in range(size.bit_length() - 1)]


def stage_order(ndp, nseq, kind):
    dp_bits = [("dp", [b]) for b in stage_bits(ndp)]
    seq_bits = [("seq", [b]) for b in stage_bits(nseq)]
    cycle = [*dp_bits[1:], *seq_bits[:1]]
    kind = min(kind, len(cycle) - 1)
    at = (0, len(cycle) - 1, 1)[kind] if kind else 0
    return dp_bits[:1] + cycle[at:] + cycle[:at] + seq_bits[1:]


def short_order(ndp, nseq):
    dp_bits = stage_bits(ndp)
    return [("dp", dp_bits[:1]), ("dp", dp_bits[1:]), ("seq", stage_bits(nseq))]


def flat_bits(stages):
    return [(axis, bit) for axis, bits in stages for bit in bits]


def source(spot, stages, nseq):
    at = {"dp": lax.axis_index("dp"), "seq": lax.axis_index("seq")}
    bits = flat_bits(stages)
    for k, (axis, bit) in enumerate(bits):
        flag = spot // (1 << (len(bits) - 1 - k)) % 2
        if not (isinstance(flag, int) and flag == 0):
            at[axis] = at[axis] + flag * bit * (1 - 2 * (at[axis] // bit % 2))
    return at["dp"] * nseq + at["seq"]


def fan(bits):
    return [sum(b for k, b in enumerate(bits) if (part >> (len(bits) - 1 - k)) & 1) for part in range(1 << len(bits))]


def combine_kernel(counts, slots, *refs):
    outs = refs[sum(counts) :]
    at = 0
    for n, (k, col) in zip(counts, slots):
        total = refs[at][...].astype(F32)
        for r in refs[at + 1 : at + n]:
            total += r[...].astype(F32)
        outs[k][:, col : col + total.shape[1]] = total.astype(outs[k].dtype)
        at += n


def combine(items, after=(), joined=()):
    steps = 2 if all(rows % 32 == 0 for _, _, rows, _ in items) else 1
    ins, specs, counts, slots, shapes, nbytes = [], [], [], [], [], 0
    for k, (arrays, lo, rows, dtype) in enumerate(items):
        block, cols = rows // steps, arrays[0][0].shape[1]
        arrays = [(a, off) for a, off in arrays if off <= lo < off + a.shape[0]]
        for a, off in arrays:
            ins.append(a)
            specs.append(pl.BlockSpec((block, cols), lambda i, at=(lo - off) // block: (at + i, 0)))
        counts.append(len(arrays))
        if k in joined:
            slots.append((len(shapes) - 1, shapes[-1][1]))
            shapes[-1] = (rows, shapes[-1][1] + cols, dtype)
        else:
            slots.append((len(shapes), 0))
            shapes.append((rows, cols, dtype))
        nbytes += rows * cols * 2 * (len(arrays) + 2)
    return call(
        functools.partial(combine_kernel, counts, slots),
        *ins,
        grid=(steps,),
        in_specs=specs,
        out_specs=[pl.BlockSpec((rows // steps, cols), lambda i: (i, 0)) for rows, cols, _ in shapes],
        out_shape=[jax.ShapeDtypeStruct((rows, cols), dtype) for rows, cols, dtype in shapes],
        name="combine",
        flops=nbytes,
        nbytes=nbytes,
        after=after,
    )


def last_kernel(counts, nseq, *refs):
    n = sum(counts)
    small_ref, done_ref, kept_ref, *outs = refs[n:]
    kept_ref[...] = done_ref[...]
    combine_kernel(counts, [(0, 0), (0, refs[0].shape[1]), (1, 0)], *refs[:n], *outs[:2])
    d = small_ref.shape[1]
    me = lax.axis_index("dp") * nseq + lax.axis_index("seq")
    lines = [(k, 1) for k in (0, 1, 2, 3, 4, 4)] + [(5, 3), (8, outs[-1].shape[1] * d // outs[2].shape[1] // d)]
    for (at, rows), out in zip(lines, outs[2:]):
        flat = jnp.concatenate([small_ref[at + r : at + r + 1, :] for r in range(rows)], axis=1)
        flat = jnp.broadcast_to(flat, (8, rows * d))
        mine = out.shape[1]
        out[...] = pltpu.roll(flat, rows * d - me * mine, 1)[:1, :mine]


def last_sums(terms, small, done, ff, ndev, nseq):
    arrays = [a for term, *_ in terms for a, _ in term]
    rows = terms[0][2]
    d = small.shape[1]
    widths = [term[0][0].shape[1] for term, *_ in terms]
    shapes = [(rows, widths[0] + widths[1]), (rows, widths[2])] + [(1, d // ndev)] * 6 + [(1, 3 * d // ndev), (1, ff // ndev)]
    return call(
        functools.partial(last_kernel, [len(term) for term, *_ in terms], nseq),
        *arrays,
        small,
        done,
        grid=(1,),
        in_specs=[whole((rows, a.shape[1])) for a in arrays] + [whole(small.shape), whole(done.shape)],
        out_specs=[whole(done.shape)] + [whole(shape) for shape in shapes],
        out_shape=[jax.ShapeDtypeStruct(done.shape, done.dtype)] + [jax.ShapeDtypeStruct(shape, F32) for shape in shapes],
        name="last",
        flops=rows * d * 20,
        nbytes=rows * d * 40,
    )


class Halving:
    def __init__(self, send, keep, stages, sizes):
        self.keep, self.stages, self.sizes = keep, list(stages), sizes
        self.rows, self.got, self.ready = keep.shape[0], [], [send]

    def targets(self):
        axis, bits = self.stages[0]
        return [(axis, offset) for offset in fan(bits)[1:]]

    def permute(self):
        for part, (axis, offset) in zip(self.ready, self.targets()):
            self.got.append((lax.ppermute(part, axis, [(i, i ^ offset) for i in range(self.sizes[axis])]), 0))
        self.stages.pop(0)

    def sends(self, lo=0, hi=1, parts=1):
        size = self.ready[0].shape[0] // parts
        return [(a, lo * size, (hi - lo) * size, to) for a, to in zip(self.ready, self.targets())]

    def receive(self, arrays, lo=0, hi=1, parts=1, last=True):
        size = self.ready[0].shape[0] // parts
        self.got += [(a, lo * size) for a in arrays]
        if last:
            self.stages.pop(0)

    def items(self):
        arrays = [(self.keep, 0), *self.got]
        parts = 1 << len(self.stages[0][1])
        self.rows //= parts
        return [(arrays, k * self.rows, self.rows, BF16) for k in range(1, parts)]

    def rest(self):
        arrays = [(self.keep, 0), *self.got]
        return arrays, 0, self.rows, BF16


def advance(sums, after):
    groups = [r.items() for r in sums]
    outs = combine([item for group in groups for item in group], after)
    at = 0
    for r, group in zip(sums, groups):
        r.ready = outs[at : at + len(group)]
        at += len(group)
    return [outs[0]]


def unit_of(x):
    mean = jnp.mean(x, axis=-1, keepdims=True)
    c = x - mean
    inv = lax.rsqrt(jnp.mean(c * c, axis=-1, keepdims=True) + EPS)
    return c * inv, inv


def norm_kernel(len_ref, x_ref, dy_ref, g1, b1, g2, b2, a_ref, m_ref, grad_ref, sum_ref):
    u, _ = unit_of(x_ref[...].astype(F32))
    a_ref[...] = (u * g1[...] + b1[...]).astype(BF16)
    m_ref[...] = (u * g2[...] + b2[...]).astype(BF16)
    rows = x_ref.shape[0]
    toks = rows * pl.num_programs(0)
    at = lax.axis_index("seq") * toks + pl.program_id(0) * rows + lax.broadcasted_iota(jnp.int32, (rows, 1), 0)
    text = sum(len_ref[k] for k in range(len_ref.shape[0] - 1))
    grad = dy_ref[...].astype(F32) * jnp.where(at < text, 1.0, 0.0)
    grad_ref[...] = grad.astype(BF16)

    @pl.when(pl.program_id(0) == 0)
    def _():
        sum_ref[...] = jnp.zeros_like(sum_ref)

    sum_ref[...] += jnp.sum(grad, axis=0, keepdims=True)


def norms(lengths, x, dy, g1, b1, g2, b2, after=()):
    rows, d = x.shape
    tr = min(256, rows)
    row = pl.BlockSpec((tr, d), lambda i, *_: (i, 0))
    return call(
        norm_kernel,
        lengths,
        x,
        dy,
        g1,
        b1,
        g2,
        b2,
        scalars=1,
        grid=(rows // tr,),
        in_specs=[row, row] + [whole((1, d))] * 4,
        out_specs=[row, row, row, whole((1, d))],
        out_shape=[jax.ShapeDtypeStruct((rows, d), BF16)] * 3 + [jax.ShapeDtypeStruct((1, d), F32)],
        flops=rows * d * 20, nbytes=rows * d * 10,
        name="norms",
        after=after,
    )


def mlp_kernel(m_ref, grad_ref, win_ref, bin_ref, wout_ref, out_ref, act_ref, dpre_ref, dm_ref, bsum_ref):
    pre = dot(m_ref[...], win_ref[...]) + bin_ref[...]
    cdf = 0.5 * (1.0 + lax.erf(pre * math.sqrt(0.5)))
    act = (pre * cdf).astype(BF16)
    act_ref[...] = act
    d_act = dot_t(grad_ref[...], wout_ref[...])
    slope = cdf + pre * (jnp.exp(-0.5 * pre * pre) * (1.0 / math.sqrt(2.0 * math.pi)))
    d_pre = (d_act * slope).astype(BF16)
    dpre_ref[...] = d_pre
    bsum_ref[...] = jnp.sum(d_pre.astype(F32), axis=0, keepdims=True)

    @pl.when(pl.program_id(0) == 0)
    def _():
        out_ref[...] = jnp.zeros_like(out_ref)
        dm_ref[...] = jnp.zeros_like(dm_ref)

    out_ref[...] += dot(act, wout_ref[...])
    dm_ref[...] += dot_t(d_pre, win_ref[...])


def mlp(m, grad, win, b_in, wout, after=(), sends=(), cid=None):
    rows, d = m.shape
    ff = win.shape[1]
    tf = 1024
    cols = pl.BlockSpec((rows, tf), lambda i: (0, i))
    line = pl.BlockSpec((1, tf), lambda i: (0, i))
    return call(
        mlp_kernel,
        m, grad, win, b_in, wout,
        grid=(ff // tf,),
        in_specs=[
            whole((rows, d)),
            whole((rows, d)),
            pl.BlockSpec((d, tf), lambda i: (0, i)),
            line,
            pl.BlockSpec((tf, d), lambda i: (i, 0)),
        ],
        out_specs=[whole((rows, d)), cols, cols, whole((rows, d)), line],
        out_shape=[
            jax.ShapeDtypeStruct((rows, d), F32),
            jax.ShapeDtypeStruct((rows, ff), BF16),
            jax.ShapeDtypeStruct((rows, ff), BF16),
            jax.ShapeDtypeStruct((rows, d), F32),
            jax.ShapeDtypeStruct((1, ff), F32),
        ],
        flops=8 * rows * d * ff, nbytes=4 * d * ff + 4 * rows * ff + 12 * rows * d, trans=rows * ff * 2,
        name="mlp",
        after=after,
        sends=sends,
        cid=cid,
    )


def turned(left, nat_ref, at):
    n = min(BLOCK, left.shape[1])
    eye = lax.broadcasted_iota(jnp.int32, (n, n), 0) == lax.broadcasted_iota(jnp.int32, (n, n), 1)
    eye = jnp.where(eye, 1.0, 0.0).astype(BF16)
    for c in range(0, left.shape[1], n):
        nat_ref[at + c : at + c + n, :] = dot_t(eye, left[:, c : c + n])


def placed(order, nat_ref, lt_ref):
    blocks = 1 << len(flat_bits(order[0]))
    size = nat_ref.shape[0] // blocks
    for b in range(blocks):
        rows = pl.ds(pl.multiple_of(source(b, *order) * size, size), size)
        lt_ref[b * size : (b + 1) * size, :] = nat_ref[rows, :].astype(BF16)


def wgrad_kernel(stacked, orders, steps, starts, per, *refs):
    n = len(starts)
    n_right = -(-sum(steps) // per)
    n_left = len(refs) - n_right - 3 * n - 2
    lefts, rights, refs = refs[:n_left], refs[n_left : n_left + n_right], refs[n_left + n_right :]
    outs, (nat_ref, lt_ref) = refs[:-2], refs[-2:]
    i = pl.program_id(0)

    @pl.when(i == 0)
    def _():
        row = col = 0
        for left in lefts:
            toks, width = left.shape
            turned(left[...], nat_ref.at[:, col : col + toks], row)
            if stacked:
                col += toks
            else:
                row += width

    for g in range(n):
        send_ref, keep_ref, bsum_ref = outs[3 * g : 3 * g + 3]

        @pl.when(i == starts[g])
        def _():
            placed(orders[g], nat_ref, lt_ref)

        for k, right_ref in enumerate(rights):
            first, end = max(starts[g], k * per), min(starts[g] + steps[g], (k + 1) * per)

            @pl.when((i >= first) & (i < end))
            def _():
                half = keep_ref.shape[0]
                right = right_ref[...]
                send_ref[...] = dot(lt_ref[half:, :], right).astype(BF16)
                keep_ref[...] = dot(lt_ref[:half, :], right).astype(BF16)
                bsum_ref[...] = jnp.sum(right.astype(F32), axis=0, keepdims=True)


def wgrad(groups, lefts, right, tn=512, after=(), sends=(), cid=None):
    rights = right if isinstance(right, list) else [right]
    toks, width = rights[0].shape
    stacked = lefts[0].shape[0] < toks
    per = width // tn
    d = lefts[0].shape[1] if stacked else sum(left.shape[1] for left in lefts)
    steps = [cols // tn for _, cols in groups]
    starts = [sum(steps[:g]) for g in range(len(groups))]
    out_specs, out_shape = [], []
    for (_, cols), first, n in zip(groups, starts, steps):
        at = lambda i, *_, first=first, n=n: (0, jnp.clip(i - first, 0, n - 1))
        out_specs += [pl.BlockSpec((d // 2, tn), at)] * 2 + [pl.BlockSpec((1, tn), at)]
        out_shape += [jax.ShapeDtypeStruct((d // 2, cols), BF16)] * 2 + [jax.ShapeDtypeStruct((1, cols), F32)]
    cols = sum(r.shape[1] for r in rights)
    return call(
        functools.partial(wgrad_kernel, stacked, [o for o, _ in groups], steps, starts, per if len(rights) > 1 else sum(steps)),
        *lefts,
        *rights,
        grid=(sum(steps),),
        in_specs=[
            *[whole(left.shape) for left in lefts],
            *[pl.BlockSpec((toks, tn), lambda i, *_, k=k: (0, jnp.clip(i - k * per, 0, per - 1))) for k in range(len(rights))],
        ],
        out_specs=out_specs,
        scratch=[pltpu.VMEM((d, toks), F32), pltpu.VMEM((d, toks), BF16)],
        out_shape=out_shape,
        flops=2 * toks * d * cols,
        nbytes=2 * toks * (d + cols) + 2 * d * cols,
        name="wgrad",
        after=after,
        sends=sends,
        cid=cid,
    )


def wgrad_rows_kernel(turns_n, orders, groups, *refs):
    n = len(groups)
    (left_ref, right_ref), refs = refs[:2], refs[2:]
    outs, (nat_ref, lt_ref) = refs[: 2 * n], refs[2 * n :]
    i = pl.program_id(0)
    tile = left_ref.shape[1]

    @pl.when(i < turns_n)
    def _():
        turned(left_ref[...], nat_ref, 0)
        lt_ref[pl.ds(pl.multiple_of(i * tile, tile), tile), :] = nat_ref[...].astype(lt_ref.dtype)

    for g, (first, steps, lo, cols) in enumerate(groups):
        send_ref, keep_ref = outs[2 * g : 2 * g + 2]
        rows = send_ref.shape[0]

        @pl.when((i >= first) & (i < first + steps))
        def _():
            total = 1 << len(flat_bits(orders[g][0]))
            blocks = total // steps
            size = rows // blocks
            for b in range(blocks):
                spot = ((i - first) * blocks + b + total // 2) % total
                at = pl.ds(pl.multiple_of(source(spot, *orders[g]) * size, size), size)
                nat_ref[b * size : (b + 1) * size, :] = lt_ref[at, :].astype(F32)
            out = dot(nat_ref[:rows, :].astype(BF16), right_ref[:, lo : lo + cols]).astype(BF16)

            @pl.when(i < first + steps // 2)
            def _():
                send_ref[...] = out

            @pl.when(i >= first + steps // 2)
            def _():
                keep_ref[...] = out


def wgrad_rows(groups, left, right, tile=1024, after=(), sends=(), cid=None):
    toks, d = right.shape
    rows = left.shape[1]
    n = rows // tile
    half = n // 2
    orders = [o for o, _ in groups]
    kind = BF16 if (rows >> len(flat_bits(orders[0][0]))) % 16 == 0 else F32
    cuts, out_specs, out_shape, lo = [], [], [], 0
    for g, (_, cols) in enumerate(groups):
        first = n * (g + 1)
        cuts.append((first, n, lo, cols))
        lo += cols
        out_specs.append(pl.BlockSpec((tile, cols), lambda i, *_, first=first: (jnp.clip(i - first, 0, half - 1), 0)))
        out_specs.append(pl.BlockSpec((tile, cols), lambda i, *_, first=first: (jnp.clip(i - first - half, 0, half - 1), 0)))
        out_shape += [jax.ShapeDtypeStruct((rows // 2, cols), BF16)] * 2
    return call(
        functools.partial(wgrad_rows_kernel, n, orders, cuts),
        left,
        right,
        grid=(n * (1 + len(groups)),),
        in_specs=[
            pl.BlockSpec((toks, tile), lambda i, *_: (0, jnp.minimum(i, n - 1))),
            pl.BlockSpec((toks, d), lambda i, *_: (0, 0)),
        ],
        out_specs=out_specs,
        scratch=[pltpu.VMEM((tile, toks), F32), pltpu.VMEM((rows, toks), kind)],
        out_shape=out_shape,
        flops=2 * toks * rows * d,
        nbytes=2 * (rows * (d + toks) + toks * d),
        name="wgrad_rows",
        after=after,
        sends=sends,
        cid=cid,
    )


def document_start(len_ref, at):
    begin, end = jnp.zeros_like(at), 0
    for k in range(len_ref.shape[0]):
        end = end + len_ref[k]
        begin = jnp.where(at >= end, end, begin)
    return begin


def d_ctx_kernel(halos, nseq, len_ref, a_ref, w_ref, out_ref, cos_ref, sin_ref, start_ref):
    out_ref[...] = dot_t(a_ref[...], w_ref[...]).astype(BF16)
    toks, rows = a_ref.shape[0], cos_ref.shape[0]
    me = lax.axis_index("seq")
    base = (me - halos) * toks
    at = base + pl.program_id(0) * rows + lax.broadcasted_iota(jnp.int32, (rows, LANES), 0)
    lane = lane_ids(rows) % HEAD
    half = ROT // 2
    freq = jnp.zeros((rows, LANES), F32)
    for k in range(half):
        freq = jnp.where(lane % half == k, 10000.0 ** (-(2.0 * k) / ROT), freq)
    angle = (at - document_start(len_ref, at)).astype(F32) * freq
    cos_ref[...] = jnp.where(lane < ROT, jnp.cos(angle), 1.0)
    sin = jnp.sin(angle)
    sin_ref[...] = jnp.where(lane < half, -sin, jnp.where(lane < ROT, sin, 0.0))
    own = me * toks + lax.broadcasted_iota(jnp.int32, (1, toks), 1)
    start_ref[...] = document_start(len_ref, own) - base


def d_context(lengths, grad, w, halos, nseq, tn=256, after=(), sends=(), cid=None):
    rows, d = grad.shape
    win = rows * (halos + 1)
    steps = d // tn
    table = pl.BlockSpec((win // steps, LANES), lambda i, *_: (i, 0))
    return call(
        functools.partial(d_ctx_kernel, halos, nseq),
        lengths,
        grad,
        w,
        scalars=1,
        grid=(steps,),
        in_specs=[whole((rows, d)), pl.BlockSpec((tn, d), lambda i, *_: (i, 0))],
        out_specs=[pl.BlockSpec((rows, tn), lambda i, *_: (0, i)), table, table, whole((1, rows))],
        out_shape=[
            jax.ShapeDtypeStruct((rows, d), BF16),
            jax.ShapeDtypeStruct((win, LANES), F32),
            jax.ShapeDtypeStruct((win, LANES), F32),
            jax.ShapeDtypeStruct((1, rows), jnp.int32),
        ],
        flops=2 * rows * d * d,
        nbytes=2 * d * (2 * rows + d),
        name="d_ctx",
        after=after,
        sends=sends,
        cid=cid,
    )


def lane_ids(rows):
    return lax.broadcasted_iota(jnp.int32, (rows, LANES), 1)


def turns():
    frm = lax.broadcasted_iota(jnp.int32, (LANES, LANES), 0)
    to = lax.broadcasted_iota(jnp.int32, (LANES, LANES), 1)
    half = ROT // 2
    within = frm % HEAD
    partner = jnp.where(within < half, frm + half, frm - half)
    rotated = within < ROT
    turned = (frm + HEAD) % LANES
    one = lambda hit: jnp.where(hit, 1.0, 0.0).astype(BF16)
    return one(turned == to), one(rotated & (partner == to)), one(rotated & ((partner + HEAD) % LANES == to))


def split(x):
    high = x.astype(BF16)
    return jnp.concatenate([high, (x - high.astype(F32)).astype(BF16)], axis=1)


def qkv_kernel(n, *refs):
    a_refs, (w_ref, bias_ref, cos_ref, sin_ref, q_ref, k_ref, v_ref) = refs[:n], refs[n:]
    turn, swap, swap_turn = turns()
    k_moves = jnp.concatenate([turn, swap_turn], axis=1)
    k_moves = jnp.concatenate([k_moves, k_moves], axis=0)
    q_moves = jnp.concatenate([swap, swap], axis=0)
    r = 0
    for a_ref in a_refs:
        rows = slice(r, r + a_ref.shape[0])
        r += a_ref.shape[0]
        first = lane_ids(a_ref.shape[0]) < HEAD
        packed = dot(a_ref[...], w_ref[...]) + bias_ref[...]
        cos, sin = cos_ref[rows, :], sin_ref[rows, :]
        for g in range(w_ref.shape[1] // PAIR):
            c = g * PAIR
            lanes = slice(g * LANES, (g + 1) * LANES)
            pa, pb, pc = packed[:, c : c + LANES], packed[:, c + LANES : c + 2 * LANES], packed[:, c + 2 * LANES : c + PAIR]
            both = dot(split(jnp.where(first, pc, pa)), k_moves)
            k_ref[rows, lanes] = (both[:, :LANES] * cos + both[:, LANES:] * sin).astype(BF16)
            v_ref[rows, lanes] = jnp.where(first, pb, pc).astype(BF16)
            if a_ref is a_refs[-1]:
                q = jnp.where(first, pa, pb)
                q_ref[:, lanes] = (q * cos + dot(split(q), q_moves) * sin).astype(BF16)


def qkv(pieces, w, bias, cos, sin, group=4, after=()):
    toks, d = pieces[-1].shape
    win = sum(p.shape[0] for p in pieces)
    cols = w.shape[1]
    out = pl.BlockSpec((win, group * LANES), lambda i: (0, i))
    return call(
        functools.partial(qkv_kernel, len(pieces)),
        *pieces, w, bias, cos, sin,
        grid=(cols // PAIR // group,),
        in_specs=[
            *[whole(p.shape) for p in pieces],
            pl.BlockSpec((d, group * PAIR), lambda i: (0, i)),
            pl.BlockSpec((1, group * PAIR), lambda i: (0, i)),
            whole((win, LANES)),
            whole((win, LANES)),
        ],
        out_specs=[pl.BlockSpec((toks, group * LANES), lambda i: (0, i)), out, out],
        out_shape=[jax.ShapeDtypeStruct((toks, cols // 3), BF16)] + [jax.ShapeDtypeStruct((win, cols // 3), BF16)] * 2,
        flops=2 * win * d * cols, nbytes=8 * win * d + 2 * d * cols,
        name="qkv",
        after=after,
    )


GROUP = 2
QB = 256


def attention_kernel(
    toks, win, start_ref, q_ref, k_ref, v_ref, do_ref, cos_ref, sin_ref, ctx_ref, dp_ref,
    k2, v2, kt, vt, s_ref, e_ref, dq_acc, dk_acc, dv_acc,
):
    nk = win // BLOCK
    halo = win - toks
    first = lane_ids(BLOCK) < HEAD
    first_q = lane_ids(QB) < HEAD
    zero = jnp.zeros((BLOCK, LANES), BF16)
    zero_q = jnp.zeros((QB, LANES), BF16)
    top = lax.broadcasted_iota(jnp.int32, (LANES, QB), 0) < HEAD
    groups = range(GROUP)
    lanes = [slice(g * LANES, (g + 1) * LANES) for g in groups]
    eye = lax.broadcasted_iota(jnp.int32, (LANES, LANES), 0) == lax.broadcasted_iota(jnp.int32, (LANES, LANES), 1)
    upper = lax.broadcasted_iota(jnp.int32, (LANES, LANES), 0) < HEAD
    eye0 = jnp.where(eye & upper, 1.0, 0.0).astype(BF16)
    eye1 = jnp.where(eye & ~upper, 1.0, 0.0).astype(BF16)

    def prepare(j, _):
        rows = pl.ds(pl.multiple_of(j * BLOCK, BLOCK), BLOCK)
        for g in groups:
            for src, two, tr in ((k_ref, k2, kt), (v_ref, v2, vt)):
                x = src[rows, lanes[g]]
                two[g, j, :BLOCK, :] = jnp.where(first, x, zero)
                two[g, j, BLOCK:, :] = jnp.where(first, zero, x)
                tr[g, j, :, :BLOCK] = dot_t(eye0, x).astype(BF16)
                tr[g, j, :, BLOCK:] = dot_t(eye1, x).astype(BF16)
        return 0

    lax.fori_loop(0, nk, prepare, 0)
    dk_acc[...] = jnp.zeros_like(dk_acc)
    dv_acc[...] = jnp.zeros_like(dv_acc)
    scale = HEAD**-0.5
    for i in range(toks // QB):
        rows = slice(i * QB, (i + 1) * QB)
        last = (halo + (i + 1) * QB) // BLOCK
        low = max(halo + i * QB - DOC_MOST + 1, 0) // BLOCK
        qs = [q_ref[rows, lanes[g]].astype(F32) * scale for g in groups]
        qts = [q.T.astype(BF16) for q in qs]
        qs = [q.astype(BF16) for q in qs]
        q2 = [jnp.concatenate([jnp.where(first_q, q, zero_q), jnp.where(first_q, zero_q, q)], axis=0) for q in qs]
        start = start_ref[:, rows]
        q_at = halo + i * QB + lax.broadcasted_iota(jnp.int32, (1, QB), 1)

        def scores(j, peaks):
            at = j * BLOCK + lax.broadcasted_iota(jnp.int32, (BLOCK, QB), 0)
            ok = (at >= start) & (at <= q_at)
            out = []
            for g in groups:
                s = dot(k2[g, j], qts[g])
                s0 = jnp.where(ok, s[:BLOCK], NEG)
                s1 = jnp.where(ok, s[BLOCK:], NEG)
                s_ref[g, j, :BLOCK, :] = s0
                s_ref[g, j, BLOCK:, :] = s1
                out.append(jnp.maximum(peaks[2 * g], jnp.max(s0, axis=0, keepdims=True)))
                out.append(jnp.maximum(peaks[2 * g + 1], jnp.max(s1, axis=0, keepdims=True)))
            return tuple(out)

        floor = jnp.full((1, QB), NEG, F32)
        peaks = lax.fori_loop(low, last, scores, (floor,) * (2 * GROUP), unroll=True)

        def weigh(j, carry):
            out = []
            for g in groups:
                t0, t1, acc = carry[3 * g : 3 * g + 3]
                e0 = jnp.exp(s_ref[g, j, :BLOCK, :] - peaks[2 * g])
                e1 = jnp.exp(s_ref[g, j, BLOCK:, :] - peaks[2 * g + 1])
                b0, b1 = e0.astype(BF16), e1.astype(BF16)
                e_ref[g, j, :BLOCK, :] = b0
                e_ref[g, j, BLOCK:, :] = b1
                acc = acc + dot(vt[g, j], jnp.concatenate([b0, b1], axis=0))
                out += [t0 + jnp.sum(e0, axis=0, keepdims=True), t1 + jnp.sum(e1, axis=0, keepdims=True), acc]
            return tuple(out)

        none = jnp.zeros((1, QB), F32)
        sums = lax.fori_loop(low, last, weigh, (none, none, jnp.zeros((LANES, QB), F32)) * GROUP, unroll=True)
        do_l, do2, d0, d1 = [], [], [], []
        for g in groups:
            t0, t1, acc = sums[3 * g : 3 * g + 3]
            share = jnp.where(top, 1.0 / t0, 1.0 / t1)
            ctx_t = acc * share
            ctx_ref[rows, lanes[g]] = ctx_t.T.astype(BF16)
            do_t = do_ref[rows, lanes[g]].astype(F32).T * share
            both = do_t * ctx_t
            d0.append(jnp.sum(both[:HEAD], axis=0, keepdims=True))
            d1.append(jnp.sum(both[HEAD:], axis=0, keepdims=True))
            do = do_t.T.astype(BF16)
            do_l.append(do_t.astype(BF16))
            do2.append(jnp.concatenate([jnp.where(first_q, do, zero_q), jnp.where(first_q, zero_q, do)], axis=0))

        def back(j, dqs):
            at = pl.ds(pl.multiple_of(j * BLOCK, BLOCK), BLOCK)
            out = []
            for g in groups:
                dp = dot(v2[g, j], do_l[g])
                e0, e1 = e_ref[g, j, :BLOCK, :], e_ref[g, j, BLOCK:, :]
                ds0 = (e0.astype(F32) * (dp[:BLOCK] - d0[g])).astype(BF16)
                ds1 = (e1.astype(F32) * (dp[BLOCK:] - d1[g])).astype(BF16)
                dv_acc[at, lanes[g]] += dot(jnp.concatenate([e0, e1], axis=1), do2[g])
                dk_acc[at, lanes[g]] += dot(jnp.concatenate([ds0, ds1], axis=1), q2[g])
                out.append(dqs[g] + dot(kt[g, j], jnp.concatenate([ds0, ds1], axis=0)))
            return tuple(out)

        dqs = lax.fori_loop(low, last, back, (jnp.zeros((LANES, QB), F32),) * GROUP, unroll=True)
        for g in groups:
            dq_acc[rows, lanes[g]] = dqs[g].T * scale

    turn, swap, swap_turn = turns()
    for j in range(nk):
        rows = slice(j * BLOCK, (j + 1) * BLOCK)
        cos, sin = cos_ref[rows, :], sin_ref[rows, :]
        for g in groups:
            dk = dk_acc[rows, lanes[g]].astype(BF16)
            dk = dot(dk, turn) * cos - dot(dk, swap_turn) * sin
            dv = dv_acc[rows, lanes[g]]
            if j * BLOCK >= halo:
                own = slice(j * BLOCK - halo, (j + 1) * BLOCK - halo)
                dq = dq_acc[own, lanes[g]]
                dq = dq * cos - dot(dq.astype(BF16), swap) * sin
            else:
                dq = jnp.zeros_like(dk)
            c = g * PAIR
            dp_ref[rows, c : c + LANES] = jnp.where(first, dq, dk).astype(BF16)
            dp_ref[rows, c + LANES : c + 2 * LANES] = jnp.where(first, dv, dq).astype(BF16)
            dp_ref[rows, c + 2 * LANES : c + PAIR] = jnp.where(first, dk, dv).astype(BF16)


def attention(start, q, k, v, d_ctx, cos, sin, pair, pairs, after=(), sends=(), cid=None):
    win, d = k.shape
    toks = d_ctx.shape[0]
    nk = win // BLOCK
    width = GROUP * LANES
    at = pair // GROUP
    own = pl.BlockSpec((toks, width), lambda i: (0, at + i))
    every = pl.BlockSpec((win, width), lambda i: (0, at + i))
    out = pairs * LANES
    return call(
        functools.partial(attention_kernel, toks, win),
        start,
        q,
        k,
        v,
        d_ctx,
        cos,
        sin,
        grid=(pairs // GROUP,),
        in_specs=[whole((1, toks)), own, every, every, own, whole((win, LANES)), whole((win, LANES))],
        out_specs=[pl.BlockSpec((toks, width), lambda i: (0, i)), pl.BlockSpec((win, GROUP * PAIR), lambda i: (0, i))],
        out_shape=[jax.ShapeDtypeStruct((toks, out), BF16), jax.ShapeDtypeStruct((win, 3 * out), BF16)],
        scratch=[
            pltpu.VMEM((GROUP, nk, 2 * BLOCK, LANES), BF16),
            pltpu.VMEM((GROUP, nk, 2 * BLOCK, LANES), BF16),
            pltpu.VMEM((GROUP, nk, LANES, 2 * BLOCK), BF16),
            pltpu.VMEM((GROUP, nk, LANES, 2 * BLOCK), BF16),
            pltpu.VMEM((GROUP, nk, 2 * BLOCK, QB), F32),
            pltpu.VMEM((GROUP, nk, 2 * BLOCK, QB), BF16),
            pltpu.VMEM((toks, width), F32),
            pltpu.VMEM((win, width), F32),
            pltpu.VMEM((win, width), F32),
        ],
        flops=pairs * toks * DOC_MOST * 4 * 6 * LANES,
        nbytes=14 * win * out,
        trans=pairs * 2 * toks * DOC_MOST,
        name="attention",
        after=after,
        sends=sends,
        cid=cid,
    )


def tail_kernel(cfg, *refs):
    ndp, nseq, halos, n_pieces, n_dp, n_ctx, joins, last_c = cfg
    refs = list(refs)
    take = lambda n: [refs.pop(0) for _ in range(n)]
    dp_rows, (w_ref,) = take(n_dp), take(1)
    n_late = n_dp - 2 + n_pieces + n_ctx + 3
    late = take(n_late)
    mlp_ref, wd_ref, bias_ref, g1, g2 = take(5)
    gsum_ref, qsum_ref, isum_ref = take(3)
    left_q, own_q = take(2)
    hidden_ref, grad_in_ref, small = take(3)
    owns = take(3)
    last_gots = [take(len(fan(last_c)) - 1) for _ in owns]
    nat, lt, own_acc, far, far_got = take(5)
    group_bufs = [take(6), take(6), [None, own_q.at[0], None, left_q, *take(2)]]
    bsum_ref, small_got = take(2)
    held = take(n_late)
    send_sem, recv_sem, late_sem = refs
    loads = [pltpu.make_async_copy(a, b, late_sem.at[k]) for k, (a, b) in enumerate(zip(late, held))]
    held = list(held)
    take_held = lambda n: [held.pop(0) for _ in range(n)]
    dp_cols, pieces, ctxs = take_held(n_dp - 2), take_held(n_pieces), take_held(n_ctx)
    grad_ref, x_ref, d_mlp_ref = held
    first_loads = n_dp - 2 + n_pieces
    toks, d = x_ref.shape
    me_dp, me_seq = lax.axis_index("dp"), lax.axis_index("seq")
    dp_bits = stage_bits(ndp)
    core, cross = fan(dp_bits[:1]), fan(dp_bits[1:])
    across, everyone = fan(last_c), fan(dp_bits)

    def device(axis, offset):
        return (me_dp ^ offset, me_seq) if axis == "dp" else (me_dp, me_seq ^ offset)

    behind = (me_dp, lax.rem(me_seq + nseq - 1, nseq))
    ahead = (me_dp, lax.rem(me_seq + 1, nseq))
    names = {}

    def copy(name, src, dst, to):
        k = names.setdefault(name, len(names))
        return pltpu.make_async_remote_copy(
            src_ref=src,
            dst_ref=dst,
            send_sem=send_sem.at[k],
            recv_sem=recv_sem.at[k],
            device_id=to,
            device_id_type=pl.DeviceIdType.MESH,
        )

    half = toks // 2

    def far_copy(k, c):
        rows = pl.ds(c * half, half)
        return copy(("far", k, c), far.at[k, rows], far_got.at[k, rows], behind)


    def first(n):
        send, _, got, *_ = group_bufs[n]
        return copy(("core", n), send, got, device("dp", core[1]))

    def second(n):
        _, _, _, out, into, _ = group_bufs[n]
        start = 1 if n < 2 else 0
        return [copy(("cross", n, k), out.at[k - start], into.at[k - 1], device("dp", cross[k])) for k in range(1, len(cross))]

    def third(n):
        out, got = group_bufs[n][5], last_gots[(n + 1) % 3]
        return [copy(("across", n, k), out.at[k - 1], got[k - 1], device("seq", across[k])) for k in range(1, len(across))]

    def to_second(n):
        _, keep, got, out, _, _ = group_bufs[n]
        first(n).wait()
        rows = out.shape[1]
        for k, c in enumerate(second(n), 1):
            at = slice(k * rows, (k + 1) * rows)
            out[k - 1] = (keep[at, :].astype(F32) + got[at, :].astype(F32)).astype(BF16)
            c.start()

    def to_third(n):
        _, keep, got, _, into, out = group_bufs[n]
        for c in second(n):
            c.wait()
        own = owns[(n + 1) % 3]
        rows = own.shape[0]
        copies = third(n)
        for k in reversed(range(len(across))):
            at = slice(k * rows, (k + 1) * rows)
            total = keep[at, :].astype(F32)
            if got is not None:
                total += got[at, :].astype(F32)
            for b in range(len(cross) - 1):
                total += into[b, at, :].astype(F32)
            if k:
                out[k - 1] = total.astype(out.dtype)
                copies[k - 1].start()
            else:
                own[...] = total

    def pass_on(k, c):
        far_copy(k - 1, c).wait()
        rows = pl.ds(c * half, half)
        far[k, rows] = (far[k, rows].astype(F32) + far_got[k - 1, rows].astype(F32)).astype(BF16)
        far_copy(k, c).start()

    def back(rows=slice(None)):
        total, at = None, 0
        for a_ref in dp_rows:
            n = a_ref.shape[1]
            term = dot_t(a_ref[rows, :], w_ref[:, at : at + n])
            total, at = term if total is None else total + term, at + n
        return total

    step = [0]
    pid = pl.program_id(0)

    def phase(fn):
        pl.when(pid == step[0])(fn)
        step[0] += 1

    for k in range(halos):

        def do_far(k=k):
            if k == 0:
                offsets = [("dp", o) for o in everyone[1:]] + [("seq", o) for o in across[1:]]
                greet([device(*o) for o in offsets] + [behind, ahead])
                for c in loads + second(2):
                    c.start()
            for c in range(2):
                rows = slice(c * half, (c + 1) * half)
                far[k, rows] = back(rows).astype(BF16)
                if k == 0 and (c == 0 or halos == 1):
                    far_copy(0, c).start()
            if k == 1:
                far_copy(0, 1).start()

        phase(do_far)

    def do_columns():
        for c in loads[:first_loads]:
            c.wait()
        col = 0
        for left in pieces:
            n = left.shape[0]
            turned(left[...], nat.at[:, :n], 0)
            placed((short_order(ndp, nseq), nseq), nat.at[:, :n], lt.at[:, col : col + n])
            col += n
        send, keep = group_bufs[0][:2]
        half, at = keep.shape[0], 0
        for right_ref in dp_cols:
            right = right_ref[...]
            n = right.shape[1]
            send[:, at : at + n] = dot(lt[half:, :], right).astype(BF16)
            keep[:, at : at + n] = dot(lt[:half, :], right).astype(BF16)
            bsum_ref[:, at : at + n] = jnp.sum(right.astype(F32), axis=0, keepdims=True)
            at += n
        first(0).start()
        if halos > 1:
            pass_on(1, 0)

    phase(do_columns)

    def do_dense():
        for c in loads[first_loads:]:
            c.wait()
        at = 0
        for ctx in ctxs:
            turned(ctx[...], nat, at)
            at += ctx.shape[1]
        placed((short_order(ndp, nseq), nseq), nat, lt.at[:, :toks])
        send, keep = group_bufs[1][:2]
        half = keep.shape[0]
        send[...] = dot(lt[half:, :toks], grad_ref[...]).astype(BF16)
        first(1).start()
        keep[...] = dot(lt[:half, :toks], grad_ref[...]).astype(BF16)
        to_second(0)

    phase(do_dense)

    def do_own():
        own_acc[...] = back()
        if halos > 1:
            pass_on(1, 1)
        to_second(1)
        to_third(2)

    phase(do_own)
    for t in range(joins):

        def do_join(t=t):
            cols = hidden_ref.shape[1]
            at = slice(t * cols, (t + 1) * cols)
            total, row = x_ref[:, at].astype(F32) + mlp_ref[...] + bias_ref[:, at], 0
            for ctx in ctxs:
                n = ctx.shape[1]
                total += dot(ctx[...], wd_ref[row : row + n, :])
                row += n
            hidden_ref[...] = total.astype(BF16)

        phase(do_join)

    def do_rest():
        for k in range(2, halos):
            for c in range(2):
                pass_on(k, c)
        to_third(0)
        to_third(1)
        small[...] = jnp.zeros_like(small)
        rows = min(128, half)
        for r in range(0, toks, rows):
            if r % half == 0:
                far_copy(halos - 1, r // half).wait()
            at = slice(r, r + rows)
            u, inv = unit_of(x_ref[at, :].astype(F32))
            d1 = own_acc[at, :] + far_got[halos - 1, at, :].astype(F32)
            d2 = d_mlp_ref[at, :]
            e = d1 * g1[...] + d2 * g2[...]
            dx = inv * (e - jnp.mean(e, axis=-1, keepdims=True) - u * jnp.mean(e * u, axis=-1, keepdims=True))
            grad_in_ref[at, :] = grad_ref[at, :].astype(F32) + dx
            for k, v in enumerate((d1 * u, d1, d2 * u, d2)):
                small[k : k + 1, :] += jnp.sum(v, axis=0, keepdims=True)
        small[4:5, :] = gsum_ref[...]
        row = 5
        for parts in ((qsum_ref, bsum_ref), (isum_ref,)):
            flat = jnp.concatenate([p[...] for p in parts], axis=1)
            for c in range(0, flat.shape[1], d):
                small[row : row + 1, :] = flat[:, c : c + d]
                row += 1
        used = 0
        for axis, offsets in (("dp", everyone), ("seq", across)):
            copies = []
            for o in offsets[1:]:
                copies.append(copy(("small", used), small, small_got.at[used], device(axis, o)))
                copies[-1].start()
                used += 1
            for c in copies:
                c.wait()
            total = small[...]
            for k in range(used - len(copies), used):
                total += small_got[k]
            small[...] = total
        for c in third(0) + third(1) + third(2):
            c.wait()

    phase(do_rest)


def tail(dps, w, pieces, ctxs, grad, x, mlp_out, d_mlp, w_d, bias, g1, g2, sums, left_q, ndp, nseq, halos, after=()):
    toks, d = x.shape
    depth = w.shape[1]
    joins = 4
    own_at = halos + 2
    dp_bits, seq_bits = stage_bits(ndp), stage_bits(nseq)
    cross, across = 1 << len(dp_bits[1:]), 1 << len(seq_bits)
    tile = d // joins
    once = lambda shape: pl.BlockSpec(shape, lambda i: (0,) * len(shape), pipeline_mode=pl.Buffered(1))
    piece_at = lambda i: (jnp.where(i < halos, i, jnp.where(i < own_at, halos - 1, halos)), 0)
    join_at = lambda i: (0, jnp.clip(i - own_at - 1, 0, joins - 1))
    hbm = pl.BlockSpec(memory_space=pl.ANY)
    cut_up = lambda a, n: a.reshape(n, a.shape[0] // n, a.shape[1])
    left_q = cut_up(left_q, cross)
    late = [*dps[2:], *pieces, *ctxs, grad, x, d_mlp]
    ins = [*dps, w, *late, mlp_out, w_d, bias, g1, g2, *sums, left_q, left_q]
    in_specs = (
        [pl.BlockSpec((toks, a.shape[1]), piece_at) for a in dps]
        + [once(w.shape)]
        + [hbm] * len(late)
        + [pl.BlockSpec((toks, tile), join_at), pl.BlockSpec((d, tile), join_at)]
        + [once((1, d))] * 3
        + [once(v.shape) for v in sums]
        + [hbm, once((1, *left_q.shape[1:]))]
    )
    rest = sum(a.shape[1] for a in dps[2:])
    lines = 4 + sum(v.shape[1] for v in sums) // d + 1
    lines += -lines % 8
    widths = [left_q.shape[2], rest, d]
    left = d // 2 // cross // across
    kind = BF16 if left % 16 == 0 else F32
    out_shape = [
        jax.ShapeDtypeStruct((toks, d), BF16),
        jax.ShapeDtypeStruct((toks, d), F32),
        jax.ShapeDtypeStruct((lines, d), F32),
        *[jax.ShapeDtypeStruct((left, n), F32) for n in widths],
        *[jax.ShapeDtypeStruct((left, n), kind) for n in widths for _ in range(across - 1)],
    ]
    fixed = lambda shape: pl.BlockSpec(shape, lambda i: (0,) * len(shape))
    out_specs = (
        [pl.BlockSpec((toks, tile), join_at), fixed((toks, d))]
        + [fixed((lines, d))]
        + [fixed((left, n)) for n in widths]
        + [hbm] * (len(widths) * (across - 1))
    )
    scratch = [
        pltpu.VMEM((d, toks), F32),
        pltpu.VMEM((d, toks * (halos + 1)), BF16),
        pltpu.VMEM((toks, d), F32),
        pltpu.VMEM((halos, toks, d), BF16),
        pltpu.VMEM((halos, toks, d), BF16),
    ]
    for n in widths[1:]:
        scratch += [pltpu.VMEM((d // 2, n), BF16)] * 3
        scratch += [pltpu.VMEM((cross - 1, d // 2 // cross, n), BF16)] * 2
        scratch += [pltpu.VMEM((across - 1, left, n), kind)]
    scratch += [pltpu.VMEM((cross - 1, *left_q.shape[1:]), BF16), pltpu.VMEM((across - 1, left, widths[0]), kind)]
    scratch += [pltpu.VMEM((1, rest), F32), pltpu.VMEM((ndp - 1 + across - 1, lines, d), F32)]
    scratch += [pltpu.VMEM(a.shape, a.dtype) for a in late]
    copies = 2 * halos + 3 * (1 + cross - 1 + across - 1) + (ndp - 1 + across - 1)
    scratch += [pltpu.SemaphoreType.DMA((copies,))] * 2 + [pltpu.SemaphoreType.DMA((len(late),))]
    cfg = (ndp, nseq, halos, len(pieces), len(dps), len(ctxs), joins, seq_bits)
    n = len(ins)

    def body(*refs):
        tail_kernel(cfg, *refs[:n], *refs[n + len(after) :])

    outs = pl.pallas_call(
        body,
        grid_spec=pltpu.PrefetchScalarGridSpec(
            num_scalar_prefetch=0,
            grid=(own_at + 1 + joins + 1,),
            in_specs=in_specs + [hbm] * len(after),
            out_specs=out_specs,
            scratch_shapes=scratch,
        ),
        out_shape=out_shape,
        compiler_params=pltpu.CompilerParams(vmem_limit_bytes=63 * MIB, collective_id=1, has_side_effects=True),
        cost_estimate=pl.CostEstimate(flops=20 * toks * d * depth, bytes_accessed=40 * toks * d, transcendentals=0),
        name="tail",
    )(*ins, *after)
    outs = list(outs)
    main, own, outs = outs[:3], outs[3:6], outs[6:]
    terms = []
    for a in own:
        terms.append(([(v, 0) for v in (a, *outs[: across - 1])], 0, left, F32))
        outs = outs[across - 1 :]
    return main, terms


def shards(
    hidden_in,
    doc_lengths,
    ln1_gain,
    ln1_bias,
    ln2_gain,
    ln2_bias,
    qkv_weight,
    qkv_bias,
    dense_weight,
    dense_bias,
    fc_in_weight,
    fc_in_bias,
    fc_out_weight,
    fc_out_bias,
    out_grad,
):
    _, toks, d = hidden_in.shape
    ff = fc_in_weight.shape[1]
    ndp, nseq = lax.axis_size("dp"), lax.axis_size("seq")
    ndev = ndp * nseq
    sizes = {"dp": ndp, "seq": nseq}
    me_dp, me_seq = lax.axis_index("dp"), lax.axis_index("seq")
    row = lambda v: v.reshape(1, -1)

    halos = max(min(-(-(DOC_MOST - 1) // toks), nseq - 1), 1)
    lengths = doc_lengths.reshape(-1)
    x = hidden_in.reshape(toks, d)
    a_own, m_own, grad, grad_sum = norms(
        lengths, x, out_grad.reshape(toks, d), row(ln1_gain), row(ln1_bias), row(ln2_gain), row(ln2_bias)
    )

    ahead = [(i, (i + 1) % nseq) for i in range(nseq)]
    on = ("ring", 1, nseq)
    fine = toks // 4 % LANES == 0
    cut = toks * 3 // 4 if fine else toks
    mlp_out, act, d_pre, d_mlp, b_in_sum, near = mlp(
        m_own, grad, fc_in_weight, row(fc_in_bias), fc_out_weight, sends=[(a_own, 0, cut, on)], cid=2
    )
    near, far = [near], []
    two = halos > 1

    orders = [stage_order(ndp, nseq, kind) for kind in range(3)]
    srcs = [(o, nseq) for o in orders]
    in_cut, out_cut = ff * 5 // 8, d // 4
    sends = [(a_own, cut, toks - cut, on)] if fine else []
    if two:
        sends.append((near[0], 0, toks // 4 if fine else toks // 2, on))
    s0, k0, line, s1, k1, _, *got = wgrad(
        [(srcs[0], in_cut), (srcs[2], ff - in_cut)], [m_own], d_pre, sends=sends, cid=3 if sends else None
    )
    near += got[:1] if fine else []
    far += got[-1:] if two else []
    early = [Halving(s0, k0, orders[0], sizes), Halving(s1, k1, orders[2], sizes)]
    s2, k2, s3, k3, *got = wgrad_rows(
        [(srcs[2], out_cut), (srcs[1], d - out_cut)],
        act,
        grad,
        after=[line],
        sends=[send for r in early for send in r.sends()]
        + ([(near[0], far[0].shape[0], toks // 2, on)] if two else []),
        cid=4,
    )
    for r in early:
        r.receive([got.pop(0)])
    far += got
    late = [Halving(s2, k2, orders[2], sizes), Halving(s3, k3, orders[1], sizes)]
    fc = early + late
    d_ctx, cos, sin, start, *got = d_context(
        lengths,
        grad,
        dense_weight,
        halos,
        nseq,
        sends=[send for r in late for send in r.sends()] + ([(near[1], 0, toks - cut, on)] if two and fine else []),
        cid=5,
    )
    for r in late:
        r.receive([got.pop(0)])
    far += got
    pieces = [*far, *near, a_own]
    for k in range(2, halos):
        far = [lax.ppermute(jnp.concatenate(far, axis=0), "seq", ahead)]
        pieces = far + pieces
    last = advance(fc, [d_ctx])
    for r in fc:
        r.permute()
    q, k, v = qkv(pieces, qkv_weight, row(qkv_bias), cos, sin, after=last)

    order_c = short_order(ndp, nseq)
    src_c = (order_c, nseq)
    pairs = d // LANES
    quarter = pairs // 4

    def part(at, n, sums=(), **more):
        sends = [send for r in sums for send in r.sends()]
        ctx, dp, *got = attention(
            start, q, k, v, d_ctx, cos, sin, at * quarter, n * quarter, sends=sends, cid=6 + at if sends else None, **more
        )
        for r in sums:
            r.receive([got.pop(0) for _ in r.targets()])
        return ctx, dp

    ctx_a, dp_a = part(0, 1)
    advance(fc, [ctx_a])
    ctx_b, dp_b = part(1, 1, fc)
    advance(fc, [ctx_b])
    qa_send, qa_keep, b_qkv_a, *got = wgrad(
        [(src_c, dp_a.shape[1] * 2)], pieces, [dp_a, dp_b], tn=dp_a.shape[1], sends=[send for r in fc for send in r.sends()], cid=10
    )
    for r in fc:
        r.receive([got.pop(0) for _ in r.targets()])
    r_qa = Halving(qa_send, qa_keep, order_c, sizes)
    last = advance(fc, [b_qkv_a])
    while len(fc[0].stages) > 1:
        for r in fc:
            r.permute()
        last = advance(fc, last)
    ctx_c, dp_c = part(2, 2, [*fc, r_qa])
    left_q, g_in, g_out = combine([r_qa.rest(), *[(*r.rest()[:3], F32) for r in fc]], [ctx_c], joined=(2, 4))
    main, terms = tail(
        [dp_a, dp_b, dp_c],
        qkv_weight,
        pieces,
        [ctx_a, ctx_b, ctx_c],
        grad,
        x,
        mlp_out,
        d_mlp,
        dense_weight,
        row(dense_bias + fc_out_bias),
        row(ln1_gain),
        row(ln2_gain),
        [grad_sum, b_qkv_a, b_in_sum],
        left_q,
        ndp,
        nseq,
        halos,
    )
    hidden_out, grad_in, small = main
    hidden_out, g_qkv, g_dense, *parts = last_sums(terms, small, hidden_out, ff, ndev, nseq)
    o1g, o1b, o2g, o2b, o_db, o_ob, o_qb, o_ib = (v.reshape(-1) for v in parts)
    return (
        hidden_out.reshape(hidden_in.shape),
        grad_in.reshape(hidden_in.shape),
        o1g,
        o1b,
        o2g,
        o2b,
        g_qkv,
        o_qb,
        g_dense,
        o_db,
        g_in,
        o_ib,
        g_out,
        o_ob,
    )


def solution(mesh):
    both = P(("dp", "seq"))
    rows = P(("dp", "seq"), None)
    toks = P("dp", "seq", None)
    return jax.shard_map(
        shards,
        mesh=mesh,
        in_specs=(toks, P("dp", None)) + (P(),) * 12 + (toks,),
        out_specs=(toks, toks, both, both, both, both, rows, both, rows, both, rows, both, rows, both),
        check_vma=False,
    )
```
